32 devices in a mesh: batch: 2 (over core), res: 16 (over z, y, x).
Axes of the slice: x: 2, y: 2, z: 4, core: 2. Of those that a mesh axis runs over, the one named last changes fastest.
Arguments:
- node_states: bfloat16 [2, 1024, 512], P('batch', 'res'), may hold values from -6 to 6
- edge_states: bfloat16 [2, 1024, 60, 192], P('batch', 'res'), may hold values from -6 to 6
- neighbours: int32 [2, 1024, 60], P('batch', 'res'), may hold values from 0 to 1023, as said below
- residue_mask: int32 [2, 1024], P('batch', 'res'), may hold values from 0 to 1, as said below
- neighbour_count: int32 [2, 1024], P('batch', 'res'), may hold values from 0 to 60, as said below
- message_in: bfloat16 [1216, 512], replicated, may hold values from -0.15625 to 0.15625
- message_in_bias: bfloat16 [512], replicated, may hold values from -1.75 to 1.75
- message_mid: bfloat16 [512, 512], replicated, may hold values from -0.25 to 0.25
- message_mid_bias: bfloat16 [512], replicated, may hold values from -1.75 to 1.75
- message_out: bfloat16 [512, 512], replicated, may hold values from -0.5 to 0.5
- message_out_bias: bfloat16 [512], replicated, may hold values from -1.75 to 1.75
- node_gain: bfloat16 [512], replicated, may hold values from 0.5 to 1.5
- node_shift: bfloat16 [512], replicated, may hold values from -1.75 to 1.75
- feed_up: bfloat16 [512, 2048], replicated, may hold values from -0.25 to 0.25
- feed_up_bias: bfloat16 [2048], replicated, may hold values from -1.75 to 1.75
- feed_down: bfloat16 [2048, 512], replicated, may hold values from -0.125 to 0.125
- feed_down_bias: bfloat16 [512], replicated, may hold values from -1.75 to 1.75
- final_gain: bfloat16 [512], replicated, may hold values from 0.5 to 1.5
- final_shift: bfloat16 [512], replicated, may hold values from -1.75 to 1.75
- edge_in: bfloat16 [1216, 192], replicated, may hold values from -0.15625 to 0.15625
- edge_in_bias: bfloat16 [192], replicated, may hold values from -1.75 to 1.75
- edge_mid: bfloat16 [192, 192], replicated, may hold values from -0.4375 to 0.4375
- edge_mid_bias: bfloat16 [192], replicated, may hold values from -1.75 to 1.75
- edge_out: bfloat16 [192, 192], replicated, may hold values from -0.4375 to 0.4375
- edge_out_bias: bfloat16 [192], replicated, may hold values from -1.75 to 1.75
- edge_gain: bfloat16 [192], replicated, may hold values from 0.5 to 1.5
- edge_shift: bfloat16 [192], replicated, may hold values from -1.75 to 1.75
- node_cotangent: bfloat16 [2, 1024, 512], P('batch', 'res'), may hold values from -6 to 6
- edge_cotangent: bfloat16 [2, 1024, 60, 192], P('batch', 'res'), may hold values from -6 to 6
Outputs:
- node_out: bfloat16 [2, 1024, 512], P('batch', 'res')
- edge_result: bfloat16 [2, 1024, 60, 192], P('batch', 'res')
- grad_node_states: float32 [2, 1024, 512], P('batch', 'res')
- grad_edge_states: float32 [2, 1024, 60, 192], P('batch', 'res')
- grad_message_in: float32 [1216, 512], replicated
- grad_message_in_bias: float32 [512], replicated
- grad_message_mid: float32 [512, 512], replicated
- grad_message_mid_bias: float32 [512], replicated
- grad_message_out: float32 [512, 512], replicated
- grad_message_out_bias: float32 [512], replicated
- grad_node_gain: float32 [512], replicated
- grad_node_shift: float32 [512], replicated
- grad_feed_up: float32 [512, 2048], replicated
- grad_feed_up_bias: float32 [2048], replicated
- grad_feed_down: float32 [2048, 512], replicated
- grad_feed_down_bias: float32 [512], replicated
- grad_final_gain: float32 [512], replicated
- grad_final_shift: float32 [512], replicated
- grad_edge_in: float32 [1216, 192], replicated
- grad_edge_in_bias: float32 [192], replicated
- grad_edge_mid: float32 [192, 192], replicated
- grad_edge_mid_bias: float32 [192], replicated
- grad_edge_out: float32 [192, 192], replicated
- grad_edge_out_bias: float32 [192], replicated
- grad_edge_gain: float32 [192], replicated
- grad_edge_shift: float32 [192], replicated
The draws below stay inside these ranges and needn't reach their ends.
Inputs may be any that keep to these rules, and one draw needn't show every extreme that they name: `neighbours`: A chain fills whole blocks of 64 residue slots from a block's start, at most 12 blocks, its real residues first. For a real residue slot 0 is the residue itself and slots 1 to neighbour_count - 1 are residues of its chain; every other slot names the residue itself. A neighbour's block is at most 11 blocks from the residue's block, and in every bucket some neighbour is exactly 11 blocks away on each side. `residue_mask`: 1 for a chain's real residues, 0 for padding. `neighbour_count`: min(60, the chain's real residues) for a real residue, 0 for padding.
All inputs are finite; a program needn't handle non-finite values.
Results may differ from the reference program's by a relative error of at most 0.015.
Values may be sent and summed in bfloat16 or wider, within the bound.
A program may use at most 320 MiB of HBM per device.

```python
from functools import partial
import jax
import jax.numpy as jnp
from jax import lax

D = 512
DE = 192
FF = 2048
K = 60
R_DEV = 64
SPAN = 11
NB = 2
RES = 1024


def chain_layout(key):
    base_key = jax.random.fold_in(key, 11)
    gap_key, length_key, pick_key = jax.random.split(base_key, 3)
    block_total = RES // R_DEV
    gap_sizes = jax.random.randint(gap_key, (NB, block_total), 1, SPAN + 2)
    gap_sizes = jnp.where(jnp.arange(block_total)[None, :] == 0, SPAN + 1, gap_sizes)
    chain_ends = jnp.cumsum(gap_sizes, axis=1)
    chain_starts = chain_ends - gap_sizes
    chain_ends = jnp.minimum(chain_ends, block_total)
    blocks = jnp.arange(block_total)
    member = ((chain_starts[:, None, :] <= blocks[None, :, None]) & (blocks[None, :, None] < chain_ends[:, None, :])).astype(jnp.int32)
    span_blocks = jnp.maximum(chain_ends - chain_starts, 1)
    extra_rows = jax.random.randint(length_key, (NB, block_total), 1, R_DEV + 1)
    chain_length = (span_blocks - 1) * R_DEV + extra_rows
    start_block = jnp.sum(member * chain_starts[:, None, :], axis=2)
    block_length = jnp.sum(member * chain_length[:, None, :], axis=2)
    residue = jnp.arange(RES)
    start_res = jnp.repeat(start_block, R_DEV, axis=1) * R_DEV
    length_res = jnp.repeat(block_length, R_DEV, axis=1)
    is_real = residue[None, :] - start_res < length_res
    near_count = jnp.where(is_real, jnp.minimum(K, length_res), 0)
    picked = jax.random.randint(pick_key, (NB, RES, K), 0, length_res[:, :, None]) + start_res[:, :, None]
    slot_index = jnp.arange(K)[None, None, :]
    self_res = jnp.broadcast_to(residue[None, :, None], (NB, RES, K))
    picked = jnp.where((slot_index == 0) | (slot_index >= near_count[:, :, None]), self_res, picked)
    first_len = chain_length[:, 0]
    forward_link = (residue[None, :, None] == 0) & (slot_index == 1)
    backward_link = (residue[None, :, None] == (first_len - 1)[:, None, None]) & (slot_index == 1)
    picked = jnp.where(forward_link, (first_len - 1)[:, None, None], picked)
    picked = jnp.where(backward_link, 0, picked)
    return (picked.astype(jnp.int32), is_real.astype(jnp.int32), near_count.astype(jnp.int32))


def draw_neighbours(key, part):
    return chain_layout(key)[0]


def draw_residue_mask(key, part):
    return chain_layout(key)[1]


def draw_neighbour_count(key, part):
    return chain_layout(key)[2]


def block_scale(rng, shape, cuts, least, largest):
    level = 1.0
    for dim, parts in cuts:
        heights = jax.random.uniform(jax.random.fold_in(jax.random.fold_in(rng, 6), dim), (parts,), jnp.float32, least / len(cuts), largest / len(cuts))
        level = level * jnp.repeat(jnp.exp(heights), shape[dim] // parts).reshape((-1,) + (1,) * (len(shape) - 1 - dim))
    return level


def normal_values(own_key, shape, width, reach, shards=(), held_as=jnp.bfloat16):
    result = width * jax.random.normal(own_key, shape, jnp.float32)
    if shards:
        result = result * block_scale(own_key, shape, shards, -0.22, 0.18)
    return jnp.clip(result, -reach, reach).astype(held_as)


def setup_inputs(seed: int = 0) -> dict:
    key_of = jax.random.split(jax.random.key(seed), 30)
    return {
        "node_states": normal_values(key_of[0], (NB, RES, D), 1.0, 6.0, ((0, 2), (1, 16))),
        "edge_states": normal_values(key_of[1], (NB, RES, K, DE), 1.0, 6.0, ((0, 2), (1, 16))),
        "neighbours": draw_neighbours(jax.random.fold_in(key_of[29], 71), 0),
        "residue_mask": draw_residue_mask(jax.random.fold_in(key_of[29], 71), 0),
        "neighbour_count": draw_neighbour_count(jax.random.fold_in(key_of[29], 71), 0),
        "message_in": normal_values(key_of[5], (2 * D + DE, D), (2 * D + DE) ** -0.5, 0.15625),
        "message_in_bias": normal_values(key_of[6], (D,), 0.3, 1.75),
        "message_mid": normal_values(key_of[7], (D, D), D ** -0.5, 0.25),
        "message_mid_bias": normal_values(key_of[8], (D,), 0.3, 1.75),
        "message_out": normal_values(key_of[9], (D, D), (D // 4) ** -0.5, 0.5),
        "message_out_bias": normal_values(key_of[10], (D,), 0.3, 1.75),
        "node_gain": jnp.clip(1.0 + 0.1 * jax.random.normal(key_of[11], (D,), jnp.float32), 0.5, 1.5).astype(jnp.bfloat16),
        "node_shift": normal_values(key_of[12], (D,), 0.3, 1.75),
        "feed_up": normal_values(key_of[13], (D, FF), D ** -0.5, 0.25),
        "feed_up_bias": normal_values(key_of[14], (FF,), 0.3, 1.75),
        "feed_down": normal_values(key_of[15], (FF, D), FF ** -0.5, 0.125),
        "feed_down_bias": normal_values(key_of[16], (D,), 0.3, 1.75),
        "final_gain": jnp.clip(1.0 + 0.1 * jax.random.normal(key_of[17], (D,), jnp.float32), 0.5, 1.5).astype(jnp.bfloat16),
        "final_shift": normal_values(key_of[18], (D,), 0.3, 1.75),
        "edge_in": normal_values(key_of[19], (2 * D + DE, DE), (2 * D + DE) ** -0.5, 0.15625),
        "edge_in_bias": normal_values(key_of[20], (DE,), 0.3, 1.75),
        "edge_mid": normal_values(key_of[21], (DE, DE), DE ** -0.5, 0.4375),
        "edge_mid_bias": normal_values(key_of[22], (DE,), 0.3, 1.75),
        "edge_out": normal_values(key_of[23], (DE, DE), DE ** -0.5, 0.4375),
        "edge_out_bias": normal_values(key_of[24], (DE,), 0.3, 1.75),
        "edge_gain": jnp.clip(1.0 + 0.1 * jax.random.normal(key_of[25], (DE,), jnp.float32), 0.5, 1.5).astype(jnp.bfloat16),
        "edge_shift": normal_values(key_of[26], (DE,), 0.3, 1.75),
        "node_cotangent": normal_values(key_of[27], (NB, RES, D), 1.0, 6.0, ((0, 2), (1, 16))),
        "edge_cotangent": normal_values(key_of[28], (NB, RES, K, DE), 1.0, 6.0, ((0, 2), (1, 16))),
    }


eps_norm = 1e-05

@jax.custom_vjp
def low(v):
    return lax.optimization_barrier(v.astype(jnp.bfloat16)).astype(jnp.float32)

@jax.custom_vjp
def low_back(v):
    return v

def low_keep(v):
    return (low(v), None)

def low_pass(kept, grad):
    return (grad,)

def back_keep(v):
    return (v, None)

def back_low(kept, grad):
    return (low(grad),)
low.defvjp(low_keep, low_pass)
low_back.defvjp(back_keep, back_low)

def product(left, right):
    return jnp.dot(left, right, precision=lax.Precision.HIGHEST)

def layer_norm(values, gain_row, shifts):
    centre = lax.optimization_barrier(jnp.mean(values, axis=-1, keepdims=True))
    centred = values - centre
    variance = lax.optimization_barrier(jnp.mean(centred * centred, axis=-1, keepdims=True))
    return centred * lax.rsqrt(variance + eps_norm) * gain_row + shifts

def gelu_exact(values):
    return jax.nn.gelu(values, approximate=False)

def message_block(params, node_rows, inputs):
    edge_rows, near_index, share, own_rows = inputs
    block_rows = own_rows.shape[0]
    others = jnp.take(node_rows, near_index.reshape(-1), axis=0)
    joined = jnp.concatenate([jnp.repeat(own_rows, K, axis=0), others, edge_rows.reshape(block_rows * K, -1)], axis=1)
    pre_one = low_back(product(joined, params['message_in']) + params['message_in_bias'])
    act_one = low(gelu_exact(pre_one))
    pre_two = low_back(product(act_one, params['message_mid']) + params['message_mid_bias'])
    act_two = low(gelu_exact(pre_two))
    message = low_back(product(act_two, params['message_out']) + params['message_out_bias'])
    return lax.optimization_barrier(jnp.sum(message.reshape(block_rows, K, -1) * share[:, :, None], axis=1))

def edge_block(params, node_low, inputs):
    edge_rows, near_index, own_rows = inputs
    block_rows = own_rows.shape[0]
    flat_edges = edge_rows.reshape(block_rows * K, -1)
    others = jnp.take(node_low, near_index.reshape(-1), axis=0)
    joined = jnp.concatenate([jnp.repeat(own_rows, K, axis=0), others, flat_edges], axis=1)
    edge_pre_one = low_back(product(joined, params['edge_in']) + params['edge_in_bias'])
    edge_act_one = low(gelu_exact(edge_pre_one))
    edge_pre_two = low_back(product(edge_act_one, params['edge_mid']) + params['edge_mid_bias'])
    edge_act_two = low(gelu_exact(edge_pre_two))
    edge_pre_three = low_back(product(edge_act_two, params['edge_out']) + params['edge_out_bias'])
    edge_new = layer_norm(flat_edges + edge_pre_three, params['edge_gain'], params['edge_shift'])
    return edge_new.reshape(block_rows, K, -1)

def forward(params, node_rows, edge_rows, near_index, share, live_mask):
    block_total = node_rows.shape[0] // R_DEV

    def split_blocks(values):
        return values.reshape((block_total, R_DEV) + values.shape[1:])
    aggregate = lax.map(jax.checkpoint(partial(message_block, params, node_rows)), (split_blocks(edge_rows), split_blocks(near_index), split_blocks(share), split_blocks(node_rows)))
    aggregate = aggregate.reshape(node_rows.shape)
    residual_sum = node_rows + live_mask[:, None] * aggregate
    first_norm = layer_norm(residual_sum, params['node_gain'], params['node_shift'])
    up_pre = low_back(product(low(first_norm), params['feed_up']) + params['feed_up_bias'])
    up_act = low(gelu_exact(up_pre))
    down_out = low_back(product(up_act, params['feed_down']) + params['feed_down_bias'])
    updated = layer_norm(first_norm + down_out, params['final_gain'], params['final_shift'])
    node_low = low(updated)
    edge_new = lax.map(jax.checkpoint(partial(edge_block, params, node_low)), (split_blocks(edge_rows), split_blocks(near_index), split_blocks(node_low)))
    return (updated, edge_new.reshape(edge_rows.shape))

def reference(node_states, edge_states, neighbours, residue_mask, neighbour_count, message_in, message_in_bias, message_mid, message_mid_bias, message_out, message_out_bias, node_gain, node_shift, feed_up, feed_up_bias, feed_down, feed_down_bias, final_gain, final_shift, edge_in, edge_in_bias, edge_mid, edge_mid_bias, edge_out, edge_out_bias, edge_gain, edge_shift, node_cotangent, edge_cotangent):
    raw = {'message_in': message_in, 'message_in_bias': message_in_bias, 'message_mid': message_mid, 'message_mid_bias': message_mid_bias, 'message_out': message_out, 'message_out_bias': message_out_bias, 'node_gain': node_gain, 'node_shift': node_shift, 'feed_up': feed_up, 'feed_up_bias': feed_up_bias, 'feed_down': feed_down, 'feed_down_bias': feed_down_bias, 'final_gain': final_gain, 'final_shift': final_shift, 'edge_in': edge_in, 'edge_in_bias': edge_in_bias, 'edge_mid': edge_mid, 'edge_mid_bias': edge_mid_bias, 'edge_out': edge_out, 'edge_out_bias': edge_out_bias, 'edge_gain': edge_gain, 'edge_shift': edge_shift}
    params = jax.tree.map(lambda value: value.astype(jnp.float32), raw)
    totals = jax.tree.map(jnp.zeros_like, params)
    node_list = []
    edge_list = []
    node_grads = []
    edge_grads = []
    for bucket in range(node_states.shape[0]):
        node_rows = node_states[bucket].astype(jnp.float32)
        edge_rows = edge_states[bucket].astype(jnp.float32)
        near_count = neighbour_count[bucket]
        valid = (jnp.arange(K)[None, :] < near_count[:, None]).astype(jnp.float32)
        share = valid / jnp.maximum(near_count, 1).astype(jnp.float32)[:, None]
        live_mask = residue_mask[bucket].astype(jnp.float32)
        runner = partial(forward, near_index=neighbours[bucket], share=share, live_mask=live_mask)
        outputs, backward = jax.vjp(runner, params, node_rows, edge_rows)
        param_grads, node_grad, edge_grad = backward((node_cotangent[bucket].astype(jnp.float32), edge_cotangent[bucket].astype(jnp.float32)))
        totals = jax.tree.map(jnp.add, totals, param_grads)
        node_list.append(outputs[0].astype(jnp.bfloat16))
        edge_list.append(outputs[1].astype(jnp.bfloat16))
        node_grads.append(node_grad)
        edge_grads.append(edge_grad)
    return (jnp.stack(node_list), jnp.stack(edge_list), jnp.stack(node_grads), jnp.stack(edge_grads), totals['message_in'], totals['message_in_bias'], totals['message_mid'], totals['message_mid_bias'], totals['message_out'], totals['message_out_bias'], totals['node_gain'], totals['node_shift'], totals['feed_up'], totals['feed_up_bias'], totals['feed_down'], totals['feed_down_bias'], totals['final_gain'], totals['final_shift'], totals['edge_in'], totals['edge_in_bias'], totals['edge_mid'], totals['edge_mid_bias'], totals['edge_out'], totals['edge_out_bias'], totals['edge_gain'], totals['edge_shift'])
```

```python
import functools
import jax
import jax.numpy as jnp
from jax import lax
from jax.experimental import pallas as pl
from jax.experimental.pallas import tpu as pltpu
from jax.sharding import PartitionSpec as P

MESH = pl.DeviceIdType.MESH
low = jnp.bfloat16
wide = jnp.float32


def chip_grid(count):
    side_x = 2 if count < 64 else 4
    side_y = side_x
    return (count // (side_x * side_y), side_y, side_x)


class Spot:
    def __init__(self, grid):
        self.grid = grid
        side_z, side_y, side_x = grid
        me = lax.axis_index("res")
        self.core = lax.axis_index("batch")
        self.z = me // (side_y * side_x)
        self.y = (me // side_x) % side_y
        self.x = me % side_x

    def device(self, z, y, x):
        return (self.core, (z * self.grid[1] + y) * self.grid[2] + x)

    def far_z(self, step):
        return (self.z + step) % self.grid[0]

    def far_y(self, step):
        return (self.y + step) % self.grid[1]

    def far_x(self, step):
        return (self.x + step) % self.grid[2]

    def peers(self):
        found = [self.device(self.far_z(s), self.y, self.x) for s in range(1, self.grid[0])]
        found += [self.device(self.z, self.far_y(s), self.x) for s in range(1, self.grid[1])]
        found += [self.device(self.z, self.y, self.far_x(s)) for s in range(1, self.grid[2])]
        return found


def meet(peers):
    barrier = pltpu.get_barrier_semaphore()
    for peer in peers:
        pl.semaphore_signal(barrier, inc=1, device_id=peer, device_id_type=MESH)
    pl.semaphore_wait(barrier, len(peers))


def remote(source, target, send, arrive, device):
    return pltpu.make_async_remote_copy(
        src_ref=source, dst_ref=target, send_sem=send, recv_sem=arrive,
        device_id=device, device_id_type=MESH,
    )


def gather_sems(grid):
    side_z, side_y, side_x = grid
    dma = pltpu.SemaphoreType.DMA
    shapes = [(side_z - 1,), (side_z, side_x - 1), (side_z, side_y - 1), (side_z, side_y - 1), (side_z, side_x - 1)]
    return [dma(s) for s in shapes for _ in range(2)]


def gather_blocks(spot, table, sems, on_plane=None):
    (s1, r1, s2a, r2a, s2b, r2b, s3a, r3a, s3b, r3b) = sems
    side_z, side_y, side_x = spot.grid
    z, y, x = spot.z, spot.y, spot.x
    sent = []

    def go(copy):
        copy.start()
        sent.append(copy)

    ups = []
    for s in range(1, side_z):
        copy = remote(table.at[z, y, x], table.at[z, y, x], s1.at[s - 1], r1.at[s - 1], spot.device(spot.far_z(s), y, x))
        go(copy)
        ups.append(copy)
    firsts = []
    for j in range(side_z):
        if j:
            ups[j - 1].wait_recv()
        zj = (z - j) % side_z
        row = []
        for s in range(1, side_x):
            copy = remote(table.at[zj, y, x, 0], table.at[zj, y, x, 0], s2a.at[j, s - 1], r2a.at[j, s - 1], spot.device(z, y, spot.far_x(s)))
            go(copy)
            row.append(copy)
        for s in range(1, side_y):
            copy = remote(table.at[zj, y, x, 1], table.at[zj, y, x, 1], s2b.at[j, s - 1], r2b.at[j, s - 1], spot.device(z, spot.far_y(s), x))
            go(copy)
            row.append(copy)
        firsts.append(row)
    lasts = []
    for j in range(side_z):
        zj = (z - j) % side_z
        for copy in firsts[j]:
            copy.wait_recv()
        row = []
        for s in range(1, side_y):
            copy = remote(table.at[zj, y, :, 0], table.at[zj, y, :, 0], s3a.at[j, s - 1], r3a.at[j, s - 1], spot.device(z, spot.far_y(s), x))
            go(copy)
            row.append(copy)
        for s in range(1, side_x):
            copy = remote(table.at[zj, :, x, 1], table.at[zj, :, x, 1], s3b.at[j, s - 1], r3b.at[j, s - 1], spot.device(z, y, spot.far_x(s)))
            go(copy)
            row.append(copy)
        lasts.append(row)
    for j in range(side_z):
        for copy in lasts[j]:
            copy.wait_recv()
        if on_plane is not None:
            on_plane((z - j) % side_z, j, sent)
    return sent


def scatter_scratch(grid, rows, width):
    side_z, side_y, side_x = grid
    dma = pltpu.SemaphoreType.DMA
    shapes = [(side_z, side_y - 1), (side_z, side_x - 1), (side_z, side_x - 1), (side_z, side_y - 1), (side_z - 1,)]
    buffers = [
        pltpu.VMEM((side_z, side_y - 1, side_x, rows, width), low),
        pltpu.VMEM((side_z, side_x - 1, side_y, rows, width), low),
        pltpu.VMEM((side_z, side_x, rows, width), low),
        pltpu.VMEM((side_z, side_y, rows, width), low),
        pltpu.VMEM((side_z, side_x - 1, rows, width), low),
        pltpu.VMEM((side_z, side_y - 1, rows, width), low),
        pltpu.VMEM((side_z, 2, rows, width), low),
        pltpu.VMEM((side_z - 1, 2, rows, width), low),
    ]
    return buffers + [dma(s) for s in shapes for _ in range(2)]


def scatter_sums(spot, part, scratch, before_plane=None):
    (ra1, rb1, ka, kb, ra2, rb2, tot, r3, s1a, q1a, s1b, q1b, s2a, q2a, s2b, q2b, s3, q3) = scratch
    side_z, side_y, side_x = spot.grid
    z, y, x = spot.z, spot.y, spot.x
    sent = []

    def go(copy):
        copy.start()
        sent.append(copy)
        return copy

    order = list(range(1, side_z)) + [0]
    one = {}
    for j in order:
        zj = (z + j) % side_z
        if before_plane is not None:
            before_plane(zj, j, sent)
        a = [go(remote(part.at[zj, spot.far_y(s), :, 0], ra1.at[j, s - 1], s1a.at[j, s - 1], q1a.at[j, s - 1], spot.device(z, spot.far_y(s), x))) for s in range(1, side_y)]
        b = [go(remote(part.at[zj, :, spot.far_x(s), 1], rb1.at[j, s - 1], s1b.at[j, s - 1], q1b.at[j, s - 1], spot.device(z, y, spot.far_x(s)))) for s in range(1, side_x)]
        one[j] = (a, b)
    two = {}
    for j in order:
        zj = (z + j) % side_z
        for copy in one[j][0]:
            copy.wait_recv()
        total = part[zj, y, :, 0].astype(wide)
        for s in range(side_y - 1):
            total = total + ra1[j, s].astype(wide)
        ka[j] = total.astype(low)
        for copy in one[j][1]:
            copy.wait_recv()
        total = part[zj, :, x, 1].astype(wide)
        for s in range(side_x - 1):
            total = total + rb1[j, s].astype(wide)
        kb[j] = total.astype(low)
        a = [go(remote(ka.at[j, spot.far_x(s)], ra2.at[j, s - 1], s2a.at[j, s - 1], q2a.at[j, s - 1], spot.device(z, y, spot.far_x(s)))) for s in range(1, side_x)]
        b = [go(remote(kb.at[j, spot.far_y(s)], rb2.at[j, s - 1], s2b.at[j, s - 1], q2b.at[j, s - 1], spot.device(z, spot.far_y(s), x))) for s in range(1, side_y)]
        two[j] = (a, b)
    three = []
    for j in order:
        zj = (z + j) % side_z
        for copy in two[j][0] + two[j][1]:
            copy.wait_recv()
        ta = ka[j, x].astype(wide)
        for s in range(side_x - 1):
            ta = ta + ra2[j, s].astype(wide)
        tb = kb[j, y].astype(wide)
        for s in range(side_y - 1):
            tb = tb + rb2[j, s].astype(wide)
        if j:
            tot[j, 0] = ta.astype(low)
            tot[j, 1] = tb.astype(low)
            three.append(go(remote(tot.at[j], r3.at[j - 1], s3.at[j - 1], q3.at[j - 1], spot.device(zj, y, x))))
    for copy in three:
        copy.wait_recv()
    for s in range(side_z - 1):
        ta = ta + r3[s, 0].astype(wide)
        tb = tb + r3[s, 1].astype(wide)
    return (ta, tb), sent
eps_norm = 1e-05
root_half = 0.7071067811865476
root_turn = 0.3989422804014327


def dot(left, right):
    return jnp.dot(left, right, preferred_element_type=wide)


def dot_back(left, right):
    return lax.dot_general(left, right, (((1,), (1,)), ((), ())), preferred_element_type=wide)


def dot_rows(left, right):
    return lax.dot_general(left, right, (((0,), (0,)), ((), ())), preferred_element_type=wide)


def gelu_pair(values):
    share = 0.5 + 0.5 * lax.erf(values * root_half)
    slope = share + values * (jnp.exp(values * values * -0.5) * root_turn)
    return values * share, slope


def norm_stats(values):
    centre = jnp.mean(values, axis=-1, keepdims=True)
    centred = values - centre
    variance = jnp.mean(centred * centred, axis=-1, keepdims=True)
    scale = lax.rsqrt(variance + eps_norm)
    return centred * scale, scale


def norm_back(hat, scale, gain, grad):
    inner = grad * gain
    return scale * (
        inner
        - jnp.mean(inner, axis=-1, keepdims=True)
        - hat * jnp.mean(inner * hat, axis=-1, keepdims=True)
    )


def as_row(ref, start=None, size=None):
    return ref[...].astype(wide).reshape(1, ref.shape[0])


def as_column(row, count):
    rows = lax.broadcasted_iota(jnp.int32, (count, count), 0)
    lanes = lax.broadcasted_iota(jnp.int32, (count, count), 1)
    return jnp.sum(jnp.where(rows == lanes, jnp.broadcast_to(row, (count, count)), 0), axis=1, keepdims=True)


def slot_column(index, slot):
    lanes = lax.broadcasted_iota(jnp.int32, index.shape, 1)
    return jnp.sum(jnp.where(lanes == slot, index, 0), axis=1, keepdims=True)


def pick_rows(index, first, slots, total):
    count = index.shape[0]
    lanes = lax.broadcasted_iota(jnp.int32, (count, total), 1)
    return jnp.concatenate(
        [jnp.where(slot_column(index, first + s) == lanes, 1.0, 0.0).astype(low) for s in range(slots)], axis=0
    )


def pick_columns(row, total):
    rows = lax.broadcasted_iota(jnp.int32, (total, row.shape[1]), 0)
    return jnp.where(rows == row, 1.0, 0.0).astype(low)


def message_forward(
    slots, index, counts, masks, nodes, table, edges, w_in, b_in, w_mid, b_mid, w_out, b_out,
    gain_one, shift_one, w_up, b_up, w_down, b_down, gain_two, shift_two, w_edge, b_edge,
    slope_one, slope_two, act_one, mixed_low, resid, second_sum, up_act, up_slope, node_out, sent, own_edge,
    projected, own, pooled,
):
    step = pl.program_id(0)
    count, width = nodes.shape
    total = table.shape[0]
    live = as_column(counts[...], count)

    @pl.when(step == 0)
    def _():
        projected[...] = dot(table[...], w_in[width : 2 * width]).astype(low)
        own[...] = dot(nodes[...], w_in[0:width]) + as_row(b_in)
        pooled[...] = jnp.zeros_like(pooled)

    picks = pick_rows(index[...], step * slots, slots, total)
    flat = edges[...].reshape(slots * count, edges.shape[2])
    pre = dot(picks, projected[...]) + dot(flat, w_in[2 * width :])
    pre = pre.reshape(slots, count, width) + own[...][None]
    act, slope = gelu_pair(pre)
    act = act.astype(low)
    act_one[...] = act
    slope_one[...] = slope.astype(low)
    pre = dot(act.reshape(slots * count, width), w_mid[...]) + as_row(b_mid)
    act, slope = gelu_pair(pre)
    act = act.reshape(slots, count, width)
    slope_two[...] = slope.astype(low).reshape(slots, count, width)
    gathered = pooled[...]
    for s in range(slots):
        gathered = gathered + jnp.where(live > step * slots + s, act[s], 0.0)
    pooled[...] = gathered

    @pl.when(step == pl.num_programs(0) - 1)
    def _():
        mean = pooled[...] / jnp.maximum(live, 1).astype(wide)
        mean_low = mean.astype(low)
        mixed_low[...] = mean_low
        some = jnp.where(live > 0, 1.0, 0.0)
        mask = as_column(masks[...], count).astype(wide)
        aggregate = dot(mean_low, w_out[...]) + some * as_row(b_out)
        total_sum = nodes[...].astype(wide) + mask * aggregate
        resid[...] = total_sum
        hat, _ = norm_stats(total_sum)
        first = hat * as_row(gain_one) + as_row(shift_one)
        up = dot(first.astype(low), w_up[...]) + as_row(b_up)
        act_up, slope_up = gelu_pair(up)
        act_up = act_up.astype(low)
        up_act[...] = act_up
        up_slope[...] = slope_up
        summed = first + dot(act_up, w_down[...]) + as_row(b_down)
        second_sum[...] = summed
        hat, _ = norm_stats(summed)
        out = (hat * as_row(gain_two) + as_row(shift_two)).astype(low)
        node_out[...] = out
        pad = jnp.zeros((count, sent.shape[1] - w_edge.shape[0]), low)
        sent[...] = jnp.concatenate([dot_back(out, w_edge[:, width : 2 * width]).astype(low), pad], axis=1)
        own_edge[...] = dot_back(out, w_edge[:, 0:width]) + as_row(b_edge)


def edge_pass(
    slots, index, rows, table, own_edge, edges, cotangent, w_edge, w_mid, b_mid, w_out, b_out, gain, shift,
    result, partial, spread, own_grad, g_in, g_mid, g_out, vectors, spread_sum,
):
    step = pl.program_id(0)
    count, width = own_edge.shape
    total = table.shape[0]
    base = w_edge.shape[1] - width

    @pl.when(step == 0)
    def _():
        spread_sum[...] = jnp.zeros_like(spread_sum)
        for ref in (own_grad, g_in, g_mid, g_out, vectors):
            ref[...] = jnp.zeros_like(ref)

    w_here = w_edge[:, base:]
    picks = pick_rows(index[...], step * slots, slots, total)
    flat = edges[...].reshape(slots * count, width)
    pre = dot(picks, table[...])[:, 0:width] + dot_back(flat, w_here)
    pre = (pre.reshape(slots, count, width) + own_edge[...][None]).reshape(slots * count, width)
    act_one, slope_one = gelu_pair(pre)
    act_one = act_one.astype(low)
    pre = dot(act_one, w_mid[...]) + as_row(b_mid)
    act_two, slope_two = gelu_pair(pre)
    act_two = act_two.astype(low)
    pre = dot(act_two, w_out[...]) + as_row(b_out)
    hat, scale = norm_stats(flat.astype(wide) + pre)
    gain_row = as_row(gain)
    result[...] = (hat * gain_row + as_row(shift)).astype(low).reshape(slots, count, width)
    grad = cotangent[...].reshape(slots * count, width).astype(wide)
    sum_grad = norm_back(hat, scale, gain_row, grad)
    three = sum_grad.astype(low)
    g_out[...] += dot_rows(act_two, three)
    two = (slope_two * dot_back(three, w_out[...])).astype(low)
    g_mid[...] += dot_rows(act_one, two)
    one = (slope_one * dot_back(two, w_mid[...])).astype(low)
    g_in[...] += dot_rows(one, flat)
    vectors[...] += jnp.concatenate(
        [
            jnp.sum(piece, axis=0, keepdims=True)
            for piece in (grad * hat, grad, three.astype(wide), two.astype(wide), one.astype(wide))
        ]
        + [jnp.zeros((3, width), wide)],
        axis=0,
    )
    own_grad[...] += jnp.sum(one.astype(wide).reshape(slots, count, width), axis=0)
    partial[...] = (sum_grad + dot(one, w_here)).reshape(slots, count, width)
    spread_sum[...] += dot(pick_columns(rows[0], total), one)

    @pl.when(step == pl.num_programs(0) - 1)
    def _():
        pad = jnp.zeros((total, spread.shape[1] - width), low)
        spread[...] = jnp.concatenate([spread_sum[...].astype(low), pad], axis=1)


def node_backward(
    slots, layout, rows, counts, masks, nodes, table, edges, slope_one, slope_two, act_one, partial,
    mixed_low, resid, second_sum, up_act, up_slope, node_out, cotangent, back_edge, own_edge_grad,
    e_in, e_mid, e_out, e_vectors,
    w_in, w_mid, w_out, gain_one, shift_one, w_up, w_down, gain_two, w_edge,
    edge_grad, spread, node_part, packed,
    level, spread_sum, own_sum, g_mid, g_edge, bias_mid, lines,
):
    step = pl.program_id(0)
    count, width = nodes.shape
    total = table.shape[0]
    narrow = w_edge.shape[0]
    hidden = w_up.shape[1]
    live = as_column(counts[...], count)

    def put(name, value):
        row = layout[name]
        packed[row : row + value.shape[0], :] = value.astype(low)

    def put_line(name, value):
        row = layout[name]
        lines[row : row + value.shape[0], 0 : value.shape[1]] = value

    @pl.when(step == 0)
    def _():
        for ref in (spread_sum, own_sum, g_mid, g_edge, bias_mid, lines):
            ref[...] = jnp.zeros_like(ref)
        out = node_out[...]
        own_low = own_edge_grad[...].astype(low)
        back_low = back_edge[...].astype(low)
        put("edge_own", dot_rows(own_low, out))
        put("edge_near", dot_rows(back_low, out))
        pad = jnp.zeros((narrow, width // 2 - narrow), wide)
        put("edge_a", jnp.concatenate([e_in[...], pad, e_mid[...], pad], axis=1))
        put("edge_b", jnp.concatenate([e_out[...], pad, jnp.zeros((narrow, width // 2), wide)], axis=1))
        put_line("e_vectors", e_vectors[...])
        grad = (
            cotangent[...].astype(wide)
            + dot(own_low, w_edge[:, 0:width])
            + dot(back_low, w_edge[:, width : 2 * width])
        )
        hat, scale = norm_stats(second_sum[...])
        put_line("v_final_gain", jnp.sum(grad * hat, axis=0, keepdims=True))
        put_line("v_final_shift", jnp.sum(grad, axis=0, keepdims=True))
        second = norm_back(hat, scale, as_row(gain_two), grad)
        down = second.astype(low)
        put_line("v_down", jnp.sum(down.astype(wide), axis=0, keepdims=True))
        put("feed_down", dot_rows(up_act[...], down))
        up = (up_slope[...] * dot_back(down, w_down[...])).astype(low)
        bias_up = jnp.sum(up.astype(wide), axis=0, keepdims=True)
        hat, scale = norm_stats(resid[...])
        normed = (hat * as_row(gain_one) + as_row(shift_one)).astype(low)
        for piece in range(hidden // width):
            part = slice(piece * width, (piece + 1) * width)
            lines[layout["v_up"] + piece : layout["v_up"] + piece + 1, :] = bias_up[:, part]
            here = layout["feed_up"] + piece * width
            packed[here : here + width, :] = dot_rows(normed, up[:, part]).astype(low)
        first = second + dot_back(up, w_up[...])
        put_line("v_node_gain", jnp.sum(first * hat, axis=0, keepdims=True))
        put_line("v_node_shift", jnp.sum(first, axis=0, keepdims=True))
        mixed = norm_back(hat, scale, as_row(gain_one), first)
        node_part[...] = mixed
        masked = as_column(masks[...], count).astype(wide) * mixed
        put_line("v_out", jnp.sum(jnp.where(live > 0, masked, 0.0), axis=0, keepdims=True))
        put("message_out", dot_rows(mixed_low[...], masked.astype(low)))
        shared = (masked / jnp.maximum(live, 1).astype(wide)).astype(low)
        level[...] = dot_back(shared, w_out[...])

    lift = level[...]
    slope = slope_two[...].astype(wide)
    mid = jnp.concatenate(
        [jnp.where(live > step * slots + s, slope[s] * lift, 0.0).astype(low) for s in range(slots)], axis=0
    )
    flat_one = act_one[...].reshape(slots * count, width)
    g_mid[...] += dot_rows(flat_one, mid)
    bias_mid[...] += jnp.sum(mid.astype(wide), axis=0, keepdims=True)
    slope = slope_one[...].reshape(slots * count, width).astype(wide)
    inner = (slope * dot_back(mid, w_mid[...])).astype(low)
    own_sum[...] += jnp.sum(inner.astype(wide).reshape(slots, count, width), axis=0)
    flat = edges[...].reshape(slots * count, narrow)
    g_edge[...] += dot_rows(flat, inner)
    edge_grad[...] = partial[...] + dot_back(inner, w_in[2 * width :]).reshape(slots, count, narrow)
    spread_sum[...] += dot(pick_columns(rows[0], total), inner)

    @pl.when(step == pl.num_programs(0) - 1)
    def _():
        spread_low = spread_sum[...].astype(low)
        spread[...] = spread_low
        own_low = own_sum[...].astype(low)
        put("message_in", dot_rows(nodes[...], own_low))
        put("message_near", dot_rows(table[...], spread_low))
        put("message_edge", g_edge[...])
        put("message_mid", g_mid[...])
        put_line("v_mid", bias_mid[...])
        put_line("v_in", jnp.sum(own_sum[...], axis=0, keepdims=True))
        here = layout["lines"]
        tall = lines.shape[0]
        packed[here : here + tall, :] = lines[...].astype(low)
        rest = packed.shape[0] - here - tall
        if rest:
            packed[here + tall :, :] = jnp.zeros((rest, width), low)
        node_part[...] += dot_back(own_low, w_in[0:width])


def lay_out(width, narrow, hidden, shares):
    pieces = hidden // width
    sizes = [
        ("message_in", width), ("message_near", width), ("message_edge", narrow), ("message_mid", width),
        ("message_out", width), ("feed_down", hidden), ("feed_up", pieces * width), ("edge_own", narrow),
        ("edge_near", narrow), ("edge_a", narrow), ("edge_b", narrow), ("lines", 32),
    ]
    layout, row = {}, 0
    for name, size in sizes:
        layout[name] = row
        row += size
    layout["rows"] = -(-row // shares) * shares
    layout["e_vectors"] = 0
    layout["v_up"] = 8
    singles = ("v_final_gain", "v_final_shift", "v_down", "v_node_gain", "v_node_shift", "v_out", "v_mid", "v_in")
    for place, name in enumerate(singles):
        layout[name] = 8 + pieces + place
    return layout


def unpack(layout, packed, *outs):
    (m_in, m_in_b, m_mid, m_mid_b, m_out, m_out_b, n_gain, n_shift, f_up, f_up_b, f_down, f_down_b,
     l_gain, l_shift, e_in, e_in_b, e_mid, e_mid_b, e_out, e_out_b, e_gain, e_shift) = outs
    width = m_mid.shape[0]
    narrow = e_mid.shape[0]
    hidden = f_up.shape[1]
    half = width // 2

    def big(name, tall, lanes=slice(None)):
        return packed[layout[name] : layout[name] + tall, lanes].astype(wide)

    m_in[0:width] = big("message_in", width)
    m_in[width : 2 * width] = big("message_near", width)
    m_in[2 * width :] = big("message_edge", narrow)
    m_mid[...] = big("message_mid", width)
    m_out[...] = big("message_out", width)
    f_down[...] = big("feed_down", hidden)
    for piece in range(hidden // width):
        here = layout["feed_up"] + piece * width
        f_up[:, piece * width : (piece + 1) * width] = packed[here : here + width, :].astype(wide)
    e_in[:, 0:width] = big("edge_own", narrow)
    e_in[:, width : 2 * width] = big("edge_near", narrow)
    e_in[:, 2 * width :] = big("edge_a", narrow, slice(0, narrow))
    e_mid[...] = big("edge_a", narrow, slice(half, half + narrow))
    e_out[...] = big("edge_b", narrow, slice(0, narrow))
    lines = packed[layout["lines"] : layout["lines"] + 32, :].astype(wide)

    def one(name):
        return lines[layout[name]]

    m_in_b[...] = one("v_in")
    m_mid_b[...] = one("v_mid")
    m_out_b[...] = one("v_out")
    n_gain[...] = one("v_node_gain")
    n_shift[...] = one("v_node_shift")
    l_gain[...] = one("v_final_gain")
    l_shift[...] = one("v_final_shift")
    f_down_b[...] = one("v_down")
    for piece in range(hidden // width):
        f_up_b[piece * width : (piece + 1) * width] = lines[layout["v_up"] + piece]
    for place, ref in enumerate((e_gain, e_shift, e_out_b, e_mid_b, e_in_b)):
        ref[...] = lines[place, 0:narrow]


def table_kernel(grid, own, table, *sems):
    spot = Spot(grid)
    copy = pltpu.make_async_copy(own, table.at[spot.z, spot.y, spot.x], sems[-1])
    copy.start()
    meet(spot.peers())
    copy.wait()
    for copy in gather_blocks(spot, table, sems[:-1]):
        copy.wait_send()


def owner_kernel(grid, part, out, *scratch):
    spot = Spot(grid)
    meet(spot.peers())
    (upper, lower), sent = scatter_sums(spot, part, scratch)
    out[0] = upper
    out[1] = lower
    for copy in sent:
        copy.wait_send()


def owner_nodes_kernel(grid, part, node_part, w_near, out, *scratch):
    spot = Spot(grid)
    meet(spot.peers())
    sums, sent = scatter_sums(spot, part, scratch)
    for half in range(2):
        out[half] = node_part[half] + dot_back(sums[half].astype(low), w_near[...])
    for copy in sent:
        copy.wait_send()


def total_kernel(grid, given, out, pair, pair_send, pair_arrive, last_send, last_arrive, *rest):
    spot = Spot(grid)
    scratch, sems = rest[:18], rest[18:]
    partner = (1 - spot.core, lax.axis_index("res"))
    meet(spot.peers() + [partner])
    core = spot.core
    mine = out.at[core]
    pairs = []
    for j in list(range(1, grid[0])) + [0]:
        zj = (spot.z + j) % grid[0]
        copy = remote(given.at[1 - core, zj], pair.at[zj], pair_send.at[j], pair_arrive.at[j], partner)
        copy.start()
        pairs.append(copy)
    waiting = iter(pairs)

    def before(zj, j, sent):
        next(waiting).wait_recv()
        mine[zj] = (given[core, zj].astype(wide) + pair[zj].astype(wide)).astype(low)

    sums, sent = scatter_sums(spot, mine, scratch, before)
    for copy in pairs + sent:
        copy.wait_send()
    for half in range(2):
        mine[spot.z, spot.y, spot.x, half] = sums[half].astype(low)
    finals = []

    def plane(zj, j, sent):
        copy = remote(mine.at[zj], mine.at[zj], last_send.at[j], last_arrive.at[j], partner)
        copy.start()
        finals.append(copy)

    sent = gather_blocks(spot, mine, sems, plane)
    for copy in finals:
        copy.wait_recv()
    for copy in finals + sent:
        copy.wait_send()


vmem = pl.BlockSpec(memory_space=pltpu.VMEM)
most_vmem = 63 << 20


def params(collective=None, **more):
    if collective is None:
        return pltpu.CompilerParams(vmem_limit_bytes=most_vmem, **more)
    return pltpu.CompilerParams(
        collective_id=collective, has_side_effects=True, vmem_limit_bytes=most_vmem, **more
    )


def gather_table(grid, rows, collective):
    count, width = rows.shape
    table = pl.pallas_call(
        functools.partial(table_kernel, grid),
        out_shape=jax.ShapeDtypeStruct(grid + (2, count // 2, width), low),
        in_specs=[vmem],
        out_specs=vmem,
        scratch_shapes=gather_sems(grid) + [pltpu.SemaphoreType.DMA],
        compiler_params=params(collective),
        name="gather_table_%d" % width,
    )(rows.reshape(2, count // 2, width))
    return table.reshape(-1, width)


def held(array):
    return pl.BlockSpec(array.shape, lambda step, dims=len(array.shape): (0,) * dims, pipeline_mode=pl.Buffered(1))


def streamed(array, slots):
    return pl.BlockSpec((slots,) + array.shape[1:], lambda step, dims=len(array.shape): (step,) + (0,) * (dims - 1))


def call(kernel, name, steps, slots, inputs, outputs, scratch):
    def spec(item, flow):
        return streamed(item, slots if item.shape[0] != steps else 1) if flow else held(item)
    return pl.pallas_call(
        kernel,
        grid=(steps,),
        in_specs=[spec(item, flow) for item, flow in inputs],
        out_specs=[spec(item, flow) for item, flow in outputs],
        out_shape=[item for item, _ in outputs],
        scratch_shapes=scratch,
        compiler_params=params(),
        name=name,
    )(*[item for item, _ in inputs])


def per_device(
    node_states, edge_states, neighbours, residue_mask, neighbour_count,
    message_in, message_in_bias, message_mid, message_mid_bias, message_out, message_out_bias,
    node_gain, node_shift, feed_up, feed_up_bias, feed_down, feed_down_bias, final_gain, final_shift,
    edge_in, edge_in_bias, edge_mid, edge_mid_bias, edge_out, edge_out_bias, edge_gain, edge_shift,
    node_cotangent, edge_cotangent,
):
    grid = chip_grid(lax.axis_size("res"))
    nodes = node_states[0]
    count, width = nodes.shape
    edges = jnp.transpose(edge_states[0], (1, 0, 2))
    edge_ct = jnp.transpose(edge_cotangent[0], (1, 0, 2))
    depth, _, narrow = edges.shape
    hidden = feed_up.shape[1]
    slots = 12
    steps = depth // slots
    total = grid[0] * grid[1] * grid[2] * count
    index = neighbours[0]
    rows = jnp.transpose(index).reshape(steps, 1, slots * count)
    edge_in_t = jnp.transpose(edge_in)
    lanes = -(-narrow // 128) * 128
    shape = jax.ShapeDtypeStruct
    slab = shape((depth, count, width), low)
    node_low, node_wide = shape((count, width), low), shape((count, width), wide)
    scratch = pltpu.VMEM

    table = gather_table(grid, nodes, 0)
    (slope_one, slope_two, act_one, mixed_low, resid, second_sum, up_act, up_slope, node_out, sent, own_edge) = call(
        functools.partial(message_forward, slots), "message_forward", steps, slots,
        [(index, False), (neighbour_count, False), (residue_mask, False), (nodes, False), (table, False), (edges, True)]
        + [(a, False) for a in (
            message_in, message_in_bias, message_mid, message_mid_bias, message_out, message_out_bias,
            node_gain, node_shift, feed_up, feed_up_bias, feed_down, feed_down_bias, final_gain, final_shift,
            edge_in_t, edge_in_bias)],
        [(slab, True)] * 3 + [(node_low, False), (node_wide, False), (node_wide, False),
         (shape((count, hidden), low), False), (shape((count, hidden), wide), False), (node_low, False),
         (shape((count, lanes), low), False), (shape((count, narrow), wide), False)],
        [scratch((total, width), low), scratch((count, width), wide), scratch((count, width), wide)],
    )
    sent_table = gather_table(grid, sent, 1)
    square = shape((narrow, narrow), wide)
    (edge_result, partial, spread_two, own_edge_grad, e_in, e_mid, e_out, e_vectors) = call(
        functools.partial(edge_pass, slots), "edge_pass", steps, slots,
        [(index, False), (rows, True), (sent_table, False), (own_edge, False), (edges, True), (edge_ct, True)]
        + [(a, False) for a in (edge_in_t, edge_mid, edge_mid_bias, edge_out, edge_out_bias, edge_gain, edge_shift)],
        [(shape(edges.shape, low), True), (shape(edges.shape, wide), True), (shape((total, lanes), low), False),
         (shape((count, narrow), wide), False), (square, False), (square, False), (square, False),
         (shape((8, narrow), wide), False)],
        [scratch((total, narrow), wide)],
    )
    back_edge = pl.pallas_call(
        functools.partial(owner_kernel, grid),
        out_shape=shape((2, count // 2, lanes), wide),
        in_specs=[vmem], out_specs=vmem,
        scratch_shapes=scatter_scratch(grid, count // 2, lanes),
        compiler_params=params(2), name="edge_owner",
    )(spread_two.reshape(grid + (2, count // 2, lanes))).reshape(count, lanes)[:, :narrow]
    shares = 4 * grid[0] * grid[1] * grid[2] * 16
    layout = lay_out(width, narrow, hidden, shares)
    (edge_grad, spread, node_part, packed) = call(
        functools.partial(node_backward, slots, layout), "node_backward", steps, slots,
        [(rows, True), (neighbour_count, False), (residue_mask, False), (nodes, False), (table, False), (edges, True),
         (slope_one, True), (slope_two, True), (act_one, True), (partial, True)]
        + [(a, False) for a in (
            mixed_low, resid, second_sum, up_act, up_slope, node_out, node_cotangent[0], back_edge, own_edge_grad,
            e_in, e_mid, e_out, e_vectors, message_in, message_mid, message_out, node_gain, node_shift,
            feed_up, feed_down, final_gain, edge_in_t)],
        [(shape(edges.shape, wide), True), (shape((total, width), low), False), (node_wide, False),
         (shape((layout["rows"], width), low), False)],
        [scratch((count, width), wide), scratch((total, width), wide), scratch((count, width), wide),
         scratch((width, width), wide), scratch((narrow, width), wide), scratch((1, width), wide),
         scratch((32, width), wide)],
    )
    grad_nodes = pl.pallas_call(
        functools.partial(owner_nodes_kernel, grid),
        out_shape=shape((2, count // 2, width), wide),
        in_specs=[vmem] * 3, out_specs=vmem,
        scratch_shapes=scatter_scratch(grid, count // 2, width),
        compiler_params=params(3), name="node_owner",
    )(spread.reshape(grid + (2, count // 2, width)), node_part.reshape(2, count // 2, width),
      message_in[width : 2 * width]).reshape(count, width)
    chunk = layout["rows"] // (4 * grid[0] * grid[1] * grid[2])
    dma = pltpu.SemaphoreType.DMA
    blocks = grid + (2, chunk, width)
    summed = pl.pallas_call(
        functools.partial(total_kernel, grid),
        out_shape=shape((2,) + blocks, low),
        in_specs=[vmem], out_specs=vmem,
        scratch_shapes=[scratch(blocks, low)] + [dma((grid[0],))] * 4
        + scatter_scratch(grid, chunk, width) + gather_sems(grid),
        compiler_params=params(4), name="grad_total",
    )(packed.reshape((2,) + blocks)).reshape(layout["rows"], width)
    vector, line = shape((width,), wide), shape((narrow,), wide)
    grads = pl.pallas_call(
        functools.partial(unpack, layout),
        out_shape=[
            shape(message_in.shape, wide), vector, shape(message_mid.shape, wide), vector,
            shape(message_out.shape, wide), vector, vector, vector, shape(feed_up.shape, wide), shape((hidden,), wide),
            shape(feed_down.shape, wide), vector, vector, vector, shape(edge_in_t.shape, wide), line,
            square, line, square, line, line, line,
        ],
        in_specs=[vmem], out_specs=[vmem] * 22,
        compiler_params=params(), name="unpack",
    )(summed)
    grads = list(grads)
    grads[14] = jnp.transpose(grads[14])
    back = (1, 0, 2)
    return (
        node_out[None],
        jnp.transpose(edge_result, back)[None],
        grad_nodes[None],
        jnp.transpose(edge_grad, back)[None],
        *grads,
    )


def solution(mesh):
    split, whole = P("batch", "res"), P()
    in_specs = (split,) * 5 + (whole,) * 22 + (split,) * 2
    out_specs = (split,) * 4 + (whole,) * 22
    return jax.shard_map(per_device, mesh=mesh, in_specs=in_specs, out_specs=out_specs, check_vma=False)
```

```python
import functools
import jax
import jax.numpy as jnp
from jax import lax
from jax.experimental import pallas as pl
from jax.experimental.pallas import tpu as pltpu
from jax.sharding import PartitionSpec as P

MESH = pl.DeviceIdType.MESH
low = jnp.bfloat16
wide = jnp.float32


def chip_grid(count):
    side_x = 2 if count < 64 else 4
    side_y = side_x
    return (count // (side_x * side_y), side_y, side_x)


class Spot:
    def __init__(self, grid):
        self.grid = grid
        side_z, side_y, side_x = grid
        me = lax.axis_index("res")
        self.core = lax.axis_index("batch")
        self.z = me // (side_y * side_x)
        self.y = (me // side_x) % side_y
        self.x = me % side_x

    def device(self, z, y, x):
        return (self.core, (z * self.grid[1] + y) * self.grid[2] + x)

    def far_z(self, step):
        return (self.z + step) % self.grid[0]

    def far_y(self, step):
        return (self.y + step) % self.grid[1]

    def far_x(self, step):
        return (self.x + step) % self.grid[2]

    def peers(self):
        found = [self.device(self.far_z(s), self.y, self.x) for s in range(1, self.grid[0])]
        found += [self.device(self.z, self.far_y(s), self.x) for s in range(1, self.grid[1])]
        found += [self.device(self.z, self.y, self.far_x(s)) for s in range(1, self.grid[2])]
        return found


def greet(peers):
    barrier = pltpu.get_barrier_semaphore()
    for peer in peers:
        pl.semaphore_signal(barrier, inc=1, device_id=peer, device_id_type=MESH)


def met(peers):
    pl.semaphore_wait(pltpu.get_barrier_semaphore(), len(peers))


def meet(peers):
    greet(peers)
    met(peers)


def remote(source, target, send, arrive, device):
    return pltpu.make_async_remote_copy(
        src_ref=source, dst_ref=target, send_sem=send, recv_sem=arrive,
        device_id=device, device_id_type=MESH,
    )


def gather_sems(grid):
    side_z, side_y, side_x = grid
    dma = pltpu.SemaphoreType.DMA
    shapes = [(side_z - 1,), (side_z, side_x - 1), (side_z, side_y - 1), (side_z, side_y - 1), (side_z, side_x - 1)]
    return [dma(s) for s in shapes for _ in range(2)]


def gather_plan(spot, table, sems):
    (s1, r1, s2a, r2a, s2b, r2b, s3a, r3a, s3b, r3b) = sems
    side_z, side_y, side_x = spot.grid
    z, y, x = spot.z, spot.y, spot.x

    def push(view, send, arrive, device):
        return remote(view, view, send, arrive, device)

    ups = [
        push(table.at[z, y, x], s1.at[s - 1], r1.at[s - 1], spot.device(spot.far_z(s), y, x))
        for s in range(1, side_z)
    ]
    firsts, lasts = [], []
    for j in range(side_z):
        zj = (z - j) % side_z
        firsts.append(
            [
                push(table.at[zj, y, x, 0], s2a.at[j, s - 1], r2a.at[j, s - 1], spot.device(z, y, spot.far_x(s)))
                for s in range(1, side_x)
            ]
            + [
                push(table.at[zj, y, x, 1], s2b.at[j, s - 1], r2b.at[j, s - 1], spot.device(z, spot.far_y(s), x))
                for s in range(1, side_y)
            ]
        )
        lasts.append(
            [
                push(table.at[zj, y, :, 0], s3a.at[j, s - 1], r3a.at[j, s - 1], spot.device(z, spot.far_y(s), x))
                for s in range(1, side_y)
            ]
            + [
                push(table.at[zj, :, x, 1], s3b.at[j, s - 1], r3b.at[j, s - 1], spot.device(z, y, spot.far_x(s)))
                for s in range(1, side_x)
            ]
        )
    return ups, firsts, lasts


def start_all(copies):
    for copy in copies:
        copy.start()


def arrived(copies):
    for copy in copies:
        copy.wait_recv()


def all_sent(copies):
    for copy in copies:
        copy.wait_send()


def flat(groups):
    return [copy for group in groups for copy in group]


def gather_run(plan, on_plane=None):
    ups, firsts, lasts = plan
    start_all(ups + firsts[0])
    yield
    for j in range(1, len(firsts)):
        arrived([ups[j - 1]])
        start_all(firsts[j])
    yield
    for j in range(len(lasts)):
        arrived(firsts[j])
        start_all(lasts[j])
    yield
    for j in range(len(lasts)):
        arrived(lasts[j])
        if on_plane is not None:
            on_plane(j)
    yield
    all_sent(ups + flat(firsts) + flat(lasts))


def drive(run):
    for _ in run:
        pass


def scatter_scratch(grid, rows, width):
    side_z, side_y, side_x = grid
    dma = pltpu.SemaphoreType.DMA
    shapes = [(side_z, side_y - 1), (side_z, side_x - 1), (side_z, side_x - 1), (side_z, side_y - 1), (side_z - 1,)]
    buffers = [
        pltpu.VMEM((side_z, side_y - 1, side_x, rows, width), low),
        pltpu.VMEM((side_z, side_x - 1, side_y, rows, width), low),
        pltpu.VMEM((side_z, side_x, rows, width), low),
        pltpu.VMEM((side_z, side_y, rows, width), low),
        pltpu.VMEM((side_z, side_x - 1, rows, width), low),
        pltpu.VMEM((side_z, side_y - 1, rows, width), low),
        pltpu.VMEM((side_z, 2, rows, width), low),
        pltpu.VMEM((side_z - 1, 2, rows, width), low),
    ]
    return buffers + [dma(s) for s in shapes for _ in range(2)]


def scatter_run(spot, part, scratch, result, before_plane=None):
    (ra1, rb1, ka, kb, ra2, rb2, tot, r3, s1a, q1a, s1b, q1b, s2a, q2a, s2b, q2b, s3, q3) = scratch
    side_z, side_y, side_x = spot.grid
    z, y, x = spot.z, spot.y, spot.x
    sent = []

    def go(copy):
        copy.start()
        sent.append(copy)
        return copy

    order = list(range(1, side_z)) + [0]
    one, two, three = {}, {}, []
    for j in order:
        zj = (z + j) % side_z
        if before_plane is not None:
            before_plane(zj, j)
        a = [
            go(remote(part.at[zj, spot.far_y(s), :, 0], ra1.at[j, s - 1], s1a.at[j, s - 1], q1a.at[j, s - 1],
                      spot.device(z, spot.far_y(s), x)))
            for s in range(1, side_y)
        ]
        b = [
            go(remote(part.at[zj, :, spot.far_x(s), 1], rb1.at[j, s - 1], s1b.at[j, s - 1], q1b.at[j, s - 1],
                      spot.device(z, y, spot.far_x(s))))
            for s in range(1, side_x)
        ]
        one[j] = (a, b)
    yield
    for j in order:
        zj = (z + j) % side_z
        arrived(one[j][0])
        total = part[zj, y, :, 0].astype(wide)
        for s in range(side_y - 1):
            total = total + ra1[j, s].astype(wide)
        ka[j] = total.astype(low)
        a = [
            go(remote(ka.at[j, spot.far_x(s)], ra2.at[j, s - 1], s2a.at[j, s - 1], q2a.at[j, s - 1],
                      spot.device(z, y, spot.far_x(s))))
            for s in range(1, side_x)
        ]
        arrived(one[j][1])
        total = part[zj, :, x, 1].astype(wide)
        for s in range(side_x - 1):
            total = total + rb1[j, s].astype(wide)
        kb[j] = total.astype(low)
        b = [
            go(remote(kb.at[j, spot.far_y(s)], rb2.at[j, s - 1], s2b.at[j, s - 1], q2b.at[j, s - 1],
                      spot.device(z, spot.far_y(s), x)))
            for s in range(1, side_y)
        ]
        two[j] = a + b
    yield
    for j in order:
        zj = (z + j) % side_z
        arrived(two[j])
        upper = ka[j, x].astype(wide)
        for s in range(side_x - 1):
            upper = upper + ra2[j, s].astype(wide)
        lower = kb[j, y].astype(wide)
        for s in range(side_y - 1):
            lower = lower + rb2[j, s].astype(wide)
        if j:
            tot[j, 0] = upper.astype(low)
            tot[j, 1] = lower.astype(low)
            three.append(
                go(remote(tot.at[j], r3.at[j - 1], s3.at[j - 1], q3.at[j - 1], spot.device(zj, y, x)))
            )
    yield
    arrived(three)
    for s in range(side_z - 1):
        upper = upper + r3[s, 0].astype(wide)
        lower = lower + r3[s, 1].astype(wide)
    result += [upper, lower]
    all_sent(sent)
eps_norm = 1e-05
root_half = 0.7071067811865476
root_turn = 0.3989422804014327


def dot(left, right):
    return jnp.dot(left, right, preferred_element_type=wide)


def dot_back(left, right):
    return lax.dot_general(left, right, (((1,), (1,)), ((), ())), preferred_element_type=wide)


def dot_rows(left, right):
    return lax.dot_general(left, right, (((0,), (0,)), ((), ())), preferred_element_type=wide)


def gelu_pair(values):
    share = 0.5 + 0.5 * lax.erf(values * root_half)
    slope = share + values * (jnp.exp(values * values * -0.5) * root_turn)
    return values * share, slope


def norm_stats(values):
    centre = jnp.mean(values, axis=-1, keepdims=True)
    centred = values - centre
    variance = jnp.mean(centred * centred, axis=-1, keepdims=True)
    scale = lax.rsqrt(variance + eps_norm)
    return centred * scale, scale


def norm_back(hat, scale, gain, grad):
    inner = grad * gain
    return scale * (
        inner
        - jnp.mean(inner, axis=-1, keepdims=True)
        - hat * jnp.mean(inner * hat, axis=-1, keepdims=True)
    )


def as_row(ref, start=None, size=None):
    return ref[...].astype(wide).reshape(1, ref.shape[0])


def as_column(row, count):
    rows = lax.broadcasted_iota(jnp.int32, (count, count), 0)
    lanes = lax.broadcasted_iota(jnp.int32, (count, count), 1)
    return jnp.sum(jnp.where(rows == lanes, jnp.broadcast_to(row, (count, count)), 0), axis=1, keepdims=True)


def slot_column(index, slot):
    lanes = lax.broadcasted_iota(jnp.int32, index.shape, 1)
    return jnp.sum(jnp.where(lanes == slot, index, 0), axis=1, keepdims=True)


def pick_rows(index, first, slots, total):
    count = index.shape[0]
    lanes = lax.broadcasted_iota(jnp.int32, (count, total), 1)
    return jnp.concatenate(
        [jnp.where(slot_column(index, first + s) == lanes, 1.0, 0.0).astype(low) for s in range(slots)], axis=0
    )


def pick_columns(row, total):
    rows = lax.broadcasted_iota(jnp.int32, (total, row.shape[1]), 0)
    return jnp.where(rows == row, 1.0, 0.0).astype(low)


def message_forward(
    slots, index, counts, masks, nodes, table, edges, w_in, b_in, w_mid, b_mid, w_out, b_out,
    gain_one, shift_one, w_up, b_up, w_down, b_down, gain_two, shift_two, w_edge, b_edge,
    slope_one, slope_two, act_one, mixed_low, resid, second_sum, up_slope, node_out, sent, own_edge,
    projected, own, pooled,
):
    step = pl.program_id(0)
    count, width = nodes.shape
    total = table.shape[0]
    live = as_column(counts[...], count)

    @pl.when(step == 0)
    def _():
        projected[...] = dot(table[...], w_in[width : 2 * width]).astype(low)
        own[...] = dot(nodes[...], w_in[0:width]) + as_row(b_in)
        pooled[...] = jnp.zeros_like(pooled)

    picks = pick_rows(index[...], step * slots, slots, total)
    edge_rows = edges[...].reshape(slots * count, edges.shape[2])
    pre = dot(picks, projected[...]) + dot(edge_rows, w_in[2 * width :])
    pre = pre.reshape(slots, count, width) + own[...][None]
    act, slope = gelu_pair(pre)
    act = act.astype(low)
    act_one[...] = act
    slope_one[...] = slope.astype(low)
    pre = dot(act.reshape(slots * count, width), w_mid[...]) + as_row(b_mid)
    act, slope = gelu_pair(pre)
    act = act.reshape(slots, count, width)
    slope_two[...] = slope.astype(low).reshape(slots, count, width)
    gathered = pooled[...]
    for s in range(slots):
        gathered = gathered + jnp.where(live > step * slots + s, act[s], 0.0)
    pooled[...] = gathered

    @pl.when(step == pl.num_programs(0) - 1)
    def _():
        mean = pooled[...] / jnp.maximum(live, 1).astype(wide)
        mean_low = mean.astype(low)
        mixed_low[...] = mean_low
        some = jnp.where(live > 0, 1.0, 0.0)
        mask = as_column(masks[...], count).astype(wide)
        aggregate = dot(mean_low, w_out[...]) + some * as_row(b_out)
        total_sum = nodes[...].astype(wide) + mask * aggregate
        resid[...] = total_sum
        hat, _ = norm_stats(total_sum)
        first = hat * as_row(gain_one) + as_row(shift_one)
        up = dot(first.astype(low), w_up[...]) + as_row(b_up)
        act_up, slope_up = gelu_pair(up)
        act_up = act_up.astype(low)
        up_slope[...] = slope_up
        summed = first + dot(act_up, w_down[...]) + as_row(b_down)
        second_sum[...] = summed
        hat, _ = norm_stats(summed)
        out = (hat * as_row(gain_two) + as_row(shift_two)).astype(low)
        node_out[...] = out
        pad = jnp.zeros((count, sent.shape[1] - w_edge.shape[0]), low)
        sent[...] = jnp.concatenate([dot_back(out, w_edge[:, width : 2 * width]).astype(low), pad], axis=1)
        own_edge[...] = dot_back(out, w_edge[:, 0:width]) + as_row(b_edge)


def edge_pass(
    slots, index, rows, table, own_edge, edges, cotangent, w_edge, w_mid, b_mid, w_out, b_out, gain, shift,
    result, partial, spread, own_grad, g_in, g_mid, g_out, vectors, spread_sum,
):
    step = pl.program_id(0)
    count, width = own_edge.shape
    total = table.shape[0]
    base = w_edge.shape[1] - width

    @pl.when(step == 0)
    def _():
        spread_sum[...] = jnp.zeros_like(spread_sum)
        for ref in (own_grad, g_in, g_mid, g_out, vectors):
            ref[...] = jnp.zeros_like(ref)

    w_here = w_edge[:, base:]
    picks = pick_rows(index[...], step * slots, slots, total)
    edge_rows = edges[...].reshape(slots * count, width)
    pre = dot(picks, table[...])[:, 0:width] + dot_back(edge_rows, w_here)
    pre = (pre.reshape(slots, count, width) + own_edge[...][None]).reshape(slots * count, width)
    act_one, slope_one = gelu_pair(pre)
    act_one = act_one.astype(low)
    pre = dot(act_one, w_mid[...]) + as_row(b_mid)
    act_two, slope_two = gelu_pair(pre)
    act_two = act_two.astype(low)
    pre = dot(act_two, w_out[...]) + as_row(b_out)
    hat, scale = norm_stats(edge_rows.astype(wide) + pre)
    gain_row = as_row(gain)
    result[...] = (hat * gain_row + as_row(shift)).astype(low).reshape(slots, count, width)
    grad = cotangent[...].reshape(slots * count, width).astype(wide)
    sum_grad = norm_back(hat, scale, gain_row, grad)
    three = sum_grad.astype(low)
    g_out[...] += dot_rows(act_two, three)
    two = (slope_two * dot_back(three, w_out[...])).astype(low)
    g_mid[...] += dot_rows(act_one, two)
    one = (slope_one * dot_back(two, w_mid[...])).astype(low)
    g_in[...] += dot_rows(one, edge_rows)
    vectors[...] += jnp.concatenate(
        [
            jnp.sum(piece, axis=0, keepdims=True)
            for piece in (grad * hat, grad, three.astype(wide), two.astype(wide), one.astype(wide))
        ]
        + [jnp.zeros((3, width), wide)],
        axis=0,
    )
    own_grad[...] += jnp.sum(one.astype(wide).reshape(slots, count, width), axis=0)
    partial[...] = (sum_grad + dot(one, w_here)).reshape(slots, count, width)
    spread_sum[...] += dot(pick_columns(rows[0], total), one)

    @pl.when(step == pl.num_programs(0) - 1)
    def _():
        pad = jnp.zeros((total, spread.shape[1] - width), low)
        spread[...] = jnp.concatenate([spread_sum[...].astype(low), pad], axis=1)


def node_backward(
    grid, slots, layout, rows, counts, masks, nodes, table, edges, slope_one, slope_two, act_one, partial,
    mixed_low, resid, second_sum, up_slope, node_out, cotangent, back_edge, own_edge_grad,
    e_in, e_mid, e_out, e_vectors,
    w_in, w_mid, w_out, gain_one, shift_one, w_up, w_down, gain_two, w_edge,
    edge_grad, spread, node_part, packed, feed_table,
    level, spread_sum, own_sum, g_mid, g_edge, bias_mid, lines, held_table, *sems,
):
    step = pl.program_id(0)
    last = pl.num_programs(0) - 1
    spot = Spot(grid)
    peers = spot.peers()
    ups, firsts, lasts = gather_plan(spot, held_table, sems)
    count, width = nodes.shape
    total = table.shape[0]
    narrow = w_edge.shape[0]
    hidden = w_up.shape[1]
    live = as_column(counts[...], count)

    def put(name, value):
        row = layout[name]
        packed[row : row + value.shape[0], :] = value.astype(low)

    def put_line(name, value):
        row = layout[name]
        lines[row : row + value.shape[0], 0 : value.shape[1]] = value

    @pl.when(step == 0)
    def _():
        greet(peers)
        for ref in (spread_sum, own_sum, g_mid, g_edge, bias_mid, lines):
            ref[...] = jnp.zeros_like(ref)
        out = node_out[...]
        own_low = own_edge_grad[...].astype(low)
        back_low = back_edge[...].astype(low)
        put("edge_own", dot_rows(own_low, out))
        put("edge_near", dot_rows(back_low, out))
        pad = jnp.zeros((narrow, width // 2 - narrow), wide)
        put("edge_a", jnp.concatenate([e_in[...], pad, e_mid[...], pad], axis=1))
        put("edge_b", jnp.concatenate([e_out[...], pad, jnp.zeros((narrow, width // 2), wide)], axis=1))
        put_line("e_vectors", e_vectors[...])
        grad = (
            cotangent[...].astype(wide)
            + dot(own_low, w_edge[:, 0:width])
            + dot(back_low, w_edge[:, width : 2 * width])
        )
        hat, scale = norm_stats(second_sum[...])
        put_line("v_final_gain", jnp.sum(grad * hat, axis=0, keepdims=True))
        put_line("v_final_shift", jnp.sum(grad, axis=0, keepdims=True))
        second = norm_back(hat, scale, as_row(gain_two), grad)
        down = second.astype(low)
        put_line("v_down", jnp.sum(down.astype(wide), axis=0, keepdims=True))
        held_table[spot.z, spot.y, spot.x, 1] = down
        up = (up_slope[...] * dot_back(down, w_down[...])).astype(low)
        bias_up = jnp.sum(up.astype(wide), axis=0, keepdims=True)
        hat, scale = norm_stats(resid[...])
        normed = (hat * as_row(gain_one) + as_row(shift_one)).astype(low)
        held_table[spot.z, spot.y, spot.x, 0] = normed
        met(peers)
        start_all(ups + firsts[0])
        for piece in range(hidden // width):
            lines[layout["v_up"] + piece : layout["v_up"] + piece + 1, :] = bias_up[:, piece * width : (piece + 1) * width]
        first = second + dot_back(up, w_up[...])
        put_line("v_node_gain", jnp.sum(first * hat, axis=0, keepdims=True))
        put_line("v_node_shift", jnp.sum(first, axis=0, keepdims=True))
        mixed = norm_back(hat, scale, as_row(gain_one), first)
        node_part[...] = mixed
        masked = as_column(masks[...], count).astype(wide) * mixed
        put_line("v_out", jnp.sum(jnp.where(live > 0, masked, 0.0), axis=0, keepdims=True))
        put("message_out", dot_rows(mixed_low[...], masked.astype(low)))
        shared = (masked / jnp.maximum(live, 1).astype(wide)).astype(low)
        level[...] = dot_back(shared, w_out[...])

    @pl.when(step == 1)
    def _():
        for j in range(1, len(firsts)):
            arrived([ups[j - 1]])
            start_all(firsts[j])

    @pl.when(step == 2)
    def _():
        for j in range(len(lasts)):
            arrived(firsts[j])
            start_all(lasts[j])

    lift = level[...]
    slope = slope_two[...].astype(wide)
    mid = jnp.concatenate(
        [jnp.where(live > step * slots + s, slope[s] * lift, 0.0).astype(low) for s in range(slots)], axis=0
    )
    flat_one = act_one[...].reshape(slots * count, width)
    g_mid[...] += dot_rows(flat_one, mid)
    bias_mid[...] += jnp.sum(mid.astype(wide), axis=0, keepdims=True)
    slope = slope_one[...].reshape(slots * count, width).astype(wide)
    inner = (slope * dot_back(mid, w_mid[...])).astype(low)
    own_sum[...] += jnp.sum(inner.astype(wide).reshape(slots, count, width), axis=0)
    edge_rows = edges[...].reshape(slots * count, narrow)
    g_edge[...] += dot_rows(edge_rows, inner)
    edge_grad[...] = partial[...] + dot_back(inner, w_in[2 * width :]).reshape(slots, count, narrow)
    spread_sum[...] += dot(pick_columns(rows[0], total), inner)

    @pl.when(step == pl.num_programs(0) - 1)
    def _():
        spread_low = spread_sum[...].astype(low)
        spread[...] = spread_low
        own_low = own_sum[...].astype(low)
        put("message_in", dot_rows(nodes[...], own_low))
        put("message_near", dot_rows(table[...], spread_low))
        put("message_edge", g_edge[...])
        put("message_mid", g_mid[...])
        put_line("v_mid", bias_mid[...])
        put_line("v_in", jnp.sum(own_sum[...], axis=0, keepdims=True))
        here = layout["lines"]
        tall = lines.shape[0]
        packed[here : here + tall, :] = lines[...].astype(low)
        rest = packed.shape[0] - here - tall
        if rest:
            packed[here + tall :, :] = jnp.zeros((rest, width), low)
        node_part[...] += dot_back(own_low, w_in[0:width])
        arrived(flat(lasts))
        all_sent(ups + flat(firsts) + flat(lasts))
        feed_table[...] = held_table[...]


def lay_out(width, narrow, hidden, shares):
    pieces = hidden // width
    sizes = [
        ("message_in", width), ("message_near", width), ("message_edge", narrow), ("message_mid", width),
        ("message_out", width), ("edge_own", narrow),
        ("edge_near", narrow), ("edge_a", narrow), ("edge_b", narrow), ("lines", 32),
    ]
    layout, row = {}, 0
    for name, size in sizes:
        layout[name] = row
        row += size
    layout["rows"] = -(-row // shares) * shares
    layout["e_vectors"] = 0
    layout["v_up"] = 8
    singles = ("v_final_gain", "v_final_shift", "v_down", "v_node_gain", "v_node_shift", "v_out", "v_mid", "v_in")
    for place, name in enumerate(singles):
        layout[name] = 8 + pieces + place
    return layout


def unpack(layout, packed, feed_up_low, feed_down_low, *outs):
    (m_in, m_in_b, m_mid, m_mid_b, m_out, m_out_b, n_gain, n_shift, f_up, f_up_b, f_down, f_down_b,
     l_gain, l_shift, e_in, e_in_b, e_mid, e_mid_b, e_out, e_out_b, e_gain, e_shift) = outs
    width = m_mid.shape[0]
    narrow = e_mid.shape[0]
    hidden = f_up.shape[1]
    half = width // 2

    def big(name, tall, lanes=slice(None)):
        return packed[layout[name] : layout[name] + tall, lanes].astype(wide)

    m_in[0:width] = big("message_in", width)
    m_in[width : 2 * width] = big("message_near", width)
    m_in[2 * width :] = big("message_edge", narrow)
    m_mid[...] = big("message_mid", width)
    m_out[...] = big("message_out", width)
    span = feed_down_low.shape[1]
    for piece in range(hidden // span):
        f_down[piece * span : (piece + 1) * span] = feed_down_low[piece].astype(wide)
        f_up[:, piece * span : (piece + 1) * span] = feed_up_low[piece].astype(wide)
    e_in[:, 0:width] = big("edge_own", narrow)
    e_in[:, width : 2 * width] = big("edge_near", narrow)
    e_in[:, 2 * width :] = big("edge_a", narrow, slice(0, narrow))
    e_mid[...] = big("edge_a", narrow, slice(half, half + narrow))
    e_out[...] = big("edge_b", narrow, slice(0, narrow))
    lines = packed[layout["lines"] : layout["lines"] + 32, :].astype(wide)

    def one(name):
        return lines[layout[name]]

    m_in_b[...] = one("v_in")
    m_mid_b[...] = one("v_mid")
    m_out_b[...] = one("v_out")
    n_gain[...] = one("v_node_gain")
    n_shift[...] = one("v_node_shift")
    l_gain[...] = one("v_final_gain")
    l_shift[...] = one("v_final_shift")
    f_down_b[...] = one("v_down")
    for piece in range(hidden // width):
        f_up_b[piece * width : (piece + 1) * width] = lines[layout["v_up"] + piece]
    for place, ref in enumerate((e_gain, e_shift, e_out_b, e_mid_b, e_in_b)):
        ref[...] = lines[place, 0:narrow]


def table_kernel(grid, own, table, *sems):
    spot = Spot(grid)
    copy = pltpu.make_async_copy(own, table.at[spot.z, spot.y, spot.x], sems[-1])
    copy.start()
    meet(spot.peers())
    copy.wait()
    drive(gather_run(gather_plan(spot, table, sems[:-1])))


def owner_kernel(grid, part, out, *scratch):
    spot = Spot(grid)
    meet(spot.peers())
    sums = []
    drive(scatter_run(spot, part, scratch, sums))
    out[0] = sums[0]
    out[1] = sums[1]


def total_run(spot, partner, given, out, scratch):
    pair, pair_send, pair_arrive, last_send, last_arrive = scratch[:5]
    parts, sems = scratch[5:23], scratch[23:]
    side_z = spot.grid[0]
    core = spot.core
    mine = out.at[core]
    pairs = {}
    for j in list(range(1, side_z)) + [0]:
        zj = (spot.z + j) % side_z
        pairs[j] = remote(given.at[1 - core, zj], pair.at[zj], pair_send.at[j], pair_arrive.at[j], partner)
        pairs[j].start()
    yield

    def before(zj, j):
        arrived([pairs[j]])
        mine[zj] = (given[core, zj].astype(wide) + pair[zj].astype(wide)).astype(low)

    sums = []
    yield from scatter_run(spot, mine, parts, sums, before)
    all_sent(pairs.values())
    for half in range(2):
        mine[spot.z, spot.y, spot.x, half] = sums[half].astype(low)
    finals = []

    def plane(j):
        zj = (spot.z - j) % side_z
        copy = remote(mine.at[zj], mine.at[zj], last_send.at[j], last_arrive.at[j], partner)
        copy.start()
        finals.append(copy)

    yield from gather_run(gather_plan(spot, mine, sems), plane)
    arrived(finals)
    all_sent(finals)


def total_scratch(grid, rows, width):
    dma = pltpu.SemaphoreType.DMA
    return (
        [pltpu.VMEM(grid + (2, rows, width), low)]
        + [dma((grid[0],))] * 4
        + scatter_scratch(grid, rows, width)
        + gather_sems(grid)
    )


def owner_run(spot, part, node_part, w_near, out, scratch):
    sums = []
    yield from scatter_run(spot, part, scratch, sums)
    for half in range(2):
        out[half] = node_part[half] + dot_back(sums[half].astype(low), w_near[...])


def feed_run(
    spot, partner, table, w_up, b_up, w_down, out_up, out_down,
    bias, send_up, send_down, near_up, near_down, sends, arrives, last_sends, last_arrives,
):
    span = w_up.shape[1] // out_up.shape[0]
    half = out_up.shape[0] // 2
    core = spot.core
    width = w_up.shape[0]
    rows = table.shape[0] * table.shape[1] * table.shape[2] * table.shape[4]
    bias[...] = as_row(b_up)

    def piece(place):
        normed = table[:, :, :, 0].reshape(rows, width)
        down = table[:, :, :, 1].reshape(rows, width)
        lanes = pl.ds(pl.multiple_of(place * span, span), span)
        act, slope = gelu_pair(dot(normed, w_up[:, lanes]) + bias[:, lanes])
        up = (slope * dot_back(down, w_down[lanes, :])).astype(low)
        return dot_rows(normed, up), dot_rows(act.astype(low), down)

    started = []
    for q in range(half):
        up, down = piece((1 - core) * half + q)
        send_up[q] = up.astype(low)
        send_down[q] = down.astype(low)
        pair = [
            remote(send_up.at[q], near_up.at[q], sends.at[0, q], arrives.at[0, q], partner),
            remote(send_down.at[q], near_down.at[q], sends.at[1, q], arrives.at[1, q], partner),
        ]
        start_all(pair)
        started.append(pair)
        yield
    finals = []
    for q in range(half):
        place = core * half + q
        up, down = piece(place)
        arrived(started[q])
        out_up[place] = (up + near_up[q].astype(wide)).astype(low)
        out_down[place] = (down + near_down[q].astype(wide)).astype(low)
        pair = [
            remote(out_up.at[place], out_up.at[place], last_sends.at[0, q], last_arrives.at[0, q], partner),
            remote(out_down.at[place], out_down.at[place], last_sends.at[1, q], last_arrives.at[1, q], partner),
        ]
        start_all(pair)
        finals += pair
        yield
    arrived(finals)
    all_sent(flat(started) + finals)


def feed_scratch(width, hidden, pieces):
    dma = pltpu.SemaphoreType.DMA
    span, half = hidden // pieces, pieces // 2
    return (
        [pltpu.VMEM((1, hidden), wide)]
        + [pltpu.VMEM((half, width, span), low), pltpu.VMEM((half, span, width), low)] * 2
        + [dma((2, half))] * 4
    )


def tail_kernel(
    grid, given, part, node_part, w_near, table, w_up, b_up, w_down, summed, out_nodes, out_up, out_down, *scratch
):
    spot = Spot(grid)
    partner = (1 - spot.core, lax.axis_index("res"))
    meet(spot.peers() + [partner])
    total = total_run(spot, partner, given, summed, scratch[:33])
    owner = owner_run(spot, part, node_part, w_near, out_nodes, scratch[33:51])
    feed = feed_run(spot, partner, table, w_up, b_up, w_down, out_up, out_down, *scratch[51:])
    runs = [owner, total, feed]
    while runs:
        for run in list(runs):
            if next(run, runs) is runs:
                runs.remove(run)


vmem = pl.BlockSpec(memory_space=pltpu.VMEM)
most_vmem = 63 << 20


def params(collective=None, **more):
    if collective is None:
        return pltpu.CompilerParams(vmem_limit_bytes=most_vmem, **more)
    return pltpu.CompilerParams(
        collective_id=collective, has_side_effects=True, vmem_limit_bytes=most_vmem, **more
    )


def gather_table(grid, rows, collective):
    count, width = rows.shape
    table = pl.pallas_call(
        functools.partial(table_kernel, grid),
        out_shape=jax.ShapeDtypeStruct(grid + (2, count // 2, width), low),
        in_specs=[vmem],
        out_specs=vmem,
        scratch_shapes=gather_sems(grid) + [pltpu.SemaphoreType.DMA],
        compiler_params=params(collective),
        name="gather_table_%d" % width,
    )(rows.reshape(2, count // 2, width))
    return table.reshape(-1, width)


def held(array):
    return pl.BlockSpec(array.shape, lambda step, dims=len(array.shape): (0,) * dims, pipeline_mode=pl.Buffered(1))


def streamed(array, slots):
    return pl.BlockSpec((slots,) + array.shape[1:], lambda step, dims=len(array.shape): (step,) + (0,) * (dims - 1))


def call(kernel, name, steps, slots, inputs, outputs, scratch, collective=None):
    def spec(item, flow):
        return streamed(item, slots if item.shape[0] != steps else 1) if flow else held(item)
    return pl.pallas_call(
        kernel,
        grid=(steps,),
        in_specs=[spec(item, flow) for item, flow in inputs],
        out_specs=[spec(item, flow) for item, flow in outputs],
        out_shape=[item for item, _ in outputs],
        scratch_shapes=scratch,
        compiler_params=params(collective),
        name=name,
    )(*[item for item, _ in inputs])


def per_device(
    node_states, edge_states, neighbours, residue_mask, neighbour_count,
    message_in, message_in_bias, message_mid, message_mid_bias, message_out, message_out_bias,
    node_gain, node_shift, feed_up, feed_up_bias, feed_down, feed_down_bias, final_gain, final_shift,
    edge_in, edge_in_bias, edge_mid, edge_mid_bias, edge_out, edge_out_bias, edge_gain, edge_shift,
    node_cotangent, edge_cotangent,
):
    grid = chip_grid(lax.axis_size("res"))
    nodes = node_states[0]
    count, width = nodes.shape
    edges = jnp.transpose(edge_states[0], (1, 0, 2))
    edge_ct = jnp.transpose(edge_cotangent[0], (1, 0, 2))
    depth, _, narrow = edges.shape
    hidden = feed_up.shape[1]
    slots = 12
    steps = depth // slots
    total = grid[0] * grid[1] * grid[2] * count
    index = neighbours[0]
    rows = jnp.transpose(index).reshape(steps, 1, slots * count)
    edge_in_t = jnp.transpose(edge_in)
    lanes = -(-narrow // 128) * 128
    shape = jax.ShapeDtypeStruct
    slab = shape((depth, count, width), low)
    node_low, node_wide = shape((count, width), low), shape((count, width), wide)
    scratch = pltpu.VMEM

    table = gather_table(grid, nodes, 0)
    (slope_one, slope_two, act_one, mixed_low, resid, second_sum, up_slope, node_out, sent, own_edge) = call(
        functools.partial(message_forward, slots), "message_forward", steps, slots,
        [(index, False), (neighbour_count, False), (residue_mask, False), (nodes, False), (table, False), (edges, True)]
        + [(a, False) for a in (
            message_in, message_in_bias, message_mid, message_mid_bias, message_out, message_out_bias,
            node_gain, node_shift, feed_up, feed_up_bias, feed_down, feed_down_bias, final_gain, final_shift,
            edge_in_t, edge_in_bias)],
        [(slab, True)] * 3 + [(node_low, False), (node_wide, False), (node_wide, False),
         (shape((count, hidden), wide), False), (node_low, False),
         (shape((count, lanes), low), False), (shape((count, narrow), wide), False)],
        [scratch((total, width), low), scratch((count, width), wide), scratch((count, width), wide)],
    )
    sent_table = gather_table(grid, sent, 1)
    square = shape((narrow, narrow), wide)
    (edge_result, partial, spread_two, own_edge_grad, e_in, e_mid, e_out, e_vectors) = call(
        functools.partial(edge_pass, slots), "edge_pass", steps, slots,
        [(index, False), (rows, True), (sent_table, False), (own_edge, False), (edges, True), (edge_ct, True)]
        + [(a, False) for a in (edge_in_t, edge_mid, edge_mid_bias, edge_out, edge_out_bias, edge_gain, edge_shift)],
        [(shape(edges.shape, low), True), (shape(edges.shape, wide), True), (shape((total, lanes), low), False),
         (shape((count, narrow), wide), False), (square, False), (square, False), (square, False),
         (shape((8, narrow), wide), False)],
        [scratch((total, narrow), wide)],
    )
    back_edge = pl.pallas_call(
        functools.partial(owner_kernel, grid),
        out_shape=shape((2, count // 2, lanes), wide),
        in_specs=[vmem], out_specs=vmem,
        scratch_shapes=scatter_scratch(grid, count // 2, lanes),
        compiler_params=params(2), name="edge_owner",
    )(spread_two.reshape(grid + (2, count // 2, lanes))).reshape(count, lanes)[:, :narrow]
    shares = 4 * grid[0] * grid[1] * grid[2] * 16
    layout = lay_out(width, narrow, hidden, shares)
    table_blocks = grid + (2, count, width)
    (edge_grad, spread, node_part, packed, feed_table) = call(
        functools.partial(node_backward, grid, slots, layout), "node_backward", steps, slots,
        [(rows, True), (neighbour_count, False), (residue_mask, False), (nodes, False), (table, False), (edges, True),
         (slope_one, True), (slope_two, True), (act_one, True), (partial, True)]
        + [(a, False) for a in (
            mixed_low, resid, second_sum, up_slope, node_out, node_cotangent[0], back_edge, own_edge_grad,
            e_in, e_mid, e_out, e_vectors, message_in, message_mid, message_out, node_gain, node_shift,
            feed_up, feed_down, final_gain, edge_in_t)],
        [(shape(edges.shape, wide), True), (shape((total, width), low), False), (node_wide, False),
         (shape((layout["rows"], width), low), False), (shape(table_blocks, low), False)],
        [scratch((count, width), wide), scratch((total, width), wide), scratch((count, width), wide),
         scratch((width, width), wide), scratch((narrow, width), wide), scratch((1, width), wide),
         scratch((32, width), wide), scratch(table_blocks, low)] + gather_sems(grid),
        collective=3,
    )
    chunk = layout["rows"] // (4 * grid[0] * grid[1] * grid[2])
    blocks = (2,) + grid + (2, chunk, width)
    pieces = hidden // 256
    (summed, grad_nodes, up_low, down_low) = pl.pallas_call(
        functools.partial(tail_kernel, grid),
        out_shape=[shape(blocks, low), shape((2, count // 2, width), wide),
                   shape((pieces, width, hidden // pieces), low), shape((pieces, hidden // pieces, width), low)],
        in_specs=[vmem] * 8, out_specs=[vmem] * 4,
        scratch_shapes=total_scratch(grid, chunk, width) + scatter_scratch(grid, count // 2, width)
        + feed_scratch(width, hidden, pieces),
        compiler_params=params(4), name="tail",
    )(packed.reshape(blocks), spread.reshape(grid + (2, count // 2, width)), node_part.reshape(2, count // 2, width),
      message_in[width : 2 * width], feed_table, feed_up, feed_up_bias, feed_down)
    grad_nodes = grad_nodes.reshape(count, width)
    vector, line = shape((width,), wide), shape((narrow,), wide)
    grads = pl.pallas_call(
        functools.partial(unpack, layout),
        out_shape=[
            shape(message_in.shape, wide), vector, shape(message_mid.shape, wide), vector,
            shape(message_out.shape, wide), vector, vector, vector, shape(feed_up.shape, wide), shape((hidden,), wide),
            shape(feed_down.shape, wide), vector, vector, vector, shape(edge_in_t.shape, wide), line,
            square, line, square, line, line, line,
        ],
        in_specs=[vmem] * 3, out_specs=[vmem] * 22,
        compiler_params=params(), name="unpack",
    )(summed.reshape(layout["rows"], width), up_low, down_low)
    grads = list(grads)
    grads[14] = jnp.transpose(grads[14])
    back = (1, 0, 2)
    return (
        node_out[None],
        jnp.transpose(edge_result, back)[None],
        grad_nodes[None],
        jnp.transpose(edge_grad, back)[None],
        *grads,
    )


def solution(mesh):
    split, whole = P("batch", "res"), P()
    in_specs = (split,) * 5 + (whole,) * 22 + (split,) * 2
    out_specs = (split,) * 4 + (whole,) * 22
    return jax.shard_map(per_device, mesh=mesh, in_specs=in_specs, out_specs=out_specs, check_vma=False)
```

```python
import functools
import math
import jax
import jax.numpy as jnp
from jax import lax
from jax.experimental import pallas as pl
from jax.experimental.pallas import tpu as pltpu
from jax.sharding import PartitionSpec as P

MESH = pl.DeviceIdType.MESH
low = jnp.bfloat16
GAP, GAP_NORMED, GAP_DOWN, GAP_EARLY = 3.5, 3.0, 4.0, 3.5
wide = jnp.float32


def chip_grid(count):
    side_x = 2 if count < 64 else 4
    side_y = side_x
    return (count // (side_x * side_y), side_y, side_x)


def flip(place, step):
    bit = 1
    while bit <= step:
        if step & bit:
            place = place + bit - 2 * bit * ((place // bit) % 2)
        bit *= 2
    return place


class Spot:
    def __init__(self, grid):
        self.grid = grid
        side_z, side_y, side_x = grid
        me = lax.axis_index("res")
        self.core = lax.axis_index("batch")
        self.z = me // (side_y * side_x)
        self.y = (me // side_x) % side_y
        self.x = me % side_x

    def device(self, z, y, x):
        return (self.core, (z * self.grid[1] + y) * self.grid[2] + x)

    def far_z(self, step):
        return flip(self.z, step)

    def far_y(self, step):
        return flip(self.y, step)

    def far_x(self, step):
        return flip(self.x, step)

    def peers(self):
        found = [self.device(self.far_z(s), self.y, self.x) for s in range(1, self.grid[0])]
        found += [self.device(self.z, self.far_y(s), self.x) for s in range(1, self.grid[1])]
        found += [self.device(self.z, self.y, self.far_x(s)) for s in range(1, self.grid[2])]
        return found


def greet(peers):
    barrier = pltpu.get_barrier_semaphore()
    for peer in peers:
        pl.semaphore_signal(barrier, inc=1, device_id=peer, device_id_type=MESH)


def met(peers):
    pl.semaphore_wait(pltpu.get_barrier_semaphore(), len(peers))


def meet(peers):
    greet(peers)
    met(peers)


def remote(source, target, send, arrive, device):
    return pltpu.make_async_remote_copy(
        src_ref=source, dst_ref=target, send_sem=send, recv_sem=arrive,
        device_id=device, device_id_type=MESH,
    )


def gather_sems(grid):
    side_z, side_y, side_x = grid
    dma = pltpu.SemaphoreType.DMA
    shapes = [(side_z - 1,), (side_z, side_x - 1), (side_z, side_y - 1), (side_z, side_y - 1), (side_z, side_x - 1)]
    return [dma(s) for s in shapes for _ in range(2)]


def gather_plan(spot, table, sems):
    (s1, r1, s2a, r2a, s2b, r2b, s3a, r3a, s3b, r3b) = sems
    side_z, side_y, side_x = spot.grid
    z, y, x = spot.z, spot.y, spot.x

    def push(view, send, arrive, device):
        return remote(view, view, send, arrive, device)

    ups = [
        push(table.at[z, y, x], s1.at[s - 1], r1.at[s - 1], spot.device(spot.far_z(s), y, x))
        for s in range(1, side_z)
    ]
    firsts, lasts = [], []
    for j in range(side_z):
        zj = flip(z, j)
        firsts.append(
            [
                push(table.at[zj, y, x, 0], s2a.at[j, s - 1], r2a.at[j, s - 1], spot.device(z, y, spot.far_x(s)))
                for s in range(1, side_x)
            ]
            + [
                push(table.at[zj, y, x, 1], s2b.at[j, s - 1], r2b.at[j, s - 1], spot.device(z, spot.far_y(s), x))
                for s in range(1, side_y)
            ]
        )
        lasts.append(
            [
                push(table.at[zj, y, :, 0], s3a.at[j, s - 1], r3a.at[j, s - 1], spot.device(z, spot.far_y(s), x))
                for s in range(1, side_y)
            ]
            + [
                push(table.at[zj, :, x, 1], s3b.at[j, s - 1], r3b.at[j, s - 1], spot.device(z, y, spot.far_x(s)))
                for s in range(1, side_x)
            ]
        )
    return ups, firsts, lasts


def start_all(copies):
    for copy in copies:
        copy.start()


def arrived(copies):
    for copy in copies:
        copy.wait_recv()


def all_sent(copies):
    for copy in copies:
        copy.wait_send()


def flat(groups):
    return [copy for group in groups for copy in group]


def gather_run(plan, on_plane=None):
    ups, firsts, lasts = plan
    count = len(lasts)
    start_all(ups + firsts[0])
    yield
    for j in range(1, count):
        arrived([ups[j - 1]])
        start_all(firsts[j])
        arrived(firsts[j - 1])
        start_all(lasts[j - 1])
        if j + 1 < count:
            yield
    arrived(firsts[count - 1])
    start_all(lasts[count - 1])
    yield
    for j in range(count):
        arrived(lasts[j])
        if on_plane is not None:
            on_plane(j)
    yield
    all_sent(ups + flat(firsts) + flat(lasts))


def drive(run):
    for _ in run:
        pass


def scatter_scratch(grid, rows, width):
    side_z, side_y, side_x = grid
    dma = pltpu.SemaphoreType.DMA
    shapes = [(side_z, side_y - 1), (side_z, side_x - 1), (side_z, side_x - 1), (side_z, side_y - 1), (side_z - 1,)]
    buffers = [
        pltpu.VMEM((side_z, side_y - 1, side_x, rows, width), low),
        pltpu.VMEM((side_z, side_x - 1, side_y, rows, width), low),
        pltpu.VMEM((side_z, side_x, rows, width), low),
        pltpu.VMEM((side_z, side_y, rows, width), low),
        pltpu.VMEM((side_z, side_x - 1, rows, width), low),
        pltpu.VMEM((side_z, side_y - 1, rows, width), low),
        pltpu.VMEM((side_z, 2, rows, width), low),
        pltpu.VMEM((side_z - 1, 2, rows, width), low),
    ]
    return buffers + [dma(s) for s in shapes for _ in range(2)]


def scatter_run(spot, part, scratch, result, before_plane=None):
    (ra1, rb1, ka, kb, ra2, rb2, tot, r3, s1a, q1a, s1b, q1b, s2a, q2a, s2b, q2b, s3, q3) = scratch
    side_z, side_y, side_x = spot.grid
    z, y, x = spot.z, spot.y, spot.x
    sent = []

    def go(copy):
        copy.start()
        sent.append(copy)
        return copy

    order = list(range(side_z - 1, -1, -1))
    one, two, three = {}, {}, []
    for j in order:
        zj = flip(z, j)
        if before_plane is not None:
            before_plane(zj, j)
        a = [
            go(remote(part.at[zj, spot.far_y(s), :, 0], ra1.at[j, s - 1], s1a.at[j, s - 1], q1a.at[j, s - 1],
                      spot.device(z, spot.far_y(s), x)))
            for s in range(1, side_y)
        ]
        b = [
            go(remote(part.at[zj, :, spot.far_x(s), 1], rb1.at[j, s - 1], s1b.at[j, s - 1], q1b.at[j, s - 1],
                      spot.device(z, y, spot.far_x(s))))
            for s in range(1, side_x)
        ]
        one[j] = (a, b)
    yield
    for j in order:
        zj = flip(z, j)
        arrived(one[j][0])
        total = part[zj, y, :, 0].astype(wide)
        for s in range(side_y - 1):
            total = total + ra1[j, s].astype(wide)
        ka[j] = total.astype(low)
        a = [
            go(remote(ka.at[j, spot.far_x(s)], ra2.at[j, s - 1], s2a.at[j, s - 1], q2a.at[j, s - 1],
                      spot.device(z, y, spot.far_x(s))))
            for s in range(1, side_x)
        ]
        arrived(one[j][1])
        total = part[zj, :, x, 1].astype(wide)
        for s in range(side_x - 1):
            total = total + rb1[j, s].astype(wide)
        kb[j] = total.astype(low)
        b = [
            go(remote(kb.at[j, spot.far_y(s)], rb2.at[j, s - 1], s2b.at[j, s - 1], q2b.at[j, s - 1],
                      spot.device(z, spot.far_y(s), x)))
            for s in range(1, side_y)
        ]
        two[j] = a + b
    yield
    for j in order:
        zj = flip(z, j)
        arrived(two[j])
        upper = ka[j, x].astype(wide)
        for s in range(side_x - 1):
            upper = upper + ra2[j, s].astype(wide)
        lower = kb[j, y].astype(wide)
        for s in range(side_y - 1):
            lower = lower + rb2[j, s].astype(wide)
        if j:
            tot[j, 0] = upper.astype(low)
            tot[j, 1] = lower.astype(low)
            three.append(
                go(remote(tot.at[j], r3.at[j - 1], s3.at[j - 1], q3.at[j - 1], spot.device(zj, y, x)))
            )
    yield
    arrived(three)
    for s in range(side_z - 1):
        upper = upper + r3[s, 0].astype(wide)
        lower = lower + r3[s, 1].astype(wide)
    result += [upper, lower]
    all_sent(sent)
eps_norm = 1e-05
root_half = 0.7071067811865476
root_turn = 0.3989422804014327


def dot(left, right):
    return jnp.dot(left, right, preferred_element_type=wide)


def dot_back(left, right):
    return lax.dot_general(left, right, (((1,), (1,)), ((), ())), preferred_element_type=wide)


def dot_rows(left, right):
    return lax.dot_general(left, right, (((0,), (0,)), ((), ())), preferred_element_type=wide)


def gelu_pair(values):
    share = 0.5 + 0.5 * lax.erf(values * root_half)
    slope = share + values * (jnp.exp(values * values * -0.5) * root_turn)
    return values * share, slope


def norm_stats(values):
    centre = jnp.mean(values, axis=-1, keepdims=True)
    centred = values - centre
    variance = jnp.mean(centred * centred, axis=-1, keepdims=True)
    scale = lax.rsqrt(variance + eps_norm)
    return centred * scale, scale


def norm_back(hat, scale, gain, grad):
    inner = grad * gain
    return scale * (
        inner
        - jnp.mean(inner, axis=-1, keepdims=True)
        - hat * jnp.mean(inner * hat, axis=-1, keepdims=True)
    )


def as_row(ref, start=None, size=None):
    return ref[...].astype(wide).reshape(1, ref.shape[0])


def as_column(row, count):
    rows = lax.broadcasted_iota(jnp.int32, (count, count), 0)
    lanes = lax.broadcasted_iota(jnp.int32, (count, count), 1)
    return jnp.sum(jnp.where(rows == lanes, jnp.broadcast_to(row, (count, count)), 0), axis=1, keepdims=True)


def slot_column(index, slot):
    lanes = lax.broadcasted_iota(jnp.int32, index.shape, 1)
    return jnp.sum(jnp.where(lanes == slot, index, 0), axis=1, keepdims=True)


def pick_rows(index, first, slots, total):
    count = index.shape[0]
    lanes = lax.broadcasted_iota(jnp.int32, (count, total), 1)
    return jnp.concatenate(
        [jnp.where(slot_column(index, first + s) == lanes, 1.0, 0.0).astype(low) for s in range(slots)], axis=0
    )


def pick_columns(row, total):
    rows = lax.broadcasted_iota(jnp.int32, (total, row.shape[1]), 0)
    return jnp.where(rows == row, 1.0, 0.0).astype(low)


def message_forward(
    slots, index, counts, masks, nodes, table, edges, w_in, b_in, w_mid, b_mid, w_out, b_out,
    gain_one, shift_one, w_up, b_up, w_down, b_down, gain_two, shift_two, w_edge, b_edge,
    slope_one, slope_two, act_one, mixed_low, resid, second_sum, up_slope, node_out, sent, own_edge,
    projected, own, pooled,
):
    step = pl.program_id(0)
    count, width = nodes.shape
    total = table.shape[0]
    live = as_column(counts[...], count)

    @pl.when(step == 0)
    def _():
        projected[...] = dot(table[...], w_in[width : 2 * width]).astype(low)
        own[...] = dot(nodes[...], w_in[0:width]) + as_row(b_in)
        pooled[...] = jnp.zeros_like(pooled)

    picks = pick_rows(index[...], step * slots, slots, total)
    edge_rows = edges[...].reshape(slots * count, edges.shape[2])
    pre = dot(picks, projected[...]) + dot(edge_rows, w_in[2 * width :])
    pre = pre.reshape(slots, count, width) + own[...][None]
    act, slope = gelu_pair(pre)
    act = act.astype(low)
    act_one[...] = act
    slope_one[...] = slope.astype(low)
    pre = dot(act.reshape(slots * count, width), w_mid[...]) + as_row(b_mid)
    act, slope = gelu_pair(pre)
    act = act.reshape(slots, count, width)
    slope_two[...] = slope.astype(low).reshape(slots, count, width)
    gathered = pooled[...]
    for s in range(slots):
        gathered = gathered + jnp.where(live > step * slots + s, act[s], 0.0)
    pooled[...] = gathered

    @pl.when(step == pl.num_programs(0) - 1)
    def _():
        mean = pooled[...] / jnp.maximum(live, 1).astype(wide)
        mean_low = mean.astype(low)
        mixed_low[...] = mean_low
        some = jnp.where(live > 0, 1.0, 0.0)
        mask = as_column(masks[...], count).astype(wide)
        aggregate = dot(mean_low, w_out[...]) + some * as_row(b_out)
        total_sum = nodes[...].astype(wide) + mask * aggregate
        resid[...] = total_sum
        hat, _ = norm_stats(total_sum)
        first = hat * as_row(gain_one) + as_row(shift_one)
        up = dot(first.astype(low), w_up[...]) + as_row(b_up)
        act_up, slope_up = gelu_pair(up)
        act_up = act_up.astype(low)
        up_slope[...] = slope_up
        summed = first + dot(act_up, w_down[...]) + as_row(b_down)
        second_sum[...] = summed
        hat, _ = norm_stats(summed)
        out = (hat * as_row(gain_two) + as_row(shift_two)).astype(low)
        node_out[...] = out
        pad = jnp.zeros((count, sent.shape[1] - w_edge.shape[0]), low)
        sent[...] = jnp.concatenate([dot_back(out, w_edge[:, width : 2 * width]).astype(low), pad], axis=1)
        own_edge[...] = dot_back(out, w_edge[:, 0:width]) + as_row(b_edge)


def edge_pass(
    slots, index, rows, table, own_edge, edges, cotangent, w_edge, w_mid, b_mid, w_out, b_out, gain, shift,
    result, partial, spread, own_grad, g_in, g_mid, g_out, vectors, spread_sum,
):
    step = pl.program_id(0)
    count, width = own_edge.shape
    total = table.shape[0]
    base = w_edge.shape[1] - width

    @pl.when(step == 0)
    def _():
        spread_sum[...] = jnp.zeros_like(spread_sum)
        for ref in (own_grad, g_in, g_mid, g_out, vectors):
            ref[...] = jnp.zeros_like(ref)

    w_here = w_edge[:, base:]
    picks = pick_rows(index[...], step * slots, slots, total)
    edge_rows = edges[...].reshape(slots * count, width)
    pre = dot(picks, table[...])[:, 0:width] + dot_back(edge_rows, w_here)
    pre = (pre.reshape(slots, count, width) + own_edge[...][None]).reshape(slots * count, width)
    act_one, slope_one = gelu_pair(pre)
    act_one = act_one.astype(low)
    pre = dot(act_one, w_mid[...]) + as_row(b_mid)
    act_two, slope_two = gelu_pair(pre)
    act_two = act_two.astype(low)
    pre = dot(act_two, w_out[...]) + as_row(b_out)
    hat, scale = norm_stats(edge_rows.astype(wide) + pre)
    gain_row = as_row(gain)
    result[...] = (hat * gain_row + as_row(shift)).astype(low).reshape(slots, count, width)
    grad = cotangent[...].reshape(slots * count, width).astype(wide)
    sum_grad = norm_back(hat, scale, gain_row, grad)
    three = sum_grad.astype(low)
    g_out[...] += dot_rows(act_two, three)
    two = (slope_two * dot_back(three, w_out[...])).astype(low)
    g_mid[...] += dot_rows(act_one, two)
    one = (slope_one * dot_back(two, w_mid[...])).astype(low)
    g_in[...] += dot_rows(one, edge_rows)
    vectors[...] += jnp.concatenate(
        [
            jnp.sum(piece, axis=0, keepdims=True)
            for piece in (grad * hat, grad, three.astype(wide), two.astype(wide), one.astype(wide))
        ]
        + [jnp.zeros((3, width), wide)],
        axis=0,
    )
    own_grad[...] += jnp.sum(one.astype(wide).reshape(slots, count, width), axis=0)
    partial[...] = (sum_grad + dot(one, w_here)).astype(low).reshape(slots, count, width)
    spread_sum[...] += dot(pick_columns(rows[0], total), one)

    @pl.when(step == pl.num_programs(0) - 1)
    def _():
        pad = jnp.zeros((total, spread.shape[1] - width), low)
        spread[...] = jnp.concatenate([spread_sum[...].astype(low), pad], axis=1)


def node_backward(
    grid, slots, layout, rows, counts, masks, nodes, table, edges, slope_one, slope_two, act_one, partial,
    mixed_low, resid, second_sum, up_slope, node_out, cotangent, back_edge, own_edge_grad,
    e_in, e_mid, e_out, e_vectors,
    w_in, w_mid, w_out, gain_one, shift_one, w_up, w_down, gain_two, w_edge,
    edge_grad, spread, node_part, packed, feed_table,
    level, spread_sum, own_sum, g_mid, g_edge, bias_mid, lines, held_table, *sems,
):
    step = pl.program_id(0)
    last = pl.num_programs(0) - 1
    spot = Spot(grid)
    peers = spot.peers()
    ups, firsts, lasts = gather_plan(spot, held_table, sems)
    count, width = nodes.shape
    total = table.shape[0]
    narrow = w_edge.shape[0]
    hidden = w_up.shape[1]
    live = as_column(counts[...], count)

    def put(name, value):
        row = layout[name]
        packed[row : row + value.shape[0], :] = value.astype(low)

    def put_line(name, value):
        row = layout[name]
        lines[row : row + value.shape[0], 0 : value.shape[1]] = value

    @pl.when(step == 0)
    def _():
        greet(peers)
        for ref in (spread_sum, own_sum, g_mid, g_edge, bias_mid, lines):
            ref[...] = jnp.zeros_like(ref)
        out = node_out[...]
        own_low = own_edge_grad[...].astype(low)
        back_low = back_edge[...].astype(low)
        put("edge_own", dot_rows(own_low, out))
        put("edge_near", dot_rows(back_low, out))
        pad = jnp.zeros((narrow, width // 2 - narrow), wide)
        put("edge_a", jnp.concatenate([e_in[...], pad, e_mid[...], pad], axis=1))
        put("edge_b", jnp.concatenate([e_out[...], pad, jnp.zeros((narrow, width // 2), wide)], axis=1))
        put_line("e_vectors", e_vectors[...])
        grad = (
            cotangent[...].astype(wide)
            + dot(own_low, w_edge[:, 0:width])
            + dot(back_low, w_edge[:, width : 2 * width])
        )
        hat, scale = norm_stats(second_sum[...])
        put_line("v_final_gain", jnp.sum(grad * hat, axis=0, keepdims=True))
        put_line("v_final_shift", jnp.sum(grad, axis=0, keepdims=True))
        second = norm_back(hat, scale, as_row(gain_two), grad)
        down = second.astype(low)
        put_line("v_down", jnp.sum(down.astype(wide), axis=0, keepdims=True))
        held_table[spot.z, spot.y, spot.x, 1] = down
        up = (up_slope[...] * dot_back(down, w_down[...])).astype(low)
        bias_up = jnp.sum(up.astype(wide), axis=0, keepdims=True)
        hat, scale = norm_stats(resid[...])
        normed = (hat * as_row(gain_one) + as_row(shift_one)).astype(low)
        held_table[spot.z, spot.y, spot.x, 0] = normed
        met(peers)
        start_all(ups + firsts[0])
        for piece in range(hidden // width):
            lines[layout["v_up"] + piece : layout["v_up"] + piece + 1, :] = bias_up[:, piece * width : (piece + 1) * width]
        first = second + dot_back(up, w_up[...])
        put_line("v_node_gain", jnp.sum(first * hat, axis=0, keepdims=True))
        put_line("v_node_shift", jnp.sum(first, axis=0, keepdims=True))
        mixed = norm_back(hat, scale, as_row(gain_one), first)
        node_part[...] = mixed
        masked = as_column(masks[...], count).astype(wide) * mixed
        put_line("v_out", jnp.sum(jnp.where(live > 0, masked, 0.0), axis=0, keepdims=True))
        put("message_out", dot_rows(mixed_low[...], masked.astype(low)))
        shared = (masked / jnp.maximum(live, 1).astype(wide)).astype(low)
        level[...] = dot_back(shared, w_out[...])

    @pl.when(step == 1)
    def _():
        for j in range(1, len(firsts)):
            arrived([ups[j - 1]])
            start_all(firsts[j])

    @pl.when(step == 2)
    def _():
        for j in range(len(lasts)):
            arrived(firsts[j])
            start_all(lasts[j])

    lift = level[...]
    slope = slope_two[...].astype(wide)
    mid = jnp.concatenate(
        [jnp.where(live > step * slots + s, slope[s] * lift, 0.0).astype(low) for s in range(slots)], axis=0
    )
    flat_one = act_one[...].reshape(slots * count, width)
    g_mid[...] += dot_rows(flat_one, mid)
    bias_mid[...] += jnp.sum(mid.astype(wide), axis=0, keepdims=True)
    slope = slope_one[...].reshape(slots * count, width).astype(wide)
    inner = (slope * dot_back(mid, w_mid[...])).astype(low)
    own_sum[...] += jnp.sum(inner.astype(wide).reshape(slots, count, width), axis=0)
    edge_rows = edges[...].reshape(slots * count, narrow)
    g_edge[...] += dot_rows(edge_rows, inner)
    edge_grad[...] = partial[...].astype(wide) + dot_back(inner, w_in[2 * width :]).reshape(slots, count, narrow)
    spread_sum[...] += dot(pick_columns(rows[0], total), inner)

    @pl.when(step == pl.num_programs(0) - 1)
    def _():
        spread_low = spread_sum[...].astype(low)
        spread[...] = spread_low
        own_low = own_sum[...].astype(low)
        put("message_in", dot_rows(nodes[...], own_low))
        put("message_near", dot_rows(table[...], spread_low))
        put("message_edge", g_edge[...])
        put("message_mid", g_mid[...])
        put_line("v_mid", bias_mid[...])
        put_line("v_in", jnp.sum(own_sum[...], axis=0, keepdims=True))
        here = layout["lines"]
        tall = lines.shape[0]
        packed[here : here + tall, :] = lines[...].astype(low)
        rest = packed.shape[0] - here - tall
        if rest:
            packed[here + tall :, :] = jnp.zeros((rest, width), low)
        node_part[...] += dot_back(own_low, w_in[0:width])
        arrived(flat(lasts))
        all_sent(ups + flat(firsts) + flat(lasts))
        feed_table[...] = held_table[...]


def lay_out_rows(width, narrow, hidden, shares):
    pieces = hidden // width
    sizes = [
        ("message_in", width), ("message_near", width), ("message_edge", narrow), ("message_mid", width),
        ("message_out", width), ("edge_own", narrow),
        ("edge_near", narrow), ("edge_a", narrow), ("edge_b", narrow), ("lines", 32),
    ]
    layout, row = {}, 0
    for name, size in sizes:
        layout[name] = row
        row += size
    layout["rows"] = -(-row // shares) * shares
    layout["e_vectors"] = 0
    layout["v_up"] = 8
    singles = ("v_final_gain", "v_final_shift", "v_down", "v_node_gain", "v_node_shift", "v_out", "v_mid", "v_in")
    for place, name in enumerate(singles):
        layout[name] = 8 + pieces + place
    return layout


def unpack_rows(layout, packed, feed_up_low, feed_down_low, *outs):
    (m_in, m_in_b, m_mid, m_mid_b, m_out, m_out_b, n_gain, n_shift, f_up, f_up_b, f_down, f_down_b,
     l_gain, l_shift, e_in, e_in_b, e_mid, e_mid_b, e_out, e_out_b, e_gain, e_shift) = outs
    width = m_mid.shape[0]
    narrow = e_mid.shape[0]
    hidden = f_up.shape[1]
    half = width // 2

    def big(name, tall, lanes=slice(None)):
        return packed[layout[name] : layout[name] + tall, lanes].astype(wide)

    m_in[0:width] = big("message_in", width)
    m_in[width : 2 * width] = big("message_near", width)
    m_in[2 * width :] = big("message_edge", narrow)
    m_mid[...] = big("message_mid", width)
    m_out[...] = big("message_out", width)
    span = feed_down_low.shape[1]
    for piece in range(hidden // span):
        f_down[piece * span : (piece + 1) * span] = feed_down_low[piece].astype(wide)
        f_up[:, piece * span : (piece + 1) * span] = feed_up_low[piece].astype(wide)
    e_in[:, 0:width] = big("edge_own", narrow)
    e_in[:, width : 2 * width] = big("edge_near", narrow)
    e_in[:, 2 * width :] = big("edge_a", narrow, slice(0, narrow))
    e_mid[...] = big("edge_a", narrow, slice(half, half + narrow))
    e_out[...] = big("edge_b", narrow, slice(0, narrow))
    lines = packed[layout["lines"] : layout["lines"] + 32, :].astype(wide)

    def one(name):
        return lines[layout[name]]

    m_in_b[...] = one("v_in")
    m_mid_b[...] = one("v_mid")
    m_out_b[...] = one("v_out")
    n_gain[...] = one("v_node_gain")
    n_shift[...] = one("v_node_shift")
    l_gain[...] = one("v_final_gain")
    l_shift[...] = one("v_final_shift")
    f_down_b[...] = one("v_down")
    for piece in range(hidden // width):
        f_up_b[piece * width : (piece + 1) * width] = lines[layout["v_up"] + piece]
    for place, ref in enumerate((e_gain, e_shift, e_out_b, e_mid_b, e_in_b)):
        ref[...] = lines[place, 0:narrow]


def sum_pieces(width, narrow, cap):
    half = width // 2
    pieces = []
    row = 0
    for name, tall, lane in (
        ("edge_own", narrow, 0), ("edge_own", narrow, half), ("e_in", narrow, 0), ("e_mid", narrow, 0),
        ("e_out", narrow, 0), ("e_lines", 16, 0),
    ):
        pieces.append((name, 0, tall, lane, 0, row))
        row += tall
    place = 0
    late = []
    for name, tall in (
        ("edge_near", narrow), ("message_out", width), ("message_mid", width), ("message_own", width),
        ("message_near", width), ("message_edge", narrow), ("lines", 16),
    ):
        done = 0
        while done < tall and place < 2 * cap:
            size = min(tall - done, cap - place % cap)
            pieces.append((name, done, size, 0, 1 + place // cap, place % cap))
            place += size
            done += size
        if done < tall:
            late.append((name, done, tall - done))
    row = 0
    for name, first, tall in late:
        for lane in (0, half):
            pieces.append((name, first, tall, lane, 3, row))
            row += tall
    return pieces


def line_places(width, hidden):
    pieces = hidden // width
    singles = ("v_final_gain", "v_final_shift", "v_down", "v_node_gain", "v_node_shift", "v_out", "v_mid", "v_in")
    places = {name: pieces + place for place, name in enumerate(singles)}
    places["v_up"] = 0
    return places


class Sums:
    def __init__(self, pieces, groups):
        self.pieces, self.groups = pieces, groups

    def put(self, name, value):
        value = value.astype(low)
        for piece, first, tall, lane, group, row in self.pieces:
            if piece != name:
                continue
            ref = self.groups[group]
            part = value[first : first + tall, lane : lane + ref.shape[-1]]
            if part.shape[1] < ref.shape[-1]:
                part = jnp.concatenate([part, jnp.zeros((tall, ref.shape[-1] - part.shape[1]), low)], axis=1)
            for start in range(0, tall, 16):
                place, rest = [], (row + start) // 16
                for size in reversed(ref.shape[:-2]):
                    place.append(rest % size)
                    rest //= size
                ref[tuple(reversed(place))] = part[start : start + 16]


def whole_kernel(
    grid, slots, pieces, places,
    index, rows, counts, masks, nodes, b_in, b_mid, b_out, gain_one, shift_one, b_up, b_down, gain_two, shift_two,
    eb_in, ew_mid, eb_mid, ew_out, eb_out, gain_three, shift_three, cotangent,
    edges_far, edge_ct_far, w_in_far, w_mid_far, w_out_far, w_up_far, w_down_far, w_edge_far,
    node_out, edge_result, edge_total, grad_nodes, total_one, total_two, total_three, total_four, out_up, out_down,
    edges, edge_ct, w_in, w_mid, w_out, w_up, w_down, w_edge, fetches, puts,
    slope_one, slope_two, act_one, partial, table, own, pooled, up_slope, sent_table, own_edge,
    spread_edge, spread_two, own_edge_grad, e_in, e_mid, e_out, e_vectors,
    spread_sum, spread, own_sum, mid_sum, g_mid, g_edge, lines, node_part, normed_table, down_table,
    given_one, given_two, given_three, given_four,
    *scratch,
):
    scratch = list(scratch)

    def take(size):
        taken = scratch[:size]
        del scratch[:size]
        return taken

    spot = Spot(grid)
    partner = (1 - spot.core, lax.axis_index("res"))
    peers = spot.peers() + [partner]
    greet(peers)
    _, half_count, width = nodes.shape
    count = 2 * half_count
    total = spread_sum.shape[0]
    narrow = w_edge.shape[0]
    hidden = w_up.shape[1]
    steps = rows.shape[0]
    local = pltpu.make_async_copy(nodes, table.at[spot.z, spot.y, spot.x], puts.at[steps + 1])
    local.start()
    pairs = (
        (w_in_far, w_in), (edges_far, edges), (w_mid_far, w_mid), (w_out_far, w_out), (w_up_far, w_up),
        (w_down_far, w_down), (w_edge_far, w_edge), (edge_ct_far, edge_ct),
    )
    coming = [pltpu.make_async_copy(there, near, fetches.at[place]) for place, (there, near) in enumerate(pairs)]
    start_all(coming)
    node_sems, sent_sems, normed_sems, down_sems = take(10), take(10), take(10), take(10)
    edge_scratch, node_scratch, feed_parts = take(18), take(18), take(9)
    totals = [take(33) for _ in range(4)]
    sums = Sums(pieces, (given_one, given_two, given_three, given_four))
    live = as_column(counts[...], count)
    mask = as_column(masks[...], count).astype(wide)
    node_rows = nodes[...].reshape(count, width)
    local.wait()
    met(peers)
    node_gather = gather_run(gather_plan(spot, table, node_sems))
    next(node_gather)
    coming[0].wait()
    own[...] = dot(node_rows, w_in[0:width]) + as_row(b_in)
    pooled[...] = jnp.zeros_like(pooled)
    drive(node_gather)
    spread[...] = dot(table[...].reshape(total, width), w_in[width : 2 * width]).astype(low).reshape(spread.shape)
    for copy in coming[1:3]:
        copy.wait()

    @pl.loop(0, steps)
    def _(step):
        here = pl.ds(step * slots, slots)
        picks = pick_rows(index[...], step * slots, slots, total)
        edge_rows = edges[here].reshape(slots * count, narrow)
        pre = dot(picks, spread[...].reshape(total, width)) + dot(edge_rows, w_in[2 * width :])
        pre = pre.reshape(slots, count, width) + own[...][None]
        act, slope = gelu_pair(pre)
        act = act.astype(low)
        act_one[here] = act
        slope_one[here] = slope.astype(low)
        pre = dot(act.reshape(slots * count, width), w_mid[...]) + as_row(b_mid)
        act, slope = gelu_pair(pre)
        act = act.reshape(slots, count, width)
        slope_two[here] = slope.astype(low).reshape(slots, count, width)
        gathered = pooled[...]
        for s in range(slots):
            gathered = gathered + jnp.where(live > step * slots + s, act[s], 0.0)
        pooled[...] = gathered

    mixed_low = (pooled[...] / jnp.maximum(live, 1).astype(wide)).astype(low)
    some = jnp.where(live > 0, 1.0, 0.0)
    for copy in coming[3:]:
        copy.wait()
    aggregate = dot(mixed_low, w_out[...]) + some * as_row(b_out)
    hat_one, scale_one = norm_stats(node_rows.astype(wide) + mask * aggregate)
    first = hat_one * as_row(gain_one) + as_row(shift_one)
    first_low = first.astype(low)
    normed_table[spot.z, spot.y, spot.x] = first_low.reshape(normed_table.shape[3:])
    act_up, slope_up = gelu_pair(dot(first_low, w_up[...]) + as_row(b_up))
    up_slope[...] = slope_up
    second_sum = first + dot(act_up.astype(low), w_down[...]) + as_row(b_down)
    hat, _ = norm_stats(second_sum)
    out = (hat * as_row(gain_two) + as_row(shift_two)).astype(low)
    node_out[...] = out
    pad = jnp.zeros((count, sent_table.shape[-1] - narrow), low)
    sent = jnp.concatenate([dot_back(out, w_edge[:, width : 2 * width]).astype(low), pad], axis=1)
    sent_table[spot.z, spot.y, spot.x] = sent.reshape(sent_table.shape[3:])
    sent_gather = gather_run(gather_plan(spot, sent_table, sent_sems))
    next(sent_gather)
    normed_gather = gather_run(gather_plan(spot, normed_table, normed_sems))
    own_edge[...] = dot_back(out, w_edge[:, 0:width]) + as_row(eb_in)
    spread_edge[...] = jnp.zeros_like(spread_edge)
    for ref in (own_edge_grad, e_in, e_mid, e_out, e_vectors):
        ref[...] = jnp.zeros_like(ref)
    next(sent_gather)
    next(normed_gather)
    drive(sent_gather)
    w_here = w_edge[:, 2 * width :]

    @pl.loop(0, steps)
    def _(step):
        here = pl.ds(step * slots, slots)
        for beat in range(1, steps):
            @pl.when(step == beat)
            def _():
                next(normed_gather, None)

        picks = pick_rows(index[...], step * slots, slots, total)
        edge_rows = edges[here].reshape(slots * count, narrow)
        near_part = dot(picks, sent_table[...].reshape(total, sent_table.shape[-1]))[:, 0:narrow]
        pre = near_part + dot_back(edge_rows, w_here)
        pre = (pre.reshape(slots, count, narrow) + own_edge[...][None]).reshape(slots * count, narrow)
        act_a, slope_a = gelu_pair(pre)
        act_a = act_a.astype(low)
        pre = dot(act_a, ew_mid[...]) + as_row(eb_mid)
        act_b, slope_b = gelu_pair(pre)
        act_b = act_b.astype(low)
        pre = dot(act_b, ew_out[...]) + as_row(eb_out)
        hat, scale = norm_stats(edge_rows.astype(wide) + pre)
        gain_row = as_row(gain_three)
        grad = edge_ct[here].reshape(slots * count, narrow).astype(wide)
        edge_ct[here] = (hat * gain_row + as_row(shift_three)).astype(low).reshape(slots, count, narrow)
        sum_grad = norm_back(hat, scale, gain_row, grad)
        three = sum_grad.astype(low)
        e_out[...] += dot_rows(act_b, three)
        two = (slope_b * dot_back(three, ew_out[...])).astype(low)
        e_mid[...] += dot_rows(act_a, two)
        one = (slope_a * dot_back(two, ew_mid[...])).astype(low)
        e_in[...] += dot_rows(one, edge_rows)
        e_vectors[...] += jnp.concatenate(
            [
                jnp.sum(piece, axis=0, keepdims=True)
                for piece in (grad * hat, grad, three.astype(wide), two.astype(wide), one.astype(wide))
            ]
            + [jnp.zeros((3, narrow), wide)],
            axis=0,
        )
        own_edge_grad[...] += jnp.sum(one.astype(wide).reshape(slots, count, narrow), axis=0)
        partial[here] = (sum_grad + dot(one, w_here)).astype(low).reshape(slots, count, narrow)
        spread_edge[...] += dot(pick_columns(rows[step], total), one)

    result_copy = pltpu.make_async_copy(edge_ct, edge_result, puts.at[steps])
    result_copy.start()
    pad = jnp.zeros((total, spread_two.shape[-1] - narrow), low)
    spread_two[...] = jnp.concatenate([spread_edge[...].astype(low), pad], axis=1).reshape(spread_two.shape)

    moving = []
    clock = [0.0]

    def launch(run, gap):
        next(run)
        moving.append([run, gap, clock[0] + gap])

    def advance(spent):
        clock[0] += spent
        for entry in list(moving):
            if clock[0] >= entry[2]:
                entry[2] = clock[0] + entry[1]
                if next(entry[0], moving) is moving:
                    moving.remove(entry)

    def put_line(name, value):
        lines[places[name] : places[name] + value.shape[0], :] = value

    back = []
    edge_run = scatter_run(spot, spread_two, edge_scratch, back)
    next(edge_run)
    own_low = own_edge_grad[...].astype(low)
    sums.put("edge_own", dot_rows(own_low, out))
    sums.put("e_in", e_in[...])
    sums.put("e_mid", e_mid[...])
    sums.put("e_out", e_out[...])
    sums.put("e_lines", jnp.concatenate([e_vectors[...], jnp.zeros((8, narrow), wide)], axis=0))
    gathers = [normed_gather, gather_run(gather_plan(spot, down_table, down_sems))]
    moving.append([normed_gather, GAP_NORMED, 0.0])
    launch(total_run(spot, partner, given_one, total_one, totals[0]), GAP_EARLY)
    lines[...] = jnp.zeros_like(lines)
    grad = cotangent[...].astype(wide) + dot(own_low, w_edge[:, 0:width])
    hat, scale = norm_stats(second_sum)
    for _ in edge_run:
        advance(3.0)

    back_low = jnp.concatenate(back, axis=0)[:, 0:narrow].astype(low)
    grad = grad + dot(back_low, w_edge[:, width : 2 * width])
    put_line("v_final_gain", jnp.sum(grad * hat, axis=0, keepdims=True))
    put_line("v_final_shift", jnp.sum(grad, axis=0, keepdims=True))
    second = norm_back(hat, scale, as_row(gain_two), grad)
    down = second.astype(low)
    down_table[spot.z, spot.y, spot.x] = down.reshape(down_table.shape[3:])
    launch(gathers[1], GAP_DOWN)
    put_line("v_down", jnp.sum(down.astype(wide), axis=0, keepdims=True))
    sums.put("edge_near", dot_rows(back_low, out))
    up = (up_slope[...] * dot_back(down, w_down[...])).astype(low)
    bias_up = jnp.sum(up.astype(wide), axis=0, keepdims=True)
    for piece in range(hidden // width):
        lines[piece : piece + 1, :] = bias_up[:, piece * width : (piece + 1) * width]
    first = second + dot_back(up, w_up[...])
    put_line("v_node_gain", jnp.sum(first * hat_one, axis=0, keepdims=True))
    put_line("v_node_shift", jnp.sum(first, axis=0, keepdims=True))
    mixed = norm_back(hat_one, scale_one, as_row(gain_one), first)
    masked = mask * mixed
    put_line("v_out", jnp.sum(jnp.where(live > 0, masked, 0.0), axis=0, keepdims=True))
    sums.put("message_out", dot_rows(mixed_low, masked.astype(low)))
    shared = (masked / jnp.maximum(live, 1).astype(wide)).astype(low)
    lift = dot_back(shared, w_out[...])

    advance(4.0)

    own_sum[...] = jnp.zeros_like(own_sum)
    mid_sum[...] = jnp.zeros_like(mid_sum)
    g_mid[...] = jnp.zeros_like(g_mid)
    for step in range(steps):
        here = slice(step * slots, (step + 1) * slots)
        slope = slope_two[here].astype(wide)
        mids = [jnp.where(live > step * slots + s, slope[s] * lift, 0.0).astype(low) for s in range(slots)]
        kept = mid_sum[...]
        for piece in mids:
            kept = kept + piece.astype(wide)
        mid_sum[...] = kept
        mid = jnp.concatenate(mids, axis=0)
        g_mid[...] += dot_rows(act_one[here].reshape(slots * count, width), mid)
        slope = slope_one[here].reshape(slots * count, width).astype(wide)
        inner = (slope * dot_back(mid, w_mid[...])).astype(low).reshape(slots, count, width)
        slope_one[here] = inner
        own_sum[...] += jnp.sum(inner.astype(wide), axis=0)
        advance(1.8)
    own_low = own_sum[...].astype(low)
    sums.put("message_own", dot_rows(node_rows, own_low))
    sums.put("message_mid", g_mid[...])
    put_line("v_mid", jnp.sum(mid_sum[...], axis=0, keepdims=True))
    put_line("v_in", jnp.sum(own_sum[...], axis=0, keepdims=True))
    launch(total_run(spot, partner, given_two, total_two, totals[1]), GAP)
    advance(0.0)
    part = mixed + dot_back(own_low, w_in[0:width])
    node_part[0] = part[0 : count // 2]
    node_part[1] = part[count // 2 :]

    spread_sum[...] = jnp.zeros_like(spread_sum)
    g_edge[...] = jnp.zeros_like(g_edge)
    for step in range(steps):
        here = slice(step * slots, (step + 1) * slots)
        inner = slope_one[here].reshape(slots * count, width)
        g_edge[...] += dot_rows(edges[here].reshape(slots * count, narrow), inner)
        spread_sum[...] += dot(pick_columns(rows[step], total), inner)
        advance(1.6)
    spread_low = spread_sum[...].astype(low)
    spread[...] = spread_low.reshape(spread.shape)
    launch(owner_run(spot, spread, node_part, w_in.at[width : 2 * width], grad_nodes, node_scratch), GAP)
    sums.put("message_near", dot_rows(table[...].reshape(total, width), spread_low))
    launch(total_run(spot, partner, given_three, total_three, totals[2]), GAP)
    sums.put("message_edge", g_edge[...])
    sums.put("lines", lines[...])
    launch(total_run(spot, partner, given_four, total_four, totals[3]), GAP)
    leaving = [result_copy]
    for step in range(steps):
        here = slice(step * slots, (step + 1) * slots)
        inner = slope_one[here].reshape(slots * count, width)
        back_part = dot_back(inner, w_in[2 * width :]).reshape(slots, count, narrow)
        partial[here] = (partial[here].astype(wide) + back_part).astype(low)
        copy = pltpu.make_async_copy(partial.at[here], edge_total.at[here], puts.at[step])
        copy.start()
        leaving.append(copy)
        advance(0.6)
    while any(entry[0] in gathers for entry in moving):
        advance(1.0)
    for _ in feed_run(spot, partner, normed_table, down_table, w_up, b_up, w_down, out_up, out_down, *feed_parts):
        advance(2.0)
    while moving:
        advance(1.0)
    for copy in leaving:
        copy.wait()


def unpack(pieces, places, *refs):
    ins, outs = refs[:8], refs[8:32]
    (m_in_far, m_in_b, m_mid_far, m_mid_b, m_out_far, m_out_b, n_gain, n_shift, f_up_far, f_up_b, f_down_far, f_down_b,
     l_gain, l_shift, e_in_far, e_in_b, e_mid, e_mid_b, e_out, e_out_b, e_gain, e_shift, edge_far, result_far) = outs
    near, (m_in, m_mid, m_out, f_up, f_down, e_in, edge), (reads, writes) = refs[32:40], refs[40:47], refs[47:]
    width, narrow, hidden = m_mid.shape[0], e_mid.shape[0], f_up.shape[1]
    coming = [pltpu.make_async_copy(there, here, reads.at[place]) for place, (there, here) in enumerate(zip(ins, near))]
    groups = near[:4]
    (up_low, down_low, part, result) = near[4:]
    for place in (4, 5, 6, 7, 0, 1, 2, 3):
        coming[place].start()
    leaving = []

    def leave(source, target):
        copy = pltpu.make_async_copy(source, target, writes.at[len(leaving)])
        copy.start()
        leaving.append(copy)

    span = down_low.shape[1]
    coming[4].wait()
    for piece in range(hidden // span):
        lanes = slice(piece * span, (piece + 1) * span)
        f_up[:, lanes] = up_low[piece].astype(wide)
        leave(f_up.at[:, lanes], f_up_far.at[:, lanes])
    coming[5].wait()
    for piece in range(hidden // span):
        lanes = slice(piece * span, (piece + 1) * span)
        f_down[lanes] = down_low[piece].astype(wide)
        leave(f_down.at[lanes], f_down_far.at[lanes])
    coming[6].wait()
    chunk = edge.shape[0] // 5
    for piece in range(5):
        here = slice(piece * chunk, (piece + 1) * chunk)
        edge[here] = part[here].astype(wide)
        leave(edge.at[here], edge_far.at[here])
    coming[7].wait()
    leave(result, result_far)
    for copy in coming[:4]:
        copy.wait()

    def move(name, target, first_row=0, first_lane=0, most=None):
        for piece, first, tall, lane, group, row in pieces:
            if piece == name:
                size = min(groups[group].shape[1], (most or width) - lane)
                target[
                    first_row + first : first_row + first + tall, first_lane + lane : first_lane + lane + size
                ] = groups[group][row : row + tall, 0:size].astype(wide)

    move("message_own", m_in)
    move("message_near", m_in, width)
    move("message_edge", m_in, 2 * width)
    leave(m_in, m_in_far)
    move("message_mid", m_mid)
    leave(m_mid, m_mid_far)
    move("message_out", m_out)
    leave(m_out, m_out_far)
    move("edge_own", e_in)
    move("edge_near", e_in, 0, width)
    move("e_in", e_in, 0, 2 * width, narrow)
    leave(e_in, e_in_far)
    move("e_mid", e_mid, 0, 0, narrow)
    move("e_out", e_out, 0, 0, narrow)

    def rows_of(name):
        found = [groups[group][row : row + 16].astype(wide) for piece, _, _, _, group, row in pieces if piece == name]
        return jnp.concatenate(found, axis=1)

    lines, e_lines = rows_of("lines"), rows_of("e_lines")
    for name, ref in (
        ("v_in", m_in_b), ("v_mid", m_mid_b), ("v_out", m_out_b), ("v_node_gain", n_gain), ("v_node_shift", n_shift),
        ("v_final_gain", l_gain), ("v_final_shift", l_shift), ("v_down", f_down_b),
    ):
        ref[...] = lines[places[name]]
    for piece in range(hidden // width):
        f_up_b[piece * width : (piece + 1) * width] = lines[piece]
    for place, ref in enumerate((e_gain, e_shift, e_out_b, e_mid_b, e_in_b)):
        ref[...] = e_lines[place, 0:narrow]
    for copy in leaving:
        copy.wait()


def table_kernel(grid, own, table, *sems):
    spot = Spot(grid)
    copy = pltpu.make_async_copy(own, table.at[spot.z, spot.y, spot.x], sems[-1])
    copy.start()
    meet(spot.peers())
    copy.wait()
    drive(gather_run(gather_plan(spot, table, sems[:-1])))


def owner_kernel(grid, part, out, *scratch):
    spot = Spot(grid)
    meet(spot.peers())
    sums = []
    drive(scatter_run(spot, part, scratch, sums))
    out[0] = sums[0]
    out[1] = sums[1]


def total_run(spot, partner, given, out, scratch):
    pair, pair_send, pair_arrive, last_send, last_arrive = scratch[:5]
    parts, sems = scratch[5:23], scratch[23:]
    side_z = spot.grid[0]
    core = spot.core
    mine = out.at[core]
    pairs = {}
    for j in range(side_z - 1, -1, -1):
        zj = spot.far_z(j)
        pairs[j] = remote(given.at[1 - core, zj], pair.at[zj], pair_send.at[j], pair_arrive.at[j], partner)
        pairs[j].start()
    yield

    def before(zj, j):
        arrived([pairs[j]])
        mine[zj] = (given[core, zj].astype(wide) + pair[zj].astype(wide)).astype(low)

    sums = []
    yield from scatter_run(spot, mine, parts, sums, before)
    all_sent(pairs.values())
    for half in range(2):
        mine[spot.z, spot.y, spot.x, half] = sums[half].astype(low)
    finals = []

    def plane(j):
        zj = spot.far_z(j)
        copy = remote(mine.at[zj], mine.at[zj], last_send.at[j], last_arrive.at[j], partner)
        copy.start()
        finals.append(copy)

    yield from gather_run(gather_plan(spot, mine, sems), plane)
    arrived(finals)
    all_sent(finals)


def total_scratch(grid, rows, width):
    dma = pltpu.SemaphoreType.DMA
    return (
        [pltpu.VMEM(grid + (2, rows, width), low)]
        + [dma((grid[0],))] * 4
        + scatter_scratch(grid, rows, width)
        + gather_sems(grid)
    )


def owner_run(spot, part, node_part, w_near, out, scratch):
    sums = []
    yield from scatter_run(spot, part, scratch, sums)
    for half in range(2):
        out[half] = node_part[half] + dot_back(sums[half].astype(low), w_near[...])


def feed_run(
    spot, partner, normed_table, down_table, w_up, b_up, w_down, out_up, out_down,
    bias, send_up, send_down, near_up, near_down, sends, arrives, last_sends, last_arrives,
):
    span = w_up.shape[1] // out_up.shape[0]
    half = out_up.shape[0] // 2
    core = spot.core
    width = w_up.shape[0]
    rows = math.prod(normed_table.shape) // width
    bias[...] = as_row(b_up)

    def piece(place):
        normed = normed_table[...].reshape(rows, width)
        down = down_table[...].reshape(rows, width)
        lanes = pl.ds(pl.multiple_of(place * span, span), span)
        act, slope = gelu_pair(dot(normed, w_up[:, lanes]) + bias[:, lanes])
        up = (slope * dot_back(down, w_down[lanes, :])).astype(low)
        return dot_rows(normed, up), dot_rows(act.astype(low), down)

    started = []
    for q in range(half):
        up, down = piece((1 - core) * half + q)
        send_up[q] = up.astype(low)
        send_down[q] = down.astype(low)
        pair = [
            remote(send_up.at[q], near_up.at[q], sends.at[0, q], arrives.at[0, q], partner),
            remote(send_down.at[q], near_down.at[q], sends.at[1, q], arrives.at[1, q], partner),
        ]
        start_all(pair)
        started.append(pair)
        yield
    finals = []
    for q in range(half):
        place = core * half + q
        up, down = piece(place)
        arrived(started[q])
        out_up[place] = (up + near_up[q].astype(wide)).astype(low)
        out_down[place] = (down + near_down[q].astype(wide)).astype(low)
        pair = [
            remote(out_up.at[place], out_up.at[place], last_sends.at[0, q], last_arrives.at[0, q], partner),
            remote(out_down.at[place], out_down.at[place], last_sends.at[1, q], last_arrives.at[1, q], partner),
        ]
        start_all(pair)
        finals += pair
        yield
    arrived(finals)
    all_sent(flat(started) + finals)


def feed_scratch(width, hidden, pieces):
    dma = pltpu.SemaphoreType.DMA
    span, half = hidden // pieces, pieces // 2
    return (
        [pltpu.VMEM((1, hidden), wide)]
        + [pltpu.VMEM((half, width, span), low), pltpu.VMEM((half, span, width), low)] * 2
        + [dma((2, half))] * 4
    )


def tail_kernel(
    grid, given, part, node_part, w_near, table, w_up, b_up, w_down, summed, out_nodes, out_up, out_down, *scratch
):
    spot = Spot(grid)
    partner = (1 - spot.core, lax.axis_index("res"))
    meet(spot.peers() + [partner])
    total = total_run(spot, partner, given, summed, scratch[:33])
    owner = owner_run(spot, part, node_part, w_near, out_nodes, scratch[33:51])
    feed = feed_run(spot, partner, table.at[:, :, :, 0], table.at[:, :, :, 1], w_up, b_up, w_down, out_up, out_down, *scratch[51:])
    runs = [owner, total, feed]
    while runs:
        for run in list(runs):
            if next(run, runs) is runs:
                runs.remove(run)


vmem = pl.BlockSpec(memory_space=pltpu.VMEM)
far = pl.BlockSpec(memory_space=pl.ANY)
most_vmem = 67_000_000


def params(collective=None, **more):
    if collective is None:
        return pltpu.CompilerParams(vmem_limit_bytes=most_vmem, **more)
    return pltpu.CompilerParams(
        collective_id=collective, has_side_effects=True, vmem_limit_bytes=most_vmem, **more
    )


def gather_table(grid, rows, collective):
    count, width = rows.shape
    table = pl.pallas_call(
        functools.partial(table_kernel, grid),
        out_shape=jax.ShapeDtypeStruct(grid + (2, count // 2, width), low),
        in_specs=[vmem],
        out_specs=vmem,
        scratch_shapes=gather_sems(grid) + [pltpu.SemaphoreType.DMA],
        compiler_params=params(collective),
        name="gather_table_%d" % width,
    )(rows.reshape(2, count // 2, width))
    return table.reshape(-1, width)


def held(array):
    return pl.BlockSpec(array.shape, lambda step, dims=len(array.shape): (0,) * dims, pipeline_mode=pl.Buffered(1))


def streamed(array, slots):
    return pl.BlockSpec((slots,) + array.shape[1:], lambda step, dims=len(array.shape): (step,) + (0,) * (dims - 1))


def call(kernel, name, steps, slots, inputs, outputs, scratch, collective=None):
    def spec(item, flow):
        return streamed(item, slots if item.shape[0] != steps else 1) if flow else held(item)
    return pl.pallas_call(
        kernel,
        grid=(steps,),
        in_specs=[spec(item, flow) for item, flow in inputs],
        out_specs=[spec(item, flow) for item, flow in outputs],
        out_shape=[item for item, _ in outputs],
        scratch_shapes=scratch,
        compiler_params=params(collective),
        name=name,
    )(*[item for item, _ in inputs])


def per_device(
    node_states, edge_states, neighbours, residue_mask, neighbour_count,
    message_in, message_in_bias, message_mid, message_mid_bias, message_out, message_out_bias,
    node_gain, node_shift, feed_up, feed_up_bias, feed_down, feed_down_bias, final_gain, final_shift,
    edge_in, edge_in_bias, edge_mid, edge_mid_bias, edge_out, edge_out_bias, edge_gain, edge_shift,
    node_cotangent, edge_cotangent,
):
    grid = chip_grid(lax.axis_size("res"))
    nodes = node_states[0]
    count, width = nodes.shape
    edges = jnp.transpose(edge_states[0], (1, 0, 2))
    edge_ct = jnp.transpose(edge_cotangent[0], (1, 0, 2))
    depth, _, narrow = edges.shape
    hidden = feed_up.shape[1]
    slots = 12
    steps = depth // slots
    total = grid[0] * grid[1] * grid[2] * count
    index = neighbours[0]
    rows = jnp.transpose(index).reshape(steps, 1, slots * count)
    edge_in_t = jnp.transpose(edge_in)
    lanes = -(-narrow // 128) * 128
    shape = jax.ShapeDtypeStruct
    slab = shape((depth, count, width), low)
    node_low, node_wide = shape((count, width), low), shape((count, width), wide)
    scratch = pltpu.VMEM

    square = shape((narrow, narrow), wide)
    if total <= 1024:
        places = line_places(width, hidden)
        blocks = (2,) + grid + (2, 16, width)
        each = math.prod(blocks[:-1])
        cut = sum_pieces(width, narrow, each)
        pieces = hidden // 256
        half_rows = (2, count // 2, width)
        lane_rows = (2, count // 2, lanes)
        dma = pltpu.SemaphoreType.DMA
        whole, few = shape(blocks, low), shape(blocks[:-1] + (width // 2,), low)
        near = [
            index, rows, neighbour_count, residue_mask, nodes.reshape(half_rows), message_in_bias, message_mid_bias,
            message_out_bias, node_gain, node_shift, feed_up_bias, feed_down_bias, final_gain, final_shift,
            edge_in_bias, edge_mid, edge_mid_bias, edge_out, edge_out_bias, edge_gain, edge_shift, node_cotangent[0],
        ]
        distant = [edges, edge_ct, message_in, message_mid, message_out, feed_up, feed_down, edge_in_t]
        strip = scratch((count, narrow), wide)
        (node_out, edge_result, edge_total, grad_nodes, *totals, up_low, down_low) = pl.pallas_call(
            functools.partial(whole_kernel, grid, slots, cut, places),
            out_shape=[node_low, shape(edges.shape, low), shape(edges.shape, low), shape(half_rows, wide),
                       few, whole, whole, few,
                       shape((pieces, width, hidden // pieces), low), shape((pieces, hidden // pieces, width), low)],
            in_specs=[vmem] * len(near) + [far] * len(distant),
            out_specs=[vmem, far, far] + [vmem] * 7,
            scratch_shapes=[scratch(a.shape, low) for a in distant] + [dma((8,)), dma((steps + 2,))]
            + [scratch(slab.shape, low)] * 3
            + [scratch(edges.shape, low), scratch(grid + half_rows, low),
               scratch((count, width), wide), scratch((count, width), wide), scratch((count, hidden), wide),
               scratch(grid + lane_rows, low), strip, scratch((total, narrow), wide), scratch(grid + lane_rows, low),
               strip] + [scratch(square.shape, wide)] * 3 + [scratch((8, narrow), wide)]
            + [scratch((total, width), wide), scratch(grid + half_rows, low),
               scratch((count, width), wide), scratch((count, width), wide), scratch((width, width), wide),
               scratch((narrow, width), wide), scratch((16, width), wide), scratch(half_rows, wide),
               scratch(grid + half_rows, low), scratch(grid + half_rows, low)]
            + [scratch(a.shape, low) for a in (few, whole, whole, few)]
            + gather_sems(grid) * 4
            + scatter_scratch(grid, count // 2, lanes) + scatter_scratch(grid, count // 2, width)
            + feed_scratch(width, hidden, pieces) + total_scratch(grid, 16, width // 2)
            + total_scratch(grid, 16, width) * 2 + total_scratch(grid, 16, width // 2),
            compiler_params=params(0), name="whole",
        )(*near, *distant)
        grad_nodes = grad_nodes.reshape(count, width)
        vector, line = shape((width,), wide), shape((narrow,), wide)
        sources = [each_total.reshape(each, -1) for each_total in totals] + [up_low, down_low, edge_total, edge_result]
        kinds = [message_in.shape, vector, message_mid.shape, vector, message_out.shape, vector, vector, vector,
                 feed_up.shape, shape((hidden,), wide), feed_down.shape, vector, vector, vector, edge_in_t.shape, line,
                 square, line, square, line, line, line, edges.shape]
        staged = [kind for kind in kinds if isinstance(kind, tuple)]
        *grads, edge_grad, edge_result = pl.pallas_call(
            functools.partial(unpack, cut, places),
            out_shape=[shape(kind, wide) if isinstance(kind, tuple) else kind for kind in kinds] + [shape(edges.shape, low)],
            in_specs=[far] * 8, out_specs=[far if isinstance(kind, tuple) else vmem for kind in kinds] + [far],
            scratch_shapes=[scratch(a.shape, low) for a in sources] + [scratch(kind, wide) for kind in staged]
            + [dma((8,)), dma((32,))],
            compiler_params=params(), name="unpack",
        )(*sources)
    else:
        table = gather_table(grid, nodes, 0)
        (slope_one, slope_two, act_one, mixed_low, resid, second_sum, up_slope, node_out, sent, own_edge) = call(
            functools.partial(message_forward, slots), "message_forward", steps, slots,
            [(index, False), (neighbour_count, False), (residue_mask, False), (nodes, False), (table, False), (edges, True)]
            + [(a, False) for a in (
                message_in, message_in_bias, message_mid, message_mid_bias, message_out, message_out_bias,
                node_gain, node_shift, feed_up, feed_up_bias, feed_down, feed_down_bias, final_gain, final_shift,
                edge_in_t, edge_in_bias)],
            [(slab, True)] * 3 + [(node_low, False), (node_wide, False), (node_wide, False),
             (shape((count, hidden), wide), False), (node_low, False),
             (shape((count, lanes), low), False), (shape((count, narrow), wide), False)],
            [scratch((total, width), low), scratch((count, width), wide), scratch((count, width), wide)],
        )
        sent_table = gather_table(grid, sent, 1)
        (edge_result, partial, spread_two, own_edge_grad, e_in, e_mid, e_out, e_vectors) = call(
            functools.partial(edge_pass, slots), "edge_pass", steps, slots,
            [(index, False), (rows, True), (sent_table, False), (own_edge, False), (edges, True), (edge_ct, True)]
            + [(a, False) for a in (edge_in_t, edge_mid, edge_mid_bias, edge_out, edge_out_bias, edge_gain, edge_shift)],
            [(shape(edges.shape, low), True), (shape(edges.shape, low), True), (shape((total, lanes), low), False),
             (shape((count, narrow), wide), False), (square, False), (square, False), (square, False),
             (shape((8, narrow), wide), False)],
            [scratch((total, narrow), wide)],
        )
        back_edge = pl.pallas_call(
            functools.partial(owner_kernel, grid),
            out_shape=shape((2, count // 2, lanes), wide),
            in_specs=[vmem], out_specs=vmem,
            scratch_shapes=scatter_scratch(grid, count // 2, lanes),
            compiler_params=params(2), name="edge_owner",
        )(spread_two.reshape(grid + (2, count // 2, lanes))).reshape(count, lanes)[:, :narrow]
        shares = 4 * grid[0] * grid[1] * grid[2] * 16
        layout = lay_out_rows(width, narrow, hidden, shares)
        table_blocks = grid + (2, count, width)
        (edge_grad, spread, node_part, packed, feed_table) = call(
            functools.partial(node_backward, grid, slots, layout), "node_backward", steps, slots,
            [(rows, True), (neighbour_count, False), (residue_mask, False), (nodes, False), (table, False), (edges, True),
             (slope_one, True), (slope_two, True), (act_one, True), (partial, True)]
            + [(a, False) for a in (
                mixed_low, resid, second_sum, up_slope, node_out, node_cotangent[0], back_edge, own_edge_grad,
                e_in, e_mid, e_out, e_vectors, message_in, message_mid, message_out, node_gain, node_shift,
                feed_up, feed_down, final_gain, edge_in_t)],
            [(shape(edges.shape, wide), True), (shape((total, width), low), False), (node_wide, False),
             (shape((layout["rows"], width), low), False), (shape(table_blocks, low), False)],
            [scratch((count, width), wide), scratch((total, width), wide), scratch((count, width), wide),
             scratch((width, width), wide), scratch((narrow, width), wide), scratch((1, width), wide),
             scratch((32, width), wide), scratch(table_blocks, low)] + gather_sems(grid),
            collective=3,
        )
        chunk = layout["rows"] // (4 * grid[0] * grid[1] * grid[2])
        blocks = (2,) + grid + (2, chunk, width)
        pieces = hidden // 256
        (summed, grad_nodes, up_low, down_low) = pl.pallas_call(
            functools.partial(tail_kernel, grid),
            out_shape=[shape(blocks, low), shape((2, count // 2, width), wide),
                       shape((pieces, width, hidden // pieces), low), shape((pieces, hidden // pieces, width), low)],
            in_specs=[vmem] * 8, out_specs=[vmem] * 4,
            scratch_shapes=total_scratch(grid, chunk, width) + scatter_scratch(grid, count // 2, width)
            + feed_scratch(width, hidden, pieces),
            compiler_params=params(4), name="tail",
        )(packed.reshape(blocks), spread.reshape(grid + (2, count // 2, width)), node_part.reshape(2, count // 2, width),
          message_in[width : 2 * width], feed_table, feed_up, feed_up_bias, feed_down)
        grad_nodes = grad_nodes.reshape(count, width)
        vector, line = shape((width,), wide), shape((narrow,), wide)
        grads = pl.pallas_call(
            functools.partial(unpack_rows, layout),
            out_shape=[
                shape(message_in.shape, wide), vector, shape(message_mid.shape, wide), vector,
                shape(message_out.shape, wide), vector, vector, vector, shape(feed_up.shape, wide), shape((hidden,), wide),
                shape(feed_down.shape, wide), vector, vector, vector, shape(edge_in_t.shape, wide), line,
                square, line, square, line, line, line,
            ],
            in_specs=[vmem] * 3, out_specs=[vmem] * 22,
            compiler_params=params(), name="unpack",
        )(summed.reshape(layout["rows"], width), up_low, down_low)
    grads = list(grads)
    grads[14] = jnp.transpose(grads[14])
    back = (1, 0, 2)
    return (
        node_out[None],
        jnp.transpose(edge_result, back)[None],
        grad_nodes[None],
        jnp.transpose(edge_grad, back)[None],
        *grads,
    )


def solution(mesh):
    split, whole = P("batch", "res"), P()
    in_specs = (split,) * 5 + (whole,) * 22 + (split,) * 2
    out_specs = (split,) * 4 + (whole,) * 22
    return jax.shard_map(per_device, mesh=mesh, in_specs=in_specs, out_specs=out_specs, check_vma=False)
```

```python
import functools
import math
import jax
import jax.numpy as jnp
from jax import lax
from jax.experimental import pallas as pl
from jax.experimental.pallas import tpu as pltpu
from jax.sharding import PartitionSpec as P

MESH = pl.DeviceIdType.MESH
low = jnp.bfloat16
FEED_BEAT = 2
wide = jnp.float32


def chip_grid(count):
    side_x = 2 if count < 64 else 4
    side_y = side_x
    return (count // (side_x * side_y), side_y, side_x)


def flip(place, step):
    bit = 1
    while bit <= step:
        if step & bit:
            place = place + bit - 2 * bit * ((place // bit) % 2)
        bit *= 2
    return place


class Spot:
    def __init__(self, grid):
        self.grid = grid
        side_z, side_y, side_x = grid
        me = lax.axis_index("res")
        self.core = lax.axis_index("batch")
        self.z = me // (side_y * side_x)
        self.y = (me // side_x) % side_y
        self.x = me % side_x

    def device(self, z, y, x):
        return (self.core, (z * self.grid[1] + y) * self.grid[2] + x)

    def far_z(self, step):
        return flip(self.z, step)

    def far_y(self, step):
        return flip(self.y, step)

    def far_x(self, step):
        return flip(self.x, step)

    def peers(self):
        found = [self.device(self.far_z(s), self.y, self.x) for s in range(1, self.grid[0])]
        found += [self.device(self.z, self.far_y(s), self.x) for s in range(1, self.grid[1])]
        found += [self.device(self.z, self.y, self.far_x(s)) for s in range(1, self.grid[2])]
        return found


def greet(peers):
    barrier = pltpu.get_barrier_semaphore()
    for peer in peers:
        pl.semaphore_signal(barrier, inc=1, device_id=peer, device_id_type=MESH)


def met(peers):
    pl.semaphore_wait(pltpu.get_barrier_semaphore(), len(peers))


def meet(peers):
    greet(peers)
    met(peers)


def remote(source, target, send, arrive, device):
    return pltpu.make_async_remote_copy(
        src_ref=source, dst_ref=target, send_sem=send, recv_sem=arrive,
        device_id=device, device_id_type=MESH,
    )


def gather_sems(grid):
    side_z, side_y, side_x = grid
    dma = pltpu.SemaphoreType.DMA
    shapes = [(side_z - 1,), (side_z, side_x - 1), (side_z, side_y - 1), (side_z, side_y - 1), (side_z, side_x - 1)]
    return [dma(s) for s in shapes for _ in range(2)]


def gather_plan(spot, table, sems):
    (s1, r1, s2a, r2a, s2b, r2b, s3a, r3a, s3b, r3b) = sems
    side_z, side_y, side_x = spot.grid
    z, y, x = spot.z, spot.y, spot.x

    def push(view, send, arrive, device):
        return remote(view, view, send, arrive, device)

    ups = [
        push(table.at[z, y, x], s1.at[s - 1], r1.at[s - 1], spot.device(spot.far_z(s), y, x))
        for s in range(1, side_z)
    ]
    firsts, lasts = [], []
    for j in range(side_z):
        zj = flip(z, j)
        firsts.append(
            [
                push(table.at[zj, y, x, 0], s2a.at[j, s - 1], r2a.at[j, s - 1], spot.device(z, y, spot.far_x(s)))
                for s in range(1, side_x)
            ]
            + [
                push(table.at[zj, y, x, 1], s2b.at[j, s - 1], r2b.at[j, s - 1], spot.device(z, spot.far_y(s), x))
                for s in range(1, side_y)
            ]
        )
        lasts.append(
            [
                push(table.at[zj, y, :, 0], s3a.at[j, s - 1], r3a.at[j, s - 1], spot.device(z, spot.far_y(s), x))
                for s in range(1, side_y)
            ]
            + [
                push(table.at[zj, :, x, 1], s3b.at[j, s - 1], r3b.at[j, s - 1], spot.device(z, y, spot.far_x(s)))
                for s in range(1, side_x)
            ]
        )
    return ups, firsts, lasts


def start_all(copies):
    for copy in copies:
        copy.start()


def arrived(copies):
    for copy in copies:
        copy.wait_recv()


def all_sent(copies):
    for copy in copies:
        copy.wait_send()


def flat(groups):
    return [copy for group in groups for copy in group]


def gather_run(plan):
    ups, firsts, lasts = plan
    count = len(lasts)
    start_all(ups + firsts[0])
    yield
    for j in range(1, count):
        arrived([ups[j - 1]])
        start_all(firsts[j])
        arrived(firsts[j - 1])
        start_all(lasts[j - 1])
        if j + 1 < count:
            yield
    arrived(firsts[count - 1])
    start_all(lasts[count - 1])
    yield
    for j in range(count):
        arrived(lasts[j])
    yield
    all_sent(ups + flat(firsts) + flat(lasts))


def drive(run):
    for _ in run:
        pass


def scatter_scratch(grid, rows, width):
    side_z, side_y, side_x = grid
    return [
        pltpu.VMEM((side_z, side_y - 1, side_x, rows, width), low),
        pltpu.VMEM((side_z, side_x - 1, side_y, rows, width), low),
        pltpu.VMEM((side_z, side_x - 1, rows, width), low),
        pltpu.VMEM((side_z, side_y - 1, rows, width), low),
        pltpu.VMEM((side_z - 1, 2, rows, width), low),
        pltpu.VMEM((side_z, side_x, rows, width), low),
        pltpu.VMEM((side_z, side_y, rows, width), low),
        pltpu.VMEM((side_z, 2, rows, width), low),
        pltpu.SemaphoreType.DMA((2, 5)),
    ]


def wait_bytes(like, sem):
    pltpu.make_async_copy(like, like, sem).wait()


def scatter_run(spot, part, scratch, result, before=None):
    (ra1, rb1, ra2, rb2, r3, ka, kb, tot, sems) = scratch
    places = (ra1, rb1, ra2, rb2, r3)
    side_z, side_y, side_x = spot.grid
    z, y, x = spot.z, spot.y, spot.x

    def go(source, target, kind, device):
        remote(source, target, sems.at[0, kind], sems.at[1, kind], device).start()

    def come(kind):
        wait_bytes(places[kind], sems.at[1, kind])

    order = range(side_z - 1, -1, -1)
    if before is not None:
        before()
    for j in order:
        zj = flip(z, j)
        for s in range(1, side_y):
            go(part.at[zj, spot.far_y(s), :, 0], ra1.at[j, s - 1], 0, spot.device(z, spot.far_y(s), x))
        for s in range(1, side_x):
            go(part.at[zj, :, spot.far_x(s), 1], rb1.at[j, s - 1], 1, spot.device(z, y, spot.far_x(s)))
    yield
    come(0)
    for j in order:
        total = part[flip(z, j), y, :, 0].astype(wide)
        for s in range(side_y - 1):
            total = total + ra1[j, s].astype(wide)
        ka[j] = total.astype(low)
        for s in range(1, side_x):
            go(ka.at[j, spot.far_x(s)], ra2.at[j, s - 1], 2, spot.device(z, y, spot.far_x(s)))
    come(1)
    for j in order:
        total = part[flip(z, j), :, x, 1].astype(wide)
        for s in range(side_x - 1):
            total = total + rb1[j, s].astype(wide)
        kb[j] = total.astype(low)
        for s in range(1, side_y):
            go(kb.at[j, spot.far_y(s)], rb2.at[j, s - 1], 3, spot.device(z, spot.far_y(s), x))
    yield
    come(2)
    come(3)
    for j in order:
        upper = ka[j, x].astype(wide)
        for s in range(side_x - 1):
            upper = upper + ra2[j, s].astype(wide)
        lower = kb[j, y].astype(wide)
        for s in range(side_y - 1):
            lower = lower + rb2[j, s].astype(wide)
        if j:
            tot[j, 0] = upper.astype(low)
            tot[j, 1] = lower.astype(low)
            go(tot.at[j], r3.at[j - 1], 4, spot.device(flip(z, j), y, x))
    yield
    come(4)
    for s in range(side_z - 1):
        upper = upper + r3[s, 0].astype(wide)
        lower = lower + r3[s, 1].astype(wide)
    result += [upper, lower]
    for kind, like in enumerate(places):
        wait_bytes(like, sems.at[0, kind])
eps_norm = 1e-05
root_half = 0.7071067811865476
root_turn = 0.3989422804014327


def dot(left, right):
    return jnp.dot(left, right, preferred_element_type=wide)


def dot_back(left, right):
    return lax.dot_general(left, right, (((1,), (1,)), ((), ())), preferred_element_type=wide)


def dot_rows(left, right):
    return lax.dot_general(left, right, (((0,), (0,)), ((), ())), preferred_element_type=wide)


def gelu_pair(values):
    share = 0.5 + 0.5 * lax.erf(values * root_half)
    slope = share + values * (jnp.exp(values * values * -0.5) * root_turn)
    return values * share, slope


def norm_stats(values):
    centre = jnp.mean(values, axis=-1, keepdims=True)
    centred = values - centre
    variance = jnp.mean(centred * centred, axis=-1, keepdims=True)
    scale = lax.rsqrt(variance + eps_norm)
    return centred * scale, scale


def norm_back(hat, scale, gain, grad):
    inner = grad * gain
    return scale * (
        inner
        - jnp.mean(inner, axis=-1, keepdims=True)
        - hat * jnp.mean(inner * hat, axis=-1, keepdims=True)
    )


def as_row(ref, start=None, size=None):
    return ref[...].astype(wide).reshape(1, ref.shape[0])


def as_column(row, count):
    rows = lax.broadcasted_iota(jnp.int32, (count, count), 0)
    lanes = lax.broadcasted_iota(jnp.int32, (count, count), 1)
    return jnp.sum(jnp.where(rows == lanes, jnp.broadcast_to(row, (count, count)), 0), axis=1, keepdims=True)


def slot_column(index, slot):
    lanes = lax.broadcasted_iota(jnp.int32, index.shape, 1)
    return jnp.sum(jnp.where(lanes == slot, index, 0), axis=1, keepdims=True)


def pick_rows(index, first, slots, total):
    count = index.shape[0]
    lanes = lax.broadcasted_iota(jnp.int32, (count, total), 1)
    return jnp.concatenate(
        [jnp.where(slot_column(index, first + s) == lanes, 1.0, 0.0).astype(low) for s in range(slots)], axis=0
    )


def pick_columns(row, total):
    rows = lax.broadcasted_iota(jnp.int32, (total, row.shape[1]), 0)
    return jnp.where(rows == row, 1.0, 0.0).astype(low)


def message_forward(
    slots, index, counts, masks, nodes, table, edges, w_in, b_in, w_mid, b_mid, w_out, b_out,
    gain_one, shift_one, w_up, b_up, w_down, b_down, gain_two, shift_two, w_edge, b_edge,
    slope_one, slope_two, act_one, mixed_low, resid, second_sum, up_slope, node_out, sent, own_edge,
    projected, own, pooled,
):
    step = pl.program_id(0)
    count, width = nodes.shape
    total = table.shape[0]
    live = as_column(counts[...], count)

    @pl.when(step == 0)
    def _():
        projected[...] = dot(table[...], w_in[width : 2 * width]).astype(low)
        own[...] = dot(nodes[...], w_in[0:width]) + as_row(b_in)
        pooled[...] = jnp.zeros_like(pooled)

    picks = pick_rows(index[...], step * slots, slots, total)
    edge_rows = edges[...].reshape(slots * count, edges.shape[2])
    pre = dot(picks, projected[...]) + dot(edge_rows, w_in[2 * width :])
    pre = pre.reshape(slots, count, width) + own[...][None]
    act, slope = gelu_pair(pre)
    act = act.astype(low)
    act_one[...] = act
    slope_one[...] = slope.astype(low)
    pre = dot(act.reshape(slots * count, width), w_mid[...]) + as_row(b_mid)
    act, slope = gelu_pair(pre)
    act = act.reshape(slots, count, width)
    slope_two[...] = slope.astype(low).reshape(slots, count, width)
    gathered = pooled[...]
    for s in range(slots):
        gathered = gathered + jnp.where(live > step * slots + s, act[s], 0.0)
    pooled[...] = gathered

    @pl.when(step == pl.num_programs(0) - 1)
    def _():
        mean = pooled[...] / jnp.maximum(live, 1).astype(wide)
        mean_low = mean.astype(low)
        mixed_low[...] = mean_low
        some = jnp.where(live > 0, 1.0, 0.0)
        mask = as_column(masks[...], count).astype(wide)
        aggregate = dot(mean_low, w_out[...]) + some * as_row(b_out)
        total_sum = nodes[...].astype(wide) + mask * aggregate
        resid[...] = total_sum
        hat, _ = norm_stats(total_sum)
        first = hat * as_row(gain_one) + as_row(shift_one)
        up = dot(first.astype(low), w_up[...]) + as_row(b_up)
        act_up, slope_up = gelu_pair(up)
        act_up = act_up.astype(low)
        up_slope[...] = slope_up
        summed = first + dot(act_up, w_down[...]) + as_row(b_down)
        second_sum[...] = summed
        hat, _ = norm_stats(summed)
        out = (hat * as_row(gain_two) + as_row(shift_two)).astype(low)
        node_out[...] = out
        pad = jnp.zeros((count, sent.shape[1] - w_edge.shape[0]), low)
        sent[...] = jnp.concatenate([dot_back(out, w_edge[:, width : 2 * width]).astype(low), pad], axis=1)
        own_edge[...] = dot_back(out, w_edge[:, 0:width]) + as_row(b_edge)


def edge_pass(
    slots, index, rows, table, own_edge, edges, cotangent, w_edge, w_mid, b_mid, w_out, b_out, gain, shift,
    result, partial, spread, own_grad, g_in, g_mid, g_out, vectors, spread_sum,
):
    step = pl.program_id(0)
    count, width = own_edge.shape
    total = table.shape[0]
    base = w_edge.shape[1] - width

    @pl.when(step == 0)
    def _():
        spread_sum[...] = jnp.zeros_like(spread_sum)
        for ref in (own_grad, g_in, g_mid, g_out, vectors):
            ref[...] = jnp.zeros_like(ref)

    w_here = w_edge[:, base:]
    picks = pick_rows(index[...], step * slots, slots, total)
    edge_rows = edges[...].reshape(slots * count, width)
    pre = dot(picks, table[...])[:, 0:width] + dot_back(edge_rows, w_here)
    pre = (pre.reshape(slots, count, width) + own_edge[...][None]).reshape(slots * count, width)
    act_one, slope_one = gelu_pair(pre)
    act_one = act_one.astype(low)
    pre = dot(act_one, w_mid[...]) + as_row(b_mid)
    act_two, slope_two = gelu_pair(pre)
    act_two = act_two.astype(low)
    pre = dot(act_two, w_out[...]) + as_row(b_out)
    hat, scale = norm_stats(edge_rows.astype(wide) + pre)
    gain_row = as_row(gain)
    result[...] = (hat * gain_row + as_row(shift)).astype(low).reshape(slots, count, width)
    grad = cotangent[...].reshape(slots * count, width).astype(wide)
    sum_grad = norm_back(hat, scale, gain_row, grad)
    three = sum_grad.astype(low)
    g_out[...] += dot_rows(act_two, three)
    two = (slope_two * dot_back(three, w_out[...])).astype(low)
    g_mid[...] += dot_rows(act_one, two)
    one = (slope_one * dot_back(two, w_mid[...])).astype(low)
    g_in[...] += dot_rows(one, edge_rows)
    vectors[...] += jnp.concatenate(
        [
            jnp.sum(piece, axis=0, keepdims=True)
            for piece in (grad * hat, grad, three.astype(wide), two.astype(wide), one.astype(wide))
        ]
        + [jnp.zeros((3, width), wide)],
        axis=0,
    )
    own_grad[...] += jnp.sum(one.astype(wide).reshape(slots, count, width), axis=0)
    partial[...] = (sum_grad + dot(one, w_here)).astype(low).reshape(slots, count, width)
    spread_sum[...] += dot(pick_columns(rows[0], total), one)

    @pl.when(step == pl.num_programs(0) - 1)
    def _():
        pad = jnp.zeros((total, spread.shape[1] - width), low)
        spread[...] = jnp.concatenate([spread_sum[...].astype(low), pad], axis=1)


def node_backward(
    grid, slots, layout, rows, counts, masks, nodes, table, edges, slope_one, slope_two, act_one, partial,
    mixed_low, resid, second_sum, up_slope, node_out, cotangent, back_edge, own_edge_grad,
    e_in, e_mid, e_out, e_vectors,
    w_in, w_mid, w_out, gain_one, shift_one, w_up, w_down, gain_two, w_edge,
    edge_grad, spread, node_part, packed, feed_table,
    level, spread_sum, own_sum, g_mid, g_edge, bias_mid, lines, held_table, *sems,
):
    step = pl.program_id(0)
    last = pl.num_programs(0) - 1
    spot = Spot(grid)
    peers = spot.peers()
    ups, firsts, lasts = gather_plan(spot, held_table, sems)
    count, width = nodes.shape
    total = table.shape[0]
    narrow = w_edge.shape[0]
    hidden = w_up.shape[1]
    live = as_column(counts[...], count)

    def put(name, value):
        row = layout[name]
        packed[row : row + value.shape[0], :] = value.astype(low)

    def put_line(name, value):
        row = layout[name]
        lines[row : row + value.shape[0], 0 : value.shape[1]] = value

    @pl.when(step == 0)
    def _():
        greet(peers)
        for ref in (spread_sum, own_sum, g_mid, g_edge, bias_mid, lines):
            ref[...] = jnp.zeros_like(ref)
        out = node_out[...]
        own_low = own_edge_grad[...].astype(low)
        back_low = back_edge[...].astype(low)
        put("edge_own", dot_rows(own_low, out))
        put("edge_near", dot_rows(back_low, out))
        pad = jnp.zeros((narrow, width // 2 - narrow), wide)
        put("edge_a", jnp.concatenate([e_in[...], pad, e_mid[...], pad], axis=1))
        put("edge_b", jnp.concatenate([e_out[...], pad, jnp.zeros((narrow, width // 2), wide)], axis=1))
        put_line("e_vectors", e_vectors[...])
        grad = (
            cotangent[...].astype(wide)
            + dot(own_low, w_edge[:, 0:width])
            + dot(back_low, w_edge[:, width : 2 * width])
        )
        hat, scale = norm_stats(second_sum[...])
        put_line("v_final_gain", jnp.sum(grad * hat, axis=0, keepdims=True))
        put_line("v_final_shift", jnp.sum(grad, axis=0, keepdims=True))
        second = norm_back(hat, scale, as_row(gain_two), grad)
        down = second.astype(low)
        put_line("v_down", jnp.sum(down.astype(wide), axis=0, keepdims=True))
        held_table[spot.z, spot.y, spot.x, 1] = down
        up = (up_slope[...] * dot_back(down, w_down[...])).astype(low)
        bias_up = jnp.sum(up.astype(wide), axis=0, keepdims=True)
        hat, scale = norm_stats(resid[...])
        normed = (hat * as_row(gain_one) + as_row(shift_one)).astype(low)
        held_table[spot.z, spot.y, spot.x, 0] = normed
        met(peers)
        start_all(ups + firsts[0])
        for piece in range(hidden // width):
            lines[layout["v_up"] + piece : layout["v_up"] + piece + 1, :] = bias_up[:, piece * width : (piece + 1) * width]
        first = second + dot_back(up, w_up[...])
        put_line("v_node_gain", jnp.sum(first * hat, axis=0, keepdims=True))
        put_line("v_node_shift", jnp.sum(first, axis=0, keepdims=True))
        mixed = norm_back(hat, scale, as_row(gain_one), first)
        node_part[...] = mixed
        masked = as_column(masks[...], count).astype(wide) * mixed
        put_line("v_out", jnp.sum(jnp.where(live > 0, masked, 0.0), axis=0, keepdims=True))
        put("message_out", dot_rows(mixed_low[...], masked.astype(low)))
        shared = (masked / jnp.maximum(live, 1).astype(wide)).astype(low)
        level[...] = dot_back(shared, w_out[...])

    @pl.when(step == 1)
    def _():
        for j in range(1, len(firsts)):
            arrived([ups[j - 1]])
            start_all(firsts[j])

    @pl.when(step == 2)
    def _():
        for j in range(len(lasts)):
            arrived(firsts[j])
            start_all(lasts[j])

    lift = level[...]
    slope = slope_two[...].astype(wide)
    mid = jnp.concatenate(
        [jnp.where(live > step * slots + s, slope[s] * lift, 0.0).astype(low) for s in range(slots)], axis=0
    )
    flat_one = act_one[...].reshape(slots * count, width)
    g_mid[...] += dot_rows(flat_one, mid)
    bias_mid[...] += jnp.sum(mid.astype(wide), axis=0, keepdims=True)
    slope = slope_one[...].reshape(slots * count, width).astype(wide)
    inner = (slope * dot_back(mid, w_mid[...])).astype(low)
    own_sum[...] += jnp.sum(inner.astype(wide).reshape(slots, count, width), axis=0)
    edge_rows = edges[...].reshape(slots * count, narrow)
    g_edge[...] += dot_rows(edge_rows, inner)
    edge_grad[...] = partial[...].astype(wide) + dot_back(inner, w_in[2 * width :]).reshape(slots, count, narrow)
    spread_sum[...] += dot(pick_columns(rows[0], total), inner)

    @pl.when(step == pl.num_programs(0) - 1)
    def _():
        spread_low = spread_sum[...].astype(low)
        spread[...] = spread_low
        own_low = own_sum[...].astype(low)
        put("message_in", dot_rows(nodes[...], own_low))
        put("message_near", dot_rows(table[...], spread_low))
        put("message_edge", g_edge[...])
        put("message_mid", g_mid[...])
        put_line("v_mid", bias_mid[...])
        put_line("v_in", jnp.sum(own_sum[...], axis=0, keepdims=True))
        here = layout["lines"]
        tall = lines.shape[0]
        packed[here : here + tall, :] = lines[...].astype(low)
        rest = packed.shape[0] - here - tall
        if rest:
            packed[here + tall :, :] = jnp.zeros((rest, width), low)
        node_part[...] += dot_back(own_low, w_in[0:width])
        arrived(flat(lasts))
        all_sent(ups + flat(firsts) + flat(lasts))
        feed_table[...] = held_table[...]


def lay_out_rows(width, narrow, hidden, shares):
    pieces = hidden // width
    sizes = [
        ("message_in", width), ("message_near", width), ("message_edge", narrow), ("message_mid", width),
        ("message_out", width), ("edge_own", narrow),
        ("edge_near", narrow), ("edge_a", narrow), ("edge_b", narrow), ("lines", 32),
    ]
    layout, row = {}, 0
    for name, size in sizes:
        layout[name] = row
        row += size
    layout["rows"] = -(-row // shares) * shares
    layout["e_vectors"] = 0
    layout["v_up"] = 8
    singles = ("v_final_gain", "v_final_shift", "v_down", "v_node_gain", "v_node_shift", "v_out", "v_mid", "v_in")
    for place, name in enumerate(singles):
        layout[name] = 8 + pieces + place
    return layout


def unpack_rows(layout, packed, feed_up_low, feed_down_low, *outs):
    (m_in, m_in_b, m_mid, m_mid_b, m_out, m_out_b, n_gain, n_shift, f_up, f_up_b, f_down, f_down_b,
     l_gain, l_shift, e_in, e_in_b, e_mid, e_mid_b, e_out, e_out_b, e_gain, e_shift) = outs
    width = m_mid.shape[0]
    narrow = e_mid.shape[0]
    hidden = f_up.shape[1]
    half = width // 2

    def big(name, tall, lanes=slice(None)):
        return packed[layout[name] : layout[name] + tall, lanes].astype(wide)

    m_in[0:width] = big("message_in", width)
    m_in[width : 2 * width] = big("message_near", width)
    m_in[2 * width :] = big("message_edge", narrow)
    m_mid[...] = big("message_mid", width)
    m_out[...] = big("message_out", width)
    span = feed_down_low.shape[1]
    for piece in range(hidden // span):
        f_down[piece * span : (piece + 1) * span] = feed_down_low[piece].astype(wide)
        f_up[:, piece * span : (piece + 1) * span] = feed_up_low[piece].astype(wide)
    e_in[:, 0:width] = big("edge_own", narrow)
    e_in[:, width : 2 * width] = big("edge_near", narrow)
    e_in[:, 2 * width :] = big("edge_a", narrow, slice(0, narrow))
    e_mid[...] = big("edge_a", narrow, slice(half, half + narrow))
    e_out[...] = big("edge_b", narrow, slice(0, narrow))
    lines = packed[layout["lines"] : layout["lines"] + 32, :].astype(wide)

    def one(name):
        return lines[layout[name]]

    m_in_b[...] = one("v_in")
    m_mid_b[...] = one("v_mid")
    m_out_b[...] = one("v_out")
    n_gain[...] = one("v_node_gain")
    n_shift[...] = one("v_node_shift")
    l_gain[...] = one("v_final_gain")
    l_shift[...] = one("v_final_shift")
    f_down_b[...] = one("v_down")
    for piece in range(hidden // width):
        f_up_b[piece * width : (piece + 1) * width] = lines[layout["v_up"] + piece]
    for place, ref in enumerate((e_gain, e_shift, e_out_b, e_mid_b, e_in_b)):
        ref[...] = lines[place, 0:narrow]


def sum_pieces(width, narrow, cap):
    half = width // 2
    pieces = []
    row = 0
    for name, tall, lane in (
        ("edge_own", narrow, 0), ("edge_own", narrow, half), ("e_in", narrow, 0), ("e_mid", narrow, 0),
        ("e_out", narrow, 0), ("e_lines", 16, 0),
    ):
        pieces.append((name, 0, tall, lane, 0, row))
        row += tall
    pieces += [("message_out", 0, width, 0, 1, 0), ("message_out", 0, width, half, 1, width)]
    place = 0
    for name, tall in (
        ("edge_near", narrow), ("message_mid", width), ("message_own", width), ("message_near", width),
        ("message_edge", narrow), ("lines", 16),
    ):
        done = 0
        while done < tall:
            size = min(tall - done, cap - place % cap)
            pieces.append((name, done, size, 0, 2 + place // cap, place % cap))
            place += size
            done += size
    return pieces


def line_places(width, hidden):
    pieces = hidden // width
    singles = ("v_final_gain", "v_final_shift", "v_down", "v_node_gain", "v_node_shift", "v_out", "v_mid", "v_in")
    places = {name: pieces + place for place, name in enumerate(singles)}
    places["v_up"] = 0
    return places


class Sums:
    def __init__(self, pieces, groups):
        self.pieces, self.groups = pieces, groups

    def put(self, name, value):
        value = value.astype(low)
        for piece, first, tall, lane, group, row in self.pieces:
            if piece != name:
                continue
            ref = self.groups[group]
            part = value[first : first + tall, lane : lane + ref.shape[-1]]
            if part.shape[1] < ref.shape[-1]:
                part = jnp.concatenate([part, jnp.zeros((tall, ref.shape[-1] - part.shape[1]), low)], axis=1)
            for start in range(0, tall, 16):
                place, rest = [], (row + start) // 16
                for size in reversed(ref.shape[:-2]):
                    place.append(rest % size)
                    rest //= size
                ref[tuple(reversed(place))] = part[start : start + 16]


def whole_kernel(
    grid, slots, pieces, places,
    near_index, counts, masks, nodes, b_in, b_mid, b_out, gain_one, shift_one, b_up, b_down, gain_two, shift_two,
    eb_in, ew_mid, eb_mid, ew_out, eb_out, gain_three, shift_three, cotangent,
    edges_far, edge_ct_far, w_in_far, w_mid_far, w_out_far, w_up_far, w_down_far, w_edge_far,
    node_out, edge_result, edge_total, grad_nodes, total_one, total_two, total_three, total_four, out_up, out_down,
    edges, edge_ct, w_in, w_mid, w_out, w_up, w_down, w_edge, fetches, puts, index, rows,
    slope_one, slope_two, act_one, partial, table, own, pooled, up_slope, sent_table, own_edge,
    spread_edge, spread_two, own_edge_grad, e_in, e_mid, e_out, e_vectors,
    spread_sum, spread, own_sum, mid_sum, g_mid, g_edge, lines, node_part, normed_table, down_table,
    given_one, given_two, given_three, given_four,
    *scratch,
):
    scratch = list(scratch)

    def take(size):
        taken = scratch[:size]
        del scratch[:size]
        return taken

    spot = Spot(grid)
    partner = (1 - spot.core, lax.axis_index("res"))
    peers = spot.peers() + [partner]
    greet(peers)
    _, half_count, width = nodes.shape
    count = 2 * half_count
    total = spread_sum.shape[0]
    narrow = w_edge.shape[0]
    hidden = w_up.shape[1]
    steps = rows.shape[0]
    local = pltpu.make_async_copy(nodes, table.at[spot.z, spot.y, spot.x], puts.at[steps + 1])
    local.start()
    pairs = (
        (w_in_far, w_in), (edges_far, edges), (w_mid_far, w_mid), (w_out_far, w_out), (w_up_far, w_up),
        (w_down_far, w_down), (w_edge_far, w_edge), (edge_ct_far, edge_ct),
    )
    coming = [pltpu.make_async_copy(there, near, fetches.at[place]) for place, (there, near) in enumerate(pairs)]
    start_all(coming)
    node_sems, sent_sems, normed_sems, down_sems = take(10), take(10), take(10), take(10)
    edge_scratch, node_scratch, feed_parts = take(9), take(9), take(9)
    totals = [take(11) for _ in range(4)]
    sums = Sums(pieces, (given_one, given_two, given_three, given_four))
    live = as_column(counts[...], count)
    lane = lax.broadcasted_iota(jnp.int32, (count, slots * count), 1)
    same = lane % count == lax.broadcasted_iota(jnp.int32, (count, slots * count), 0)
    fold = jnp.where(same, 1.0, 0.0).astype(low)
    ones = jnp.ones((8, slots * count), low)
    mask = as_column(masks[...], count).astype(wide)
    node_rows = nodes[...].reshape(count, width)
    local.wait()
    met(peers)
    node_gather = gather_run(gather_plan(spot, table, node_sems))
    next(node_gather)
    coming[0].wait()
    index[...] = jnp.transpose(near_index[:, 0, :])
    for step in range(steps):
        rows[step] = jnp.concatenate([near_index[step * slots + s] for s in range(slots)], axis=1)
    own[...] = dot(node_rows, w_in[0:width]) + as_row(b_in)
    pooled[...] = jnp.zeros_like(pooled)
    drive(node_gather)
    spread[...] = dot(table[...].reshape(total, width), w_in[width : 2 * width]).astype(low).reshape(spread.shape)
    for copy in coming[1:3]:
        copy.wait()

    @pl.loop(0, steps)
    def _(step):
        here = pl.ds(step * slots, slots)
        picks = pick_rows(index[...], step * slots, slots, total)
        edge_rows = edges[here].reshape(slots * count, narrow)
        pre = dot(picks, spread[...].reshape(total, width)) + dot(edge_rows, w_in[2 * width :])
        pre = pre.reshape(slots, count, width) + own[...][None]
        act, slope = gelu_pair(pre)
        act = act.astype(low)
        act_one[here] = act
        slope_one[here] = slope.astype(low)
        pre = dot(act.reshape(slots * count, width), w_mid[...]) + as_row(b_mid)
        act, slope = gelu_pair(pre)
        slope_two[here] = slope.astype(low).reshape(slots, count, width)
        valid = jnp.where(same & (live > step * slots + lane // count), 1.0, 0.0).astype(low)
        pooled[...] += dot(valid, act.astype(low))

    mixed_low = (pooled[...] / jnp.maximum(live, 1).astype(wide)).astype(low)
    some = jnp.where(live > 0, 1.0, 0.0)
    for copy in coming[3:]:
        copy.wait()
    aggregate = dot(mixed_low, w_out[...]) + some * as_row(b_out)
    hat_one, scale_one = norm_stats(node_rows.astype(wide) + mask * aggregate)
    first = hat_one * as_row(gain_one) + as_row(shift_one)
    first_low = first.astype(low)
    normed_table[spot.z, spot.y, spot.x] = first_low.reshape(normed_table.shape[3:])
    act_up, slope_up = gelu_pair(dot(first_low, w_up[...]) + as_row(b_up))
    up_slope[...] = slope_up
    second_sum = first + dot(act_up.astype(low), w_down[...]) + as_row(b_down)
    hat, _ = norm_stats(second_sum)
    out = (hat * as_row(gain_two) + as_row(shift_two)).astype(low)
    node_out[...] = out
    pad = jnp.zeros((count, sent_table.shape[-1] - narrow), low)
    sent = jnp.concatenate([dot_back(out, w_edge[:, width : 2 * width]).astype(low), pad], axis=1)
    sent_table[spot.z, spot.y, spot.x] = sent.reshape(sent_table.shape[3:])
    sent_gather = gather_run(gather_plan(spot, sent_table, sent_sems))
    next(sent_gather)
    normed_gather = gather_run(gather_plan(spot, normed_table, normed_sems))
    own_edge[...] = dot_back(out, w_edge[:, 0:width]) + as_row(eb_in)
    spread_edge[...] = jnp.zeros_like(spread_edge)
    for ref in (own_edge_grad, e_in, e_mid, e_out, e_vectors):
        ref[...] = jnp.zeros_like(ref)
    next(sent_gather)
    next(normed_gather)
    drive(sent_gather)
    w_here = w_edge[:, 2 * width :]

    @pl.loop(0, steps)
    def _(step):
        here = pl.ds(step * slots, slots)
        for beat in range(1, steps):
            @pl.when(step == beat)
            def _():
                next(normed_gather, None)

        picks = pick_rows(index[...], step * slots, slots, total)
        edge_rows = edges[here].reshape(slots * count, narrow)
        near_part = dot(picks, sent_table[...].reshape(total, sent_table.shape[-1]))[:, 0:narrow]
        pre = near_part + dot_back(edge_rows, w_here)
        pre = (pre.reshape(slots, count, narrow) + own_edge[...][None]).reshape(slots * count, narrow)
        act_a, slope_a = gelu_pair(pre)
        act_a = act_a.astype(low)
        pre = dot(act_a, ew_mid[...]) + as_row(eb_mid)
        act_b, slope_b = gelu_pair(pre)
        act_b = act_b.astype(low)
        pre = dot(act_b, ew_out[...]) + as_row(eb_out)
        hat, scale = norm_stats(edge_rows.astype(wide) + pre)
        gain_row = as_row(gain_three)
        grad_low = edge_ct[here].reshape(slots * count, narrow)
        grad = grad_low.astype(wide)
        edge_ct[here] = (hat * gain_row + as_row(shift_three)).astype(low).reshape(slots, count, narrow)
        sum_grad = norm_back(hat, scale, gain_row, grad)
        three = sum_grad.astype(low)
        e_out[...] += dot_rows(act_b, three)
        two = (slope_b * dot_back(three, ew_out[...])).astype(low)
        e_mid[...] += dot_rows(act_a, two)
        one = (slope_a * dot_back(two, ew_mid[...])).astype(low)
        e_in[...] += dot_rows(one, edge_rows)
        e_vectors[...] += jnp.concatenate(
            [
                jnp.sum(grad * hat, axis=0, keepdims=True), dot(ones, grad_low)[0:1], dot(ones, three)[0:1],
                dot(ones, two)[0:1], jnp.zeros((4, narrow), wide),
            ],
            axis=0,
        )
        own_edge_grad[...] += dot(fold, one)
        partial[here] = (sum_grad + dot(one, w_here)).astype(low).reshape(slots, count, narrow)
        spread_edge[...] += dot(pick_columns(rows[step], total), one)

    result_copy = pltpu.make_async_copy(edge_ct, edge_result, puts.at[steps])
    result_copy.start()
    pad = jnp.zeros((total, spread_two.shape[-1] - narrow), low)
    spread_two[...] = jnp.concatenate([spread_edge[...].astype(low), pad], axis=1).reshape(spread_two.shape)

    moving = []

    def launch(run):
        next(run)
        moving.append(run)

    def beat():
        for run in list(moving):
            if next(run, moving) is moving:
                moving.remove(run)

    def put_line(name, value):
        lines[places[name] : places[name] + value.shape[0], :] = value

    back = []
    edge_run = scatter_run(spot, spread_two, edge_scratch, back)
    next(edge_run)
    own_low = own_edge_grad[...].astype(low)
    sums.put("edge_own", dot_rows(own_low, out))
    sums.put("e_in", e_in[...])
    sums.put("e_mid", e_mid[...])
    sums.put("e_out", e_out[...])
    sums.put("e_lines", jnp.concatenate(
        [e_vectors[0:4], jnp.sum(own_edge_grad[...], axis=0, keepdims=True), jnp.zeros((11, narrow), wide)], axis=0
    ))
    gathers = [normed_gather, gather_run(gather_plan(spot, down_table, down_sems))]
    moving.append(normed_gather)
    launch(total_run(spot, partner, given_one, total_one, totals[0]))
    lines[...] = jnp.zeros_like(lines)
    grad = cotangent[...].astype(wide) + dot(own_low, w_edge[:, 0:width])
    hat, scale = norm_stats(second_sum)
    drive(edge_run)

    back_low = jnp.concatenate(back, axis=0)[:, 0:narrow].astype(low)
    grad = grad + dot(back_low, w_edge[:, width : 2 * width])
    put_line("v_final_gain", jnp.sum(grad * hat, axis=0, keepdims=True))
    put_line("v_final_shift", jnp.sum(grad, axis=0, keepdims=True))
    second = norm_back(hat, scale, as_row(gain_two), grad)
    down = second.astype(low)
    down_table[spot.z, spot.y, spot.x] = down.reshape(down_table.shape[3:])
    launch(gathers[1])
    put_line("v_down", jnp.sum(down.astype(wide), axis=0, keepdims=True))
    sums.put("edge_near", dot_rows(back_low, out))
    up = (up_slope[...] * dot_back(down, w_down[...])).astype(low)
    bias_up = jnp.sum(up.astype(wide), axis=0, keepdims=True)
    for piece in range(hidden // width):
        lines[piece : piece + 1, :] = bias_up[:, piece * width : (piece + 1) * width]
    first = second + dot_back(up, w_up[...])
    put_line("v_node_gain", jnp.sum(first * hat_one, axis=0, keepdims=True))
    put_line("v_node_shift", jnp.sum(first, axis=0, keepdims=True))
    mixed = norm_back(hat_one, scale_one, as_row(gain_one), first)
    masked = mask * mixed
    put_line("v_out", jnp.sum(jnp.where(live > 0, masked, 0.0), axis=0, keepdims=True))
    sums.put("message_out", dot_rows(mixed_low, masked.astype(low)))
    shared = (masked / jnp.maximum(live, 1).astype(wide)).astype(low)
    lift = dot_back(shared, w_out[...])

    beat()
    launch(total_run(spot, partner, given_two, total_two, totals[1]))

    own_sum[...] = jnp.zeros_like(own_sum)
    mid_sum[...] = jnp.zeros_like(mid_sum)
    g_mid[...] = jnp.zeros_like(g_mid)
    for step in range(steps):
        here = slice(step * slots, (step + 1) * slots)
        slope = slope_two[here].astype(wide)
        mids = [jnp.where(live > step * slots + s, slope[s] * lift, 0.0).astype(low) for s in range(slots)]
        mid = jnp.concatenate(mids, axis=0)
        mid_sum[...] += dot(ones, mid)
        g_mid[...] += dot_rows(act_one[here].reshape(slots * count, width), mid)
        slope = slope_one[here].reshape(slots * count, width).astype(wide)
        inner = (slope * dot_back(mid, w_mid[...])).astype(low)
        slope_one[here] = inner.reshape(slots, count, width)
        own_sum[...] += dot(fold, inner)
        if step == steps // 2:
            beat()
    own_low = own_sum[...].astype(low)
    sums.put("message_own", dot_rows(node_rows, own_low))
    sums.put("message_mid", g_mid[...])
    put_line("v_mid", mid_sum[0:1])
    put_line("v_in", jnp.sum(own_sum[...], axis=0, keepdims=True))
    beat()
    launch(total_run(spot, partner, given_three, total_three, totals[2]))
    part = mixed + dot_back(own_low, w_in[0:width])
    node_part[0] = part[0 : count // 2]
    node_part[1] = part[count // 2 :]

    spread_sum[...] = jnp.zeros_like(spread_sum)
    g_edge[...] = jnp.zeros_like(g_edge)
    for step in range(steps):
        here = slice(step * slots, (step + 1) * slots)
        inner = slope_one[here].reshape(slots * count, width)
        g_edge[...] += dot_rows(edges[here].reshape(slots * count, narrow), inner)
        spread_sum[...] += dot(pick_columns(rows[step], total), inner)
        if step == steps // 2:
            beat()
    spread_low = spread_sum[...].astype(low)
    spread[...] = spread_low.reshape(spread.shape)
    beat()
    launch(owner_run(spot, spread, node_part, w_in.at[width : 2 * width], grad_nodes, node_scratch))
    sums.put("message_near", dot_rows(table[...].reshape(total, width), spread_low))
    sums.put("message_edge", g_edge[...])
    sums.put("lines", lines[...])
    launch(total_run(spot, partner, given_four, total_four, totals[3]))

    @pl.loop(0, steps)
    def _(step):
        here = pl.ds(step * slots, slots)
        inner = slope_one[here].reshape(slots * count, width)
        back_part = dot_back(inner, w_in[2 * width :]).reshape(slots, count, narrow)
        partial[here] = (partial[here].astype(wide) + back_part).astype(low)

    leaving = [result_copy, pltpu.make_async_copy(partial, edge_total, puts.at[0])]
    leaving[1].start()
    beat()
    while any(run in gathers for run in moving):
        beat()
    feed = feed_run(spot, partner, normed_table, down_table, w_up, b_up, w_down, out_up, out_down, *feed_parts)
    for place, _ in enumerate(feed):
        if place % FEED_BEAT == FEED_BEAT - 1:
            beat()
    while moving:
        beat()
    for copy in leaving:
        copy.wait()


def unpack(pieces, places, node_in, grad_in, *refs):
    node_out, grad_out, refs = refs[8], refs[9], refs[:8] + refs[10:]
    ins, outs = refs[:8], refs[8:32]
    node_out[...] = node_in[...]
    grad_out[...] = grad_in[...].reshape(grad_out.shape)
    (m_in_far, m_in_b, m_mid_far, m_mid_b, m_out_far, m_out_b, n_gain, n_shift, f_up_far, f_up_b, f_down_far, f_down_b,
     l_gain, l_shift, e_in_far, e_in_b, e_mid, e_mid_b, e_out, e_out_b, e_gain, e_shift, edge_far, result_far) = outs
    near, (m_in, m_mid, m_out, f_up, f_down, e_in, edge), (reads, writes) = refs[32:40], refs[40:47], refs[47:]
    width, narrow, hidden = m_mid.shape[0], e_mid.shape[0], f_up.shape[1]
    coming = [pltpu.make_async_copy(there, here, reads.at[place]) for place, (there, here) in enumerate(zip(ins, near))]
    groups = near[:4]
    (up_low, down_low, part, result) = near[4:]
    for place in (4, 5, 6, 7, 0, 1, 2, 3):
        coming[place].start()
    leaving = []

    def leave(source, target):
        copy = pltpu.make_async_copy(source, target, writes.at[len(leaving)])
        copy.start()
        leaving.append(copy)

    span = down_low.shape[1]
    coming[4].wait()
    for piece in range(hidden // span):
        lanes = slice(piece * span, (piece + 1) * span)
        f_up[:, lanes] = up_low[piece].astype(wide)
        leave(f_up.at[:, lanes], f_up_far.at[:, lanes])
    coming[5].wait()
    for piece in range(hidden // span):
        lanes = slice(piece * span, (piece + 1) * span)
        f_down[lanes] = down_low[piece].astype(wide)
        leave(f_down.at[lanes], f_down_far.at[lanes])
    coming[6].wait()
    chunk = edge.shape[0] // 5
    for piece in range(5):
        here = slice(piece * chunk, (piece + 1) * chunk)
        edge[here] = part[here].astype(wide)
        leave(edge.at[here], edge_far.at[here])
    coming[7].wait()
    leave(result, result_far)
    for copy in coming[:4]:
        copy.wait()

    def move(name, target, first_row=0, first_lane=0, most=None):
        for piece, first, tall, lane, group, row in pieces:
            if piece == name:
                size = min(groups[group].shape[1], (most or width) - lane)
                target[
                    first_row + first : first_row + first + tall, first_lane + lane : first_lane + lane + size
                ] = groups[group][row : row + tall, 0:size].astype(wide)

    move("message_own", m_in)
    move("message_near", m_in, width)
    move("message_edge", m_in, 2 * width)
    leave(m_in, m_in_far)
    move("message_mid", m_mid)
    leave(m_mid, m_mid_far)
    move("message_out", m_out)
    leave(m_out, m_out_far)
    move("edge_own", e_in)
    move("edge_near", e_in, 0, width)
    move("e_in", e_in, 0, 2 * width, narrow)
    leave(e_in, e_in_far)
    move("e_mid", e_mid, 0, 0, narrow)
    move("e_out", e_out, 0, 0, narrow)

    def rows_of(name):
        found = [groups[group][row : row + 16].astype(wide) for piece, _, _, _, group, row in pieces if piece == name]
        return jnp.concatenate(found, axis=1)

    lines, e_lines = rows_of("lines"), rows_of("e_lines")
    for name, ref in (
        ("v_in", m_in_b), ("v_mid", m_mid_b), ("v_out", m_out_b), ("v_node_gain", n_gain), ("v_node_shift", n_shift),
        ("v_final_gain", l_gain), ("v_final_shift", l_shift), ("v_down", f_down_b),
    ):
        ref[...] = lines[places[name]]
    for piece in range(hidden // width):
        f_up_b[piece * width : (piece + 1) * width] = lines[piece]
    for place, ref in enumerate((e_gain, e_shift, e_out_b, e_mid_b, e_in_b)):
        ref[...] = e_lines[place, 0:narrow]
    for copy in leaving:
        copy.wait()


def table_kernel(grid, own, table, *sems):
    spot = Spot(grid)
    copy = pltpu.make_async_copy(own, table.at[spot.z, spot.y, spot.x], sems[-1])
    copy.start()
    meet(spot.peers())
    copy.wait()
    drive(gather_run(gather_plan(spot, table, sems[:-1])))


def owner_kernel(grid, part, out, *scratch):
    spot = Spot(grid)
    meet(spot.peers())
    sums = []
    drive(scatter_run(spot, part, scratch, sums))
    out[0] = sums[0]
    out[1] = sums[1]


def total_run(spot, partner, given, out, scratch):
    pair, parts, sems = scratch[0], scratch[1:10], scratch[10]
    (ra1, rb1, ra2, rb2, r3) = parts[:5]
    places = (pair, pair, r3, ra2, rb2, ra1, rb1)
    side_z, side_y, side_x = spot.grid
    z, y, x = spot.z, spot.y, spot.x
    core = spot.core
    mine = out.at[core]

    def go(source, target, kind, device):
        remote(source, target, sems.at[0, kind], sems.at[1, kind], device).start()

    def come(kind):
        wait_bytes(places[kind], sems.at[1, kind])

    go(given.at[1 - core], pair, 0, partner)
    yield

    def before():
        come(0)
        mine[...] = (given[core].astype(wide) + pair[...].astype(wide)).astype(low)

    sums = []
    yield from scatter_run(spot, mine, parts, sums, before)
    for half in range(2):
        mine[z, y, x, half] = sums[half].astype(low)

    def first(zj):
        for s in range(1, side_x):
            go(mine.at[zj, y, x, 0], mine.at[zj, y, x, 0], 3, spot.device(z, y, spot.far_x(s)))
        for s in range(1, side_y):
            go(mine.at[zj, y, x, 1], mine.at[zj, y, x, 1], 4, spot.device(z, spot.far_y(s), x))

    for s in range(1, side_z):
        go(mine.at[z, y, x], mine.at[z, y, x], 2, spot.device(spot.far_z(s), y, x))
    first(z)
    yield
    come(2)
    for s in range(1, side_z):
        first(spot.far_z(s))
    yield
    come(3)
    come(4)
    for j in range(side_z):
        zj = flip(z, j)
        for s in range(1, side_y):
            go(mine.at[zj, y, :, 0], mine.at[zj, y, :, 0], 5, spot.device(z, spot.far_y(s), x))
        for s in range(1, side_x):
            go(mine.at[zj, :, x, 1], mine.at[zj, :, x, 1], 6, spot.device(z, y, spot.far_x(s)))
    yield
    come(5)
    come(6)
    go(mine, mine, 1, partner)
    yield
    come(1)
    for kind, like in enumerate(places):
        wait_bytes(like, sems.at[0, kind])


def total_scratch(grid, rows, width):
    return (
        [pltpu.VMEM(grid + (2, rows, width), low)]
        + scatter_scratch(grid, rows, width)
        + [pltpu.SemaphoreType.DMA((2, 7))]
    )


def owner_run(spot, part, node_part, w_near, out, scratch):
    sums = []
    yield from scatter_run(spot, part, scratch, sums)
    for half in range(2):
        out[half] = node_part[half] + dot_back(sums[half].astype(low), w_near[...])


def feed_run(
    spot, partner, normed_table, down_table, w_up, b_up, w_down, out_up, out_down,
    bias, send_up, send_down, near_up, near_down, sends, arrives, last_sends, last_arrives,
):
    span = w_up.shape[1] // out_up.shape[0]
    half = out_up.shape[0] // 2
    core = spot.core
    width = w_up.shape[0]
    rows = math.prod(normed_table.shape) // width
    bias[...] = as_row(b_up)

    def piece(place):
        normed = normed_table[...].reshape(rows, width)
        down = down_table[...].reshape(rows, width)
        lanes = pl.ds(pl.multiple_of(place * span, span), span)
        act, slope = gelu_pair(dot(normed, w_up[:, lanes]) + bias[:, lanes])
        up = (slope * dot_back(down, w_down[lanes, :])).astype(low)
        return dot_rows(normed, up), dot_rows(act.astype(low), down)

    started = []
    for q in range(half):
        up, down = piece((1 - core) * half + q)
        send_up[q] = up.astype(low)
        send_down[q] = down.astype(low)
        pair = [
            remote(send_up.at[q], near_up.at[q], sends.at[0, q], arrives.at[0, q], partner),
            remote(send_down.at[q], near_down.at[q], sends.at[1, q], arrives.at[1, q], partner),
        ]
        start_all(pair)
        started.append(pair)
        yield
    finals = []
    for q in range(half):
        place = core * half + q
        up, down = piece(place)
        arrived(started[q])
        out_up[place] = (up + near_up[q].astype(wide)).astype(low)
        out_down[place] = (down + near_down[q].astype(wide)).astype(low)
        pair = [
            remote(out_up.at[place], out_up.at[place], last_sends.at[0, q], last_arrives.at[0, q], partner),
            remote(out_down.at[place], out_down.at[place], last_sends.at[1, q], last_arrives.at[1, q], partner),
        ]
        start_all(pair)
        finals += pair
        yield
    arrived(finals)
    all_sent(flat(started) + finals)


def feed_scratch(width, hidden, pieces):
    dma = pltpu.SemaphoreType.DMA
    span, half = hidden // pieces, pieces // 2
    return (
        [pltpu.VMEM((1, hidden), wide)]
        + [pltpu.VMEM((half, width, span), low), pltpu.VMEM((half, span, width), low)] * 2
        + [dma((2, half))] * 4
    )


def tail_kernel(
    grid, given, part, node_part, w_near, table, w_up, b_up, w_down, summed, out_nodes, out_up, out_down, *scratch
):
    spot = Spot(grid)
    partner = (1 - spot.core, lax.axis_index("res"))
    meet(spot.peers() + [partner])
    total = total_run(spot, partner, given, summed, scratch[:11])
    owner = owner_run(spot, part, node_part, w_near, out_nodes, scratch[11:20])
    feed = feed_run(spot, partner, table.at[:, :, :, 0], table.at[:, :, :, 1], w_up, b_up, w_down, out_up, out_down, *scratch[20:])
    runs = [owner, total, feed]
    while runs:
        for run in list(runs):
            if next(run, runs) is runs:
                runs.remove(run)


vmem = pl.BlockSpec(memory_space=pltpu.VMEM)
far = pl.BlockSpec(memory_space=pl.ANY)
most_vmem = 67_000_000


def params(collective=None, **more):
    if collective is None:
        return pltpu.CompilerParams(vmem_limit_bytes=most_vmem, **more)
    return pltpu.CompilerParams(
        collective_id=collective, has_side_effects=True, vmem_limit_bytes=most_vmem, **more
    )


def gather_table(grid, rows, collective):
    count, width = rows.shape
    table = pl.pallas_call(
        functools.partial(table_kernel, grid),
        out_shape=jax.ShapeDtypeStruct(grid + (2, count // 2, width), low),
        in_specs=[vmem],
        out_specs=vmem,
        scratch_shapes=gather_sems(grid) + [pltpu.SemaphoreType.DMA],
        compiler_params=params(collective),
        name="gather_table_%d" % width,
    )(rows.reshape(2, count // 2, width))
    return table.reshape(-1, width)


def held(array):
    return pl.BlockSpec(array.shape, lambda step, dims=len(array.shape): (0,) * dims, pipeline_mode=pl.Buffered(1))


def streamed(array, slots):
    return pl.BlockSpec((slots,) + array.shape[1:], lambda step, dims=len(array.shape): (step,) + (0,) * (dims - 1))


def call(kernel, name, steps, slots, inputs, outputs, scratch, collective=None):
    def spec(item, flow):
        return streamed(item, slots if item.shape[0] != steps else 1) if flow else held(item)
    return pl.pallas_call(
        kernel,
        grid=(steps,),
        in_specs=[spec(item, flow) for item, flow in inputs],
        out_specs=[spec(item, flow) for item, flow in outputs],
        out_shape=[item for item, _ in outputs],
        scratch_shapes=scratch,
        compiler_params=params(collective),
        name=name,
    )(*[item for item, _ in inputs])


def per_device(
    node_states, edge_states, neighbours, residue_mask, neighbour_count,
    message_in, message_in_bias, message_mid, message_mid_bias, message_out, message_out_bias,
    node_gain, node_shift, feed_up, feed_up_bias, feed_down, feed_down_bias, final_gain, final_shift,
    edge_in, edge_in_bias, edge_mid, edge_mid_bias, edge_out, edge_out_bias, edge_gain, edge_shift,
    node_cotangent, edge_cotangent,
):
    grid = chip_grid(lax.axis_size("res"))
    nodes = node_states[0]
    count, width = nodes.shape
    edges = jnp.transpose(edge_states[0], (1, 0, 2))
    edge_ct = jnp.transpose(edge_cotangent[0], (1, 0, 2))
    depth, _, narrow = edges.shape
    hidden = feed_up.shape[1]
    slots = 12
    steps = depth // slots
    total = grid[0] * grid[1] * grid[2] * count
    edge_in_t = jnp.transpose(edge_in)
    lanes = -(-narrow // 128) * 128
    shape = jax.ShapeDtypeStruct
    slab = shape((depth, count, width), low)
    node_low, node_wide = shape((count, width), low), shape((count, width), wide)
    scratch = pltpu.VMEM

    square = shape((narrow, narrow), wide)
    if total <= 1024:
        places = line_places(width, hidden)
        blocks = (2,) + grid + (2, 16, width)
        each = math.prod(blocks[:-1])
        cut = sum_pieces(width, narrow, each)
        pieces = hidden // 256
        near_index = jnp.transpose(neighbours, (2, 0, 1))
        half_rows = (2, count // 2, width)
        lane_rows = (2, count // 2, lanes)
        dma = pltpu.SemaphoreType.DMA
        whole, few = shape(blocks, low), shape(blocks[:-1] + (width // 2,), low)
        near = [
            near_index, neighbour_count, residue_mask, nodes.reshape(half_rows), message_in_bias, message_mid_bias,
            message_out_bias, node_gain, node_shift, feed_up_bias, feed_down_bias, final_gain, final_shift,
            edge_in_bias, edge_mid, edge_mid_bias, edge_out, edge_out_bias, edge_gain, edge_shift, node_cotangent[0],
        ]
        distant = [edges, edge_ct, message_in, message_mid, message_out, feed_up, feed_down, edge_in_t]
        strip = scratch((count, narrow), wide)
        (node_out, edge_result, edge_total, grad_nodes, *totals, up_low, down_low) = pl.pallas_call(
            functools.partial(whole_kernel, grid, slots, cut, places),
            out_shape=[node_low, shape(edges.shape, low), shape(edges.shape, low), shape(half_rows, wide),
                       few, few, whole, whole,
                       shape((pieces, width, hidden // pieces), low), shape((pieces, hidden // pieces, width), low)],
            in_specs=[vmem] * len(near) + [far] * len(distant),
            out_specs=[vmem, far, far] + [vmem] * 7,
            scratch_shapes=[scratch(a.shape, low) for a in distant] + [dma((8,)), dma((steps + 2,)), scratch((count, depth), jnp.int32), scratch((steps, 1, slots * count), jnp.int32)]
            + [scratch(slab.shape, low)] * 3
            + [scratch(edges.shape, low), scratch(grid + half_rows, low),
               scratch((count, width), wide), scratch((count, width), wide), scratch((count, hidden), wide),
               scratch(grid + lane_rows, low), strip, scratch((total, narrow), wide), scratch(grid + lane_rows, low),
               strip] + [scratch(square.shape, wide)] * 3 + [scratch((8, narrow), wide)]
            + [scratch((total, width), wide), scratch(grid + half_rows, low),
               scratch((count, width), wide), scratch((8, width), wide), scratch((width, width), wide),
               scratch((narrow, width), wide), scratch((16, width), wide), scratch(half_rows, wide),
               scratch(grid + half_rows, low), scratch(grid + half_rows, low)]
            + [scratch(a.shape, low) for a in (few, few, whole, whole)]
            + gather_sems(grid) * 4
            + scatter_scratch(grid, count // 2, lanes) + scatter_scratch(grid, count // 2, width)
            + feed_scratch(width, hidden, pieces) + total_scratch(grid, 16, width // 2) * 2
            + total_scratch(grid, 16, width) * 2,
            compiler_params=params(0), name="whole",
        )(*near, *distant)
        vector, line = shape((width,), wide), shape((narrow,), wide)
        sources = [each_total.reshape(each, -1) for each_total in totals] + [up_low, down_low, edge_total, edge_result]
        kinds = [message_in.shape, vector, message_mid.shape, vector, message_out.shape, vector, vector, vector,
                 feed_up.shape, shape((hidden,), wide), feed_down.shape, vector, vector, vector, edge_in_t.shape, line,
                 square, line, square, line, line, line, edges.shape]
        staged = [kind for kind in kinds if isinstance(kind, tuple)]
        node_out, grad_nodes, *grads, edge_grad, edge_result = pl.pallas_call(
            functools.partial(unpack, cut, places),
            out_shape=[node_low, node_wide] + [shape(kind, wide) if isinstance(kind, tuple) else kind for kind in kinds] + [shape(edges.shape, low)],
            in_specs=[vmem] * 2 + [far] * 8, out_specs=[vmem] * 2 + [far if isinstance(kind, tuple) else vmem for kind in kinds] + [far],
            scratch_shapes=[scratch(a.shape, low) for a in sources] + [scratch(kind, wide) for kind in staged]
            + [dma((8,)), dma((32,))],
            compiler_params=params(), name="unpack",
        )(node_out, grad_nodes, *sources)
    else:
        index = neighbours[0]
        rows = jnp.transpose(index).reshape(steps, 1, slots * count)
        table = gather_table(grid, nodes, 0)
        (slope_one, slope_two, act_one, mixed_low, resid, second_sum, up_slope, node_out, sent, own_edge) = call(
            functools.partial(message_forward, slots), "message_forward", steps, slots,
            [(index, False), (neighbour_count, False), (residue_mask, False), (nodes, False), (table, False), (edges, True)]
            + [(a, False) for a in (
                message_in, message_in_bias, message_mid, message_mid_bias, message_out, message_out_bias,
                node_gain, node_shift, feed_up, feed_up_bias, feed_down, feed_down_bias, final_gain, final_shift,
                edge_in_t, edge_in_bias)],
            [(slab, True)] * 3 + [(node_low, False), (node_wide, False), (node_wide, False),
             (shape((count, hidden), wide), False), (node_low, False),
             (shape((count, lanes), low), False), (shape((count, narrow), wide), False)],
            [scratch((total, width), low), scratch((count, width), wide), scratch((count, width), wide)],
        )
        sent_table = gather_table(grid, sent, 1)
        (edge_result, partial, spread_two, own_edge_grad, e_in, e_mid, e_out, e_vectors) = call(
            functools.partial(edge_pass, slots), "edge_pass", steps, slots,
            [(index, False), (rows, True), (sent_table, False), (own_edge, False), (edges, True), (edge_ct, True)]
            + [(a, False) for a in (edge_in_t, edge_mid, edge_mid_bias, edge_out, edge_out_bias, edge_gain, edge_shift)],
            [(shape(edges.shape, low), True), (shape(edges.shape, low), True), (shape((total, lanes), low), False),
             (shape((count, narrow), wide), False), (square, False), (square, False), (square, False),
             (shape((8, narrow), wide), False)],
            [scratch((total, narrow), wide)],
        )
        back_edge = pl.pallas_call(
            functools.partial(owner_kernel, grid),
            out_shape=shape((2, count // 2, lanes), wide),
            in_specs=[vmem], out_specs=vmem,
            scratch_shapes=scatter_scratch(grid, count // 2, lanes),
            compiler_params=params(2), name="edge_owner",
        )(spread_two.reshape(grid + (2, count // 2, lanes))).reshape(count, lanes)[:, :narrow]
        shares = 4 * grid[0] * grid[1] * grid[2] * 16
        layout = lay_out_rows(width, narrow, hidden, shares)
        table_blocks = grid + (2, count, width)
        (edge_grad, spread, node_part, packed, feed_table) = call(
            functools.partial(node_backward, grid, slots, layout), "node_backward", steps, slots,
            [(rows, True), (neighbour_count, False), (residue_mask, False), (nodes, False), (table, False), (edges, True),
             (slope_one, True), (slope_two, True), (act_one, True), (partial, True)]
            + [(a, False) for a in (
                mixed_low, resid, second_sum, up_slope, node_out, node_cotangent[0], back_edge, own_edge_grad,
                e_in, e_mid, e_out, e_vectors, message_in, message_mid, message_out, node_gain, node_shift,
                feed_up, feed_down, final_gain, edge_in_t)],
            [(shape(edges.shape, wide), True), (shape((total, width), low), False), (node_wide, False),
             (shape((layout["rows"], width), low), False), (shape(table_blocks, low), False)],
            [scratch((count, width), wide), scratch((total, width), wide), scratch((count, width), wide),
             scratch((width, width), wide), scratch((narrow, width), wide), scratch((1, width), wide),
             scratch((32, width), wide), scratch(table_blocks, low)] + gather_sems(grid),
            collective=3,
        )
        chunk = layout["rows"] // (4 * grid[0] * grid[1] * grid[2])
        blocks = (2,) + grid + (2, chunk, width)
        pieces = hidden // 256
        (summed, grad_nodes, up_low, down_low) = pl.pallas_call(
            functools.partial(tail_kernel, grid),
            out_shape=[shape(blocks, low), shape((2, count // 2, width), wide),
                       shape((pieces, width, hidden // pieces), low), shape((pieces, hidden // pieces, width), low)],
            in_specs=[vmem] * 8, out_specs=[vmem] * 4,
            scratch_shapes=total_scratch(grid, chunk, width) + scatter_scratch(grid, count // 2, width)
            + feed_scratch(width, hidden, pieces),
            compiler_params=params(4), name="tail",
        )(packed.reshape(blocks), spread.reshape(grid + (2, count // 2, width)), node_part.reshape(2, count // 2, width),
          message_in[width : 2 * width], feed_table, feed_up, feed_up_bias, feed_down)
        grad_nodes = grad_nodes.reshape(count, width)
        vector, line = shape((width,), wide), shape((narrow,), wide)
        grads = pl.pallas_call(
            functools.partial(unpack_rows, layout),
            out_shape=[
                shape(message_in.shape, wide), vector, shape(message_mid.shape, wide), vector,
                shape(message_out.shape, wide), vector, vector, vector, shape(feed_up.shape, wide), shape((hidden,), wide),
                shape(feed_down.shape, wide), vector, vector, vector, shape(edge_in_t.shape, wide), line,
                square, line, square, line, line, line,
            ],
            in_specs=[vmem] * 3, out_specs=[vmem] * 22,
            compiler_params=params(), name="unpack",
        )(summed.reshape(layout["rows"], width), up_low, down_low)
    grads = list(grads)
    grads[14] = jnp.transpose(grads[14])
    back = (1, 0, 2)
    return (
        node_out[None],
        jnp.transpose(edge_result, back)[None],
        grad_nodes[None],
        jnp.transpose(edge_grad, back)[None],
        *grads,
    )


def solution(mesh):
    split, whole = P("batch", "res"), P()
    in_specs = (split,) * 5 + (whole,) * 22 + (split,) * 2
    out_specs = (split,) * 4 + (whole,) * 22
    return jax.shard_map(per_device, mesh=mesh, in_specs=in_specs, out_specs=out_specs, check_vma=False)
```

```python
import functools
import math
import jax
import jax.numpy as jnp
from jax import lax
from jax.experimental import pallas as pl
from jax.experimental.pallas import tpu as pltpu
from jax.sharding import PartitionSpec as P

MESH = pl.DeviceIdType.MESH
low = jnp.bfloat16
FEED_BEAT = 2
wide = jnp.float32


def chip_grid(count):
    side_x = 2 if count < 64 else 4
    side_y = side_x
    return (count // (side_x * side_y), side_y, side_x)


def flip(place, step):
    bit = 1
    while bit <= step:
        if step & bit:
            place = place + bit - 2 * bit * ((place // bit) % 2)
        bit *= 2
    return place


class Spot:
    def __init__(self, grid):
        self.grid = grid
        side_z, side_y, side_x = grid
        me = lax.axis_index("res")
        self.core = lax.axis_index("batch")
        self.z = me // (side_y * side_x)
        self.y = (me // side_x) % side_y
        self.x = me % side_x

    def device(self, z, y, x):
        return (self.core, (z * self.grid[1] + y) * self.grid[2] + x)

    def far_z(self, step):
        return flip(self.z, step)

    def far_y(self, step):
        return flip(self.y, step)

    def far_x(self, step):
        return flip(self.x, step)

    def peers(self):
        found = [self.device(self.far_z(s), self.y, self.x) for s in range(1, self.grid[0])]
        found += [self.device(self.z, self.far_y(s), self.x) for s in range(1, self.grid[1])]
        found += [self.device(self.z, self.y, self.far_x(s)) for s in range(1, self.grid[2])]
        return found


def greet(peers):
    barrier = pltpu.get_barrier_semaphore()
    for peer in peers:
        pl.semaphore_signal(barrier, inc=1, device_id=peer, device_id_type=MESH)


def met(peers):
    pl.semaphore_wait(pltpu.get_barrier_semaphore(), len(peers))


def meet(peers):
    greet(peers)
    met(peers)


def remote(source, target, send, arrive, device):
    return pltpu.make_async_remote_copy(
        src_ref=source, dst_ref=target, send_sem=send, recv_sem=arrive,
        device_id=device, device_id_type=MESH,
    )


def gather_sems(grid):
    side_z, side_y, side_x = grid
    dma = pltpu.SemaphoreType.DMA
    shapes = [(side_z - 1,), (side_z, side_x - 1), (side_z, side_y - 1), (side_z, side_y - 1), (side_z, side_x - 1)]
    return [dma(s) for s in shapes for _ in range(2)]


def gather_plan(spot, table, sems):
    (s1, r1, s2a, r2a, s2b, r2b, s3a, r3a, s3b, r3b) = sems
    side_z, side_y, side_x = spot.grid
    z, y, x = spot.z, spot.y, spot.x

    def push(view, send, arrive, device):
        return remote(view, view, send, arrive, device)

    ups = [
        push(table.at[z, y, x], s1.at[s - 1], r1.at[s - 1], spot.device(spot.far_z(s), y, x))
        for s in range(1, side_z)
    ]
    firsts, lasts = [], []
    for j in range(side_z):
        zj = flip(z, j)
        firsts.append(
            [
                push(table.at[zj, y, x, 0], s2a.at[j, s - 1], r2a.at[j, s - 1], spot.device(z, y, spot.far_x(s)))
                for s in range(1, side_x)
            ]
            + [
                push(table.at[zj, y, x, 1], s2b.at[j, s - 1], r2b.at[j, s - 1], spot.device(z, spot.far_y(s), x))
                for s in range(1, side_y)
            ]
        )
        lasts.append(
            [
                push(table.at[zj, y, :, 0], s3a.at[j, s - 1], r3a.at[j, s - 1], spot.device(z, spot.far_y(s), x))
                for s in range(1, side_y)
            ]
            + [
                push(table.at[zj, :, x, 1], s3b.at[j, s - 1], r3b.at[j, s - 1], spot.device(z, y, spot.far_x(s)))
                for s in range(1, side_x)
            ]
        )
    return ups, firsts, lasts


def start_all(copies):
    for copy in copies:
        copy.start()


def arrived(copies):
    for copy in copies:
        copy.wait_recv()


def all_sent(copies):
    for copy in copies:
        copy.wait_send()


def flat(groups):
    return [copy for group in groups for copy in group]


def gather_run(plan):
    ups, firsts, lasts = plan
    count = len(lasts)
    start_all(ups + firsts[0])
    yield
    for j in range(1, count):
        arrived([ups[j - 1]])
        start_all(firsts[j])
        arrived(firsts[j - 1])
        start_all(lasts[j - 1])
        if j + 1 < count:
            yield
    arrived(firsts[count - 1])
    start_all(lasts[count - 1])
    yield
    for j in range(count):
        arrived(lasts[j])
    yield
    all_sent(ups + flat(firsts) + flat(lasts))


def drive(run):
    for _ in run:
        pass


def scatter_scratch(grid, rows, width):
    side_z, side_y, side_x = grid
    return [
        pltpu.VMEM((side_z, side_y - 1, side_x, rows, width), low),
        pltpu.VMEM((side_z, side_x - 1, side_y, rows, width), low),
        pltpu.VMEM((side_z, side_x - 1, rows, width), low),
        pltpu.VMEM((side_z, side_y - 1, rows, width), low),
        pltpu.VMEM((side_z - 1, 2, rows, width), low),
        pltpu.VMEM((side_z, side_x, rows, width), low),
        pltpu.VMEM((side_z, side_y, rows, width), low),
        pltpu.VMEM((side_z, 2, rows, width), low),
        pltpu.SemaphoreType.DMA((2, 5)),
    ]


def wait_bytes(like, sem):
    pltpu.make_async_copy(like, like, sem).wait()


def scatter_run(spot, part, scratch, result, before=None):
    (ra1, rb1, ra2, rb2, r3, ka, kb, tot, sems) = scratch
    places = (ra1, rb1, ra2, rb2, r3)
    side_z, side_y, side_x = spot.grid
    z, y, x = spot.z, spot.y, spot.x

    def go(source, target, kind, device):
        remote(source, target, sems.at[0, kind], sems.at[1, kind], device).start()

    def come(kind):
        wait_bytes(places[kind], sems.at[1, kind])

    order = range(side_z - 1, -1, -1)
    if before is not None:
        before()
    for j in order:
        zj = flip(z, j)
        for s in range(1, side_y):
            go(part.at[zj, spot.far_y(s), :, 0], ra1.at[j, s - 1], 0, spot.device(z, spot.far_y(s), x))
        for s in range(1, side_x):
            go(part.at[zj, :, spot.far_x(s), 1], rb1.at[j, s - 1], 1, spot.device(z, y, spot.far_x(s)))
    yield
    come(0)
    for j in order:
        total = part[flip(z, j), y, :, 0].astype(wide)
        for s in range(side_y - 1):
            total = total + ra1[j, s].astype(wide)
        ka[j] = total.astype(low)
        for s in range(1, side_x):
            go(ka.at[j, spot.far_x(s)], ra2.at[j, s - 1], 2, spot.device(z, y, spot.far_x(s)))
    come(1)
    for j in order:
        total = part[flip(z, j), :, x, 1].astype(wide)
        for s in range(side_x - 1):
            total = total + rb1[j, s].astype(wide)
        kb[j] = total.astype(low)
        for s in range(1, side_y):
            go(kb.at[j, spot.far_y(s)], rb2.at[j, s - 1], 3, spot.device(z, spot.far_y(s), x))
    yield
    come(2)
    come(3)
    for j in order:
        upper = ka[j, x].astype(wide)
        for s in range(side_x - 1):
            upper = upper + ra2[j, s].astype(wide)
        lower = kb[j, y].astype(wide)
        for s in range(side_y - 1):
            lower = lower + rb2[j, s].astype(wide)
        if j:
            tot[j, 0] = upper.astype(low)
            tot[j, 1] = lower.astype(low)
            go(tot.at[j], r3.at[j - 1], 4, spot.device(flip(z, j), y, x))
    yield
    come(4)
    for s in range(side_z - 1):
        upper = upper + r3[s, 0].astype(wide)
        lower = lower + r3[s, 1].astype(wide)
    result += [upper, lower]
    for kind, like in enumerate(places):
        wait_bytes(like, sems.at[0, kind])
eps_norm = 1e-05
root_half = 0.7071067811865476
turn_scale = 0.5641895835477563
minus_log2e = -1.4426950408889634


def dot(left, right):
    return jnp.dot(left, right, preferred_element_type=wide)


def dot_back(left, right):
    return lax.dot_general(left, right, (((1,), (1,)), ((), ())), preferred_element_type=wide)


def dot_rows(left, right):
    return lax.dot_general(left, right, (((0,), (0,)), ((), ())), preferred_element_type=wide)


def gelu_pair(values):
    scaled = values * root_half
    share = 0.5 + 0.5 * lax.erf(scaled)
    slope = share + scaled * turn_scale * jnp.exp2(scaled * scaled * minus_log2e)
    return values * share, slope


def norm_stats(values):
    centre = jnp.mean(values, axis=-1, keepdims=True)
    centred = values - centre
    variance = jnp.mean(centred * centred, axis=-1, keepdims=True)
    scale = lax.rsqrt(variance + eps_norm)
    return centred * scale, scale


def norm_back(hat, scale, gain, grad):
    inner = grad * gain
    return scale * (
        inner
        - jnp.mean(inner, axis=-1, keepdims=True)
        - hat * jnp.mean(inner * hat, axis=-1, keepdims=True)
    )


def as_row(ref, start=None, size=None):
    return ref[...].astype(wide).reshape(1, ref.shape[0])


def as_column(row, count):
    rows = lax.broadcasted_iota(jnp.int32, (count, count), 0)
    lanes = lax.broadcasted_iota(jnp.int32, (count, count), 1)
    return jnp.sum(jnp.where(rows == lanes, jnp.broadcast_to(row, (count, count)), 0), axis=1, keepdims=True)


def slot_column(index, slot):
    lanes = lax.broadcasted_iota(jnp.int32, index.shape, 1)
    return jnp.sum(jnp.where(lanes == slot, index, 0), axis=1, keepdims=True)


def pick_rows(index, first, slots, total):
    count = index.shape[0]
    lanes = lax.broadcasted_iota(jnp.int16, (count, total), 1)
    one, none = jnp.ones((), low), jnp.zeros((), low)
    return jnp.concatenate(
        [
            jnp.where(jnp.broadcast_to(slot_column(index, first + s), (count, total)).astype(jnp.int16) == lanes, one, none)
            for s in range(slots)
        ],
        axis=0,
    )


def pick_columns(row, total):
    rows = lax.broadcasted_iota(jnp.int16, (total, row.shape[1]), 0)
    one, none = jnp.ones((), low), jnp.zeros((), low)
    return jnp.where(rows == jnp.broadcast_to(row.astype(jnp.int16), rows.shape), one, none)


def message_forward(
    slots, index, counts, masks, nodes, table, edges, w_in, b_in, w_mid, b_mid, w_out, b_out,
    gain_one, shift_one, w_up, b_up, w_down, b_down, gain_two, shift_two, w_edge, b_edge,
    slope_one, slope_two, act_one, mixed_low, resid, second_sum, up_slope, node_out, sent, own_edge,
    projected, own, pooled,
):
    step = pl.program_id(0)
    count, width = nodes.shape
    total = table.shape[0]
    live = as_column(counts[...], count)

    @pl.when(step == 0)
    def _():
        projected[...] = dot(table[...], w_in[width : 2 * width]).astype(low)
        own[...] = dot(nodes[...], w_in[0:width]) + as_row(b_in)
        pooled[...] = jnp.zeros_like(pooled)

    picks = pick_rows(index[...], step * slots, slots, total)
    edge_rows = edges[...].reshape(slots * count, edges.shape[2])
    pre = dot(picks, projected[...]) + dot(edge_rows, w_in[2 * width :])
    pre = pre.reshape(slots, count, width) + own[...][None]
    act, slope = gelu_pair(pre)
    act = act.astype(low)
    act_one[...] = act
    slope_one[...] = slope.astype(low)
    pre = dot(act.reshape(slots * count, width), w_mid[...]) + as_row(b_mid)
    act, slope = gelu_pair(pre)
    act = act.reshape(slots, count, width)
    slope_two[...] = slope.astype(low).reshape(slots, count, width)
    gathered = pooled[...]
    for s in range(slots):
        gathered = gathered + jnp.where(live > step * slots + s, act[s], 0.0)
    pooled[...] = gathered

    @pl.when(step == pl.num_programs(0) - 1)
    def _():
        mean = pooled[...] / jnp.maximum(live, 1).astype(wide)
        mean_low = mean.astype(low)
        mixed_low[...] = mean_low
        some = jnp.where(live > 0, 1.0, 0.0)
        mask = as_column(masks[...], count).astype(wide)
        aggregate = dot(mean_low, w_out[...]) + some * as_row(b_out)
        total_sum = nodes[...].astype(wide) + mask * aggregate
        resid[...] = total_sum
        hat, _ = norm_stats(total_sum)
        first = hat * as_row(gain_one) + as_row(shift_one)
        up = dot(first.astype(low), w_up[...]) + as_row(b_up)
        act_up, slope_up = gelu_pair(up)
        act_up = act_up.astype(low)
        up_slope[...] = slope_up
        summed = first + dot(act_up, w_down[...]) + as_row(b_down)
        second_sum[...] = summed
        hat, _ = norm_stats(summed)
        out = (hat * as_row(gain_two) + as_row(shift_two)).astype(low)
        node_out[...] = out
        pad = jnp.zeros((count, sent.shape[1] - w_edge.shape[0]), low)
        sent[...] = jnp.concatenate([dot_back(out, w_edge[:, width : 2 * width]).astype(low), pad], axis=1)
        own_edge[...] = dot_back(out, w_edge[:, 0:width]) + as_row(b_edge)


def edge_pass(
    slots, index, rows, table, own_edge, edges, cotangent, w_edge, w_mid, b_mid, w_out, b_out, gain, shift,
    result, partial, spread, own_grad, g_in, g_mid, g_out, vectors, spread_sum,
):
    step = pl.program_id(0)
    count, width = own_edge.shape
    total = table.shape[0]
    base = w_edge.shape[1] - width

    @pl.when(step == 0)
    def _():
        spread_sum[...] = jnp.zeros_like(spread_sum)
        for ref in (own_grad, g_in, g_mid, g_out, vectors):
            ref[...] = jnp.zeros_like(ref)

    w_here = w_edge[:, base:]
    picks = pick_rows(index[...], step * slots, slots, total)
    edge_rows = edges[...].reshape(slots * count, width)
    pre = dot(picks, table[...])[:, 0:width] + dot_back(edge_rows, w_here)
    pre = (pre.reshape(slots, count, width) + own_edge[...][None]).reshape(slots * count, width)
    act_one, slope_one = gelu_pair(pre)
    act_one = act_one.astype(low)
    pre = dot(act_one, w_mid[...]) + as_row(b_mid)
    act_two, slope_two = gelu_pair(pre)
    act_two = act_two.astype(low)
    pre = dot(act_two, w_out[...]) + as_row(b_out)
    hat, scale = norm_stats(edge_rows.astype(wide) + pre)
    gain_row = as_row(gain)
    result[...] = (hat * gain_row + as_row(shift)).astype(low).reshape(slots, count, width)
    grad = cotangent[...].reshape(slots * count, width).astype(wide)
    sum_grad = norm_back(hat, scale, gain_row, grad)
    three = sum_grad.astype(low)
    g_out[...] += dot_rows(act_two, three)
    two = (slope_two * dot_back(three, w_out[...])).astype(low)
    g_mid[...] += dot_rows(act_one, two)
    one = (slope_one * dot_back(two, w_mid[...])).astype(low)
    g_in[...] += dot_rows(one, edge_rows)
    vectors[...] += jnp.concatenate(
        [
            jnp.sum(piece, axis=0, keepdims=True)
            for piece in (grad * hat, grad, three.astype(wide), two.astype(wide), one.astype(wide))
        ]
        + [jnp.zeros((3, width), wide)],
        axis=0,
    )
    own_grad[...] += jnp.sum(one.astype(wide).reshape(slots, count, width), axis=0)
    partial[...] = (sum_grad + dot(one, w_here)).astype(low).reshape(slots, count, width)
    spread_sum[...] += dot(pick_columns(rows[0], total), one)

    @pl.when(step == pl.num_programs(0) - 1)
    def _():
        pad = jnp.zeros((total, spread.shape[1] - width), low)
        spread[...] = jnp.concatenate([spread_sum[...].astype(low), pad], axis=1)


def node_backward(
    grid, slots, layout, rows, counts, masks, nodes, table, edges, slope_one, slope_two, act_one, partial,
    mixed_low, resid, second_sum, up_slope, node_out, cotangent, back_edge, own_edge_grad,
    e_in, e_mid, e_out, e_vectors,
    w_in, w_mid, w_out, gain_one, shift_one, w_up, w_down, gain_two, w_edge,
    edge_grad, spread, node_part, packed, feed_table,
    level, spread_sum, own_sum, g_mid, g_edge, bias_mid, lines, held_table, *sems,
):
    step = pl.program_id(0)
    last = pl.num_programs(0) - 1
    spot = Spot(grid)
    peers = spot.peers()
    ups, firsts, lasts = gather_plan(spot, held_table, sems)
    count, width = nodes.shape
    total = table.shape[0]
    narrow = w_edge.shape[0]
    hidden = w_up.shape[1]
    live = as_column(counts[...], count)

    def put(name, value):
        row = layout[name]
        packed[row : row + value.shape[0], :] = value.astype(low)

    def put_line(name, value):
        row = layout[name]
        lines[row : row + value.shape[0], 0 : value.shape[1]] = value

    @pl.when(step == 0)
    def _():
        greet(peers)
        for ref in (spread_sum, own_sum, g_mid, g_edge, bias_mid, lines):
            ref[...] = jnp.zeros_like(ref)
        out = node_out[...]
        own_low = own_edge_grad[...].astype(low)
        back_low = back_edge[...].astype(low)
        put("edge_own", dot_rows(own_low, out))
        put("edge_near", dot_rows(back_low, out))
        pad = jnp.zeros((narrow, width // 2 - narrow), wide)
        put("edge_a", jnp.concatenate([e_in[...], pad, e_mid[...], pad], axis=1))
        put("edge_b", jnp.concatenate([e_out[...], pad, jnp.zeros((narrow, width // 2), wide)], axis=1))
        put_line("e_vectors", e_vectors[...])
        grad = (
            cotangent[...].astype(wide)
            + dot(own_low, w_edge[:, 0:width])
            + dot(back_low, w_edge[:, width : 2 * width])
        )
        hat, scale = norm_stats(second_sum[...])
        put_line("v_final_gain", jnp.sum(grad * hat, axis=0, keepdims=True))
        put_line("v_final_shift", jnp.sum(grad, axis=0, keepdims=True))
        second = norm_back(hat, scale, as_row(gain_two), grad)
        down = second.astype(low)
        put_line("v_down", jnp.sum(down.astype(wide), axis=0, keepdims=True))
        held_table[spot.z, spot.y, spot.x, 1] = down
        up = (up_slope[...] * dot_back(down, w_down[...])).astype(low)
        bias_up = jnp.sum(up.astype(wide), axis=0, keepdims=True)
        hat, scale = norm_stats(resid[...])
        normed = (hat * as_row(gain_one) + as_row(shift_one)).astype(low)
        held_table[spot.z, spot.y, spot.x, 0] = normed
        met(peers)
        start_all(ups + firsts[0])
        for piece in range(hidden // width):
            lines[layout["v_up"] + piece : layout["v_up"] + piece + 1, :] = bias_up[:, piece * width : (piece + 1) * width]
        first = second + dot_back(up, w_up[...])
        put_line("v_node_gain", jnp.sum(first * hat, axis=0, keepdims=True))
        put_line("v_node_shift", jnp.sum(first, axis=0, keepdims=True))
        mixed = norm_back(hat, scale, as_row(gain_one), first)
        node_part[...] = mixed
        masked = as_column(masks[...], count).astype(wide) * mixed
        put_line("v_out", jnp.sum(jnp.where(live > 0, masked, 0.0), axis=0, keepdims=True))
        put("message_out", dot_rows(mixed_low[...], masked.astype(low)))
        shared = (masked / jnp.maximum(live, 1).astype(wide)).astype(low)
        level[...] = dot_back(shared, w_out[...])

    @pl.when(step == 1)
    def _():
        for j in range(1, len(firsts)):
            arrived([ups[j - 1]])
            start_all(firsts[j])

    @pl.when(step == 2)
    def _():
        for j in range(len(lasts)):
            arrived(firsts[j])
            start_all(lasts[j])

    lift = level[...]
    slope = slope_two[...].astype(wide)
    mid = jnp.concatenate(
        [jnp.where(live > step * slots + s, slope[s] * lift, 0.0).astype(low) for s in range(slots)], axis=0
    )
    flat_one = act_one[...].reshape(slots * count, width)
    g_mid[...] += dot_rows(flat_one, mid)
    bias_mid[...] += jnp.sum(mid.astype(wide), axis=0, keepdims=True)
    slope = slope_one[...].reshape(slots * count, width).astype(wide)
    inner = (slope * dot_back(mid, w_mid[...])).astype(low)
    own_sum[...] += jnp.sum(inner.astype(wide).reshape(slots, count, width), axis=0)
    edge_rows = edges[...].reshape(slots * count, narrow)
    g_edge[...] += dot_rows(edge_rows, inner)
    edge_grad[...] = partial[...].astype(wide) + dot_back(inner, w_in[2 * width :]).reshape(slots, count, narrow)
    spread_sum[...] += dot(pick_columns(rows[0], total), inner)

    @pl.when(step == pl.num_programs(0) - 1)
    def _():
        spread_low = spread_sum[...].astype(low)
        spread[...] = spread_low
        own_low = own_sum[...].astype(low)
        put("message_in", dot_rows(nodes[...], own_low))
        put("message_near", dot_rows(table[...], spread_low))
        put("message_edge", g_edge[...])
        put("message_mid", g_mid[...])
        put_line("v_mid", bias_mid[...])
        put_line("v_in", jnp.sum(own_sum[...], axis=0, keepdims=True))
        here = layout["lines"]
        tall = lines.shape[0]
        packed[here : here + tall, :] = lines[...].astype(low)
        rest = packed.shape[0] - here - tall
        if rest:
            packed[here + tall :, :] = jnp.zeros((rest, width), low)
        node_part[...] += dot_back(own_low, w_in[0:width])
        arrived(flat(lasts))
        all_sent(ups + flat(firsts) + flat(lasts))
        feed_table[...] = held_table[...]


def lay_out_rows(width, narrow, hidden, shares):
    pieces = hidden // width
    sizes = [
        ("message_in", width), ("message_near", width), ("message_edge", narrow), ("message_mid", width),
        ("message_out", width), ("edge_own", narrow),
        ("edge_near", narrow), ("edge_a", narrow), ("edge_b", narrow), ("lines", 32),
    ]
    layout, row = {}, 0
    for name, size in sizes:
        layout[name] = row
        row += size
    layout["rows"] = -(-row // shares) * shares
    layout["e_vectors"] = 0
    layout["v_up"] = 8
    singles = ("v_final_gain", "v_final_shift", "v_down", "v_node_gain", "v_node_shift", "v_out", "v_mid", "v_in")
    for place, name in enumerate(singles):
        layout[name] = 8 + pieces + place
    return layout


def unpack_rows(layout, packed, feed_up_low, feed_down_low, *outs):
    (m_in, m_in_b, m_mid, m_mid_b, m_out, m_out_b, n_gain, n_shift, f_up, f_up_b, f_down, f_down_b,
     l_gain, l_shift, e_in, e_in_b, e_mid, e_mid_b, e_out, e_out_b, e_gain, e_shift) = outs
    width = m_mid.shape[0]
    narrow = e_mid.shape[0]
    hidden = f_up.shape[1]
    half = width // 2

    def big(name, tall, lanes=slice(None)):
        return packed[layout[name] : layout[name] + tall, lanes].astype(wide)

    m_in[0:width] = big("message_in", width)
    m_in[width : 2 * width] = big("message_near", width)
    m_in[2 * width :] = big("message_edge", narrow)
    m_mid[...] = big("message_mid", width)
    m_out[...] = big("message_out", width)
    span = feed_down_low.shape[1]
    for piece in range(hidden // span):
        f_down[piece * span : (piece + 1) * span] = feed_down_low[piece].astype(wide)
        f_up[:, piece * span : (piece + 1) * span] = feed_up_low[piece].astype(wide)
    e_in[:, 0:width] = big("edge_own", narrow)
    e_in[:, width : 2 * width] = big("edge_near", narrow)
    e_in[:, 2 * width :] = big("edge_a", narrow, slice(0, narrow))
    e_mid[...] = big("edge_a", narrow, slice(half, half + narrow))
    e_out[...] = big("edge_b", narrow, slice(0, narrow))
    lines = packed[layout["lines"] : layout["lines"] + 32, :].astype(wide)

    def one(name):
        return lines[layout[name]]

    m_in_b[...] = one("v_in")
    m_mid_b[...] = one("v_mid")
    m_out_b[...] = one("v_out")
    n_gain[...] = one("v_node_gain")
    n_shift[...] = one("v_node_shift")
    l_gain[...] = one("v_final_gain")
    l_shift[...] = one("v_final_shift")
    f_down_b[...] = one("v_down")
    for piece in range(hidden // width):
        f_up_b[piece * width : (piece + 1) * width] = lines[layout["v_up"] + piece]
    for place, ref in enumerate((e_gain, e_shift, e_out_b, e_mid_b, e_in_b)):
        ref[...] = lines[place, 0:narrow]


def sum_pieces(width, narrow, cap):
    half = width // 2
    pieces = []
    row = 0
    for name, tall, lane in (
        ("edge_own", narrow, 0), ("edge_own", narrow, half), ("e_in", narrow, 0), ("e_mid", narrow, 0),
        ("e_out", narrow, 0), ("e_lines", 16, 0),
    ):
        pieces.append((name, 0, tall, lane, 0, row))
        row += tall
    pieces += [("message_out", 0, width, 0, 1, 0), ("message_out", 0, width, half, 1, width)]
    place = 0
    for name, tall in (
        ("edge_near", narrow), ("message_mid", width), ("message_own", width), ("message_near", width),
        ("message_edge", narrow), ("lines", 16),
    ):
        done = 0
        while done < tall:
            size = min(tall - done, cap - place % cap)
            pieces.append((name, done, size, 0, 2 + place // cap, place % cap))
            place += size
            done += size
    return pieces


def line_places(width, hidden):
    pieces = hidden // width
    singles = ("v_final_gain", "v_final_shift", "v_down", "v_node_gain", "v_node_shift", "v_out", "v_mid", "v_in")
    places = {name: pieces + place for place, name in enumerate(singles)}
    places["v_up"] = 0
    return places


class Sums:
    def __init__(self, pieces, groups):
        self.pieces, self.groups = pieces, groups

    def put(self, name, value):
        value = value.astype(low)
        for piece, first, tall, lane, group, row in self.pieces:
            if piece != name:
                continue
            ref = self.groups[group]
            part = value[first : first + tall, lane : lane + ref.shape[-1]]
            if part.shape[1] < ref.shape[-1]:
                part = jnp.concatenate([part, jnp.zeros((tall, ref.shape[-1] - part.shape[1]), low)], axis=1)
            for start in range(0, tall, 16):
                place, rest = [], (row + start) // 16
                for size in reversed(ref.shape[:-2]):
                    place.append(rest % size)
                    rest //= size
                ref[tuple(reversed(place))] = part[start : start + 16]


def whole_kernel(
    grid, slots, pieces, places,
    near_index, counts, masks, nodes, b_in, b_mid, b_out, gain_one, shift_one, b_up, b_down, gain_two, shift_two,
    eb_in, ew_mid, eb_mid, ew_out, eb_out, gain_three, shift_three, cotangent,
    edges_far, edge_ct_far, w_in_far, w_mid_far, w_out_far, w_up_far, w_down_far, w_edge_far,
    node_out, edge_result, edge_total, grad_nodes, total_one, total_two, total_three, total_four, out_up, out_down,
    edges, edge_ct, w_in, w_mid, w_out, w_up, w_down, w_edge, fetches, puts, index, rows,
    slope_one, slope_two, act_one, partial, table, own, pooled, up_slope, sent_table, own_edge,
    spread_edge, spread_two, own_edge_grad, e_in, e_mid, e_out, e_vectors,
    spread_sum, spread, own_sum, mid_sum, g_mid, g_edge, lines, node_part, normed_table, down_table,
    spare_narrow, spare_wide,
    *scratch,
):
    scratch = list(scratch)

    def take(size):
        taken = scratch[:size]
        del scratch[:size]
        return taken

    spot = Spot(grid)
    partner = (1 - spot.core, lax.axis_index("res"))
    peers = spot.peers() + [partner]
    greet(peers)
    _, half_count, width = nodes.shape
    count = 2 * half_count
    total = spread_sum.shape[0]
    narrow = w_edge.shape[0]
    hidden = w_up.shape[1]
    steps = rows.shape[0]
    local = pltpu.make_async_copy(nodes, table.at[spot.z, spot.y, spot.x], puts.at[steps + 1])
    local.start()
    pairs = (
        (w_in_far, w_in), (edges_far, edges), (w_mid_far, w_mid), (w_out_far, w_out), (w_up_far, w_up),
        (w_down_far, w_down), (w_edge_far, w_edge), (edge_ct_far, edge_ct),
    )
    coming = [pltpu.make_async_copy(there, near, fetches.at[place]) for place, (there, near) in enumerate(pairs)]
    start_all(coming)
    node_sems, sent_sems, normed_sems, down_sems = take(10), take(10), take(10), take(10)
    edge_scratch, node_scratch, feed_parts = take(9), take(9), take(5)
    totals = [take(11) for _ in range(4)]
    sums = Sums(pieces, (total_one, total_two, total_three, total_four))
    live = as_column(counts[...], count)
    lane = lax.broadcasted_iota(jnp.int32, (count, slots * count), 1)
    same = lane % count == lax.broadcasted_iota(jnp.int32, (count, slots * count), 0)
    fold = jnp.where(same, 1.0, 0.0).astype(low)
    ones = jnp.ones((8, slots * count), low)
    mask = as_column(masks[...], count).astype(wide)
    node_rows = nodes[...].reshape(count, width)
    local.wait()
    met(peers)
    node_gather = gather_run(gather_plan(spot, table, node_sems))
    next(node_gather)
    coming[0].wait()
    index[...] = jnp.transpose(near_index[:, 0, :])
    for step in range(steps):
        rows[step] = jnp.concatenate([near_index[step * slots + s] for s in range(slots)], axis=1)
    own[...] = dot(node_rows, w_in[0:width]) + as_row(b_in)
    pooled[...] = jnp.zeros_like(pooled)
    drive(node_gather)
    spread[...] = dot(table[...].reshape(total, width), w_in[width : 2 * width]).astype(low).reshape(spread.shape)
    for copy in coming[1:3]:
        copy.wait()

    @pl.loop(0, steps)
    def _(step):
        here = pl.ds(step * slots, slots)
        picks = pick_rows(index[...], step * slots, slots, total)
        edge_rows = edges[here].reshape(slots * count, narrow)
        pre = dot(picks, spread[...].reshape(total, width)) + dot(edge_rows, w_in[2 * width :])
        pre = pre.reshape(slots, count, width) + own[...][None]
        act, slope = gelu_pair(pre)
        act = act.astype(low)
        act_one[here] = act
        slope_one[here] = slope.astype(low)
        pre = dot(act.reshape(slots * count, width), w_mid[...]) + as_row(b_mid)
        act, slope = gelu_pair(pre)
        slope_two[here] = slope.astype(low).reshape(slots, count, width)
        valid = jnp.where(same & (live > step * slots + lane // count), 1.0, 0.0).astype(low)
        pooled[...] += dot(valid, act.astype(low))

    mixed_low = (pooled[...] / jnp.maximum(live, 1).astype(wide)).astype(low)
    some = jnp.where(live > 0, 1.0, 0.0)
    for copy in coming[3:]:
        copy.wait()
    aggregate = dot(mixed_low, w_out[...]) + some * as_row(b_out)
    hat_one, scale_one = norm_stats(node_rows.astype(wide) + mask * aggregate)
    first = hat_one * as_row(gain_one) + as_row(shift_one)
    first_low = first.astype(low)
    normed_table[spot.z, spot.y, spot.x] = first_low.reshape(normed_table.shape[3:])
    act_up, slope_up = gelu_pair(dot(first_low, w_up[...]) + as_row(b_up))
    up_slope[...] = slope_up
    second_sum = first + dot(act_up.astype(low), w_down[...]) + as_row(b_down)
    hat, _ = norm_stats(second_sum)
    out = (hat * as_row(gain_two) + as_row(shift_two)).astype(low)
    node_out[...] = out
    pad = jnp.zeros((count, sent_table.shape[-1] - narrow), low)
    sent = jnp.concatenate([dot_back(out, w_edge[:, width : 2 * width]).astype(low), pad], axis=1)
    sent_table[spot.z, spot.y, spot.x] = sent.reshape(sent_table.shape[3:])
    sent_gather = gather_run(gather_plan(spot, sent_table, sent_sems))
    next(sent_gather)
    normed_gather = gather_run(gather_plan(spot, normed_table, normed_sems))
    own_edge[...] = dot_back(out, w_edge[:, 0:width]) + as_row(eb_in)
    spread_edge[...] = jnp.zeros_like(spread_edge)
    for ref in (own_edge_grad, e_in, e_mid, e_out, e_vectors):
        ref[...] = jnp.zeros_like(ref)
    next(sent_gather)
    next(normed_gather)
    drive(sent_gather)
    w_here = w_edge[:, 2 * width :]

    @pl.loop(0, steps)
    def _(step):
        here = pl.ds(step * slots, slots)
        for beat in range(1, steps):
            @pl.when(step == beat)
            def _():
                next(normed_gather, None)

        picks = pick_rows(index[...], step * slots, slots, total)
        edge_rows = edges[here].reshape(slots * count, narrow)
        near_part = dot(picks, sent_table[...].reshape(total, sent_table.shape[-1]))[:, 0:narrow]
        pre = near_part + dot_back(edge_rows, w_here)
        pre = (pre.reshape(slots, count, narrow) + own_edge[...][None]).reshape(slots * count, narrow)
        act_a, slope_a = gelu_pair(pre)
        act_a = act_a.astype(low)
        pre = dot(act_a, ew_mid[...]) + as_row(eb_mid)
        act_b, slope_b = gelu_pair(pre)
        act_b = act_b.astype(low)
        pre = dot(act_b, ew_out[...]) + as_row(eb_out)
        hat, scale = norm_stats(edge_rows.astype(wide) + pre)
        gain_row = as_row(gain_three)
        grad_low = edge_ct[here].reshape(slots * count, narrow)
        grad = grad_low.astype(wide)
        edge_ct[here] = (hat * gain_row + as_row(shift_three)).astype(low).reshape(slots, count, narrow)
        sum_grad = norm_back(hat, scale, gain_row, grad)
        three = sum_grad.astype(low)
        e_out[...] += dot_rows(act_b, three)
        two = (slope_b * dot_back(three, ew_out[...])).astype(low)
        e_mid[...] += dot_rows(act_a, two)
        one = (slope_a * dot_back(two, ew_mid[...])).astype(low)
        e_in[...] += dot_rows(one, edge_rows)
        e_vectors[...] += jnp.concatenate(
            [
                jnp.sum(grad * hat, axis=0, keepdims=True), dot(ones, grad_low)[0:1], dot(ones, three)[0:1],
                dot(ones, two)[0:1], jnp.zeros((4, narrow), wide),
            ],
            axis=0,
        )
        own_edge_grad[...] += dot(fold, one)
        partial[here] = (sum_grad + dot(one, w_here)).astype(low).reshape(slots, count, narrow)
        spread_edge[...] += dot(pick_columns(rows[step], total), one)

    result_copy = pltpu.make_async_copy(edge_ct, edge_result, puts.at[steps])
    result_copy.start()
    pad = jnp.zeros((total, spread_two.shape[-1] - narrow), low)
    spread_two[...] = jnp.concatenate([spread_edge[...].astype(low), pad], axis=1).reshape(spread_two.shape)

    moving = []

    def launch(run):
        next(run)
        moving.append(run)

    def beat():
        for run in list(moving):
            if next(run, moving) is moving:
                moving.remove(run)

    def put_line(name, value):
        lines[places[name] : places[name] + value.shape[0], :] = value

    back = []
    edge_run = scatter_run(spot, spread_two, edge_scratch, back)
    next(edge_run)
    own_low = own_edge_grad[...].astype(low)
    sums.put("edge_own", dot_rows(own_low, out))
    sums.put("e_in", e_in[...])
    sums.put("e_mid", e_mid[...])
    sums.put("e_out", e_out[...])
    sums.put("e_lines", jnp.concatenate(
        [e_vectors[0:4], jnp.sum(own_edge_grad[...], axis=0, keepdims=True), jnp.zeros((11, narrow), wide)], axis=0
    ))
    gathers = [normed_gather, gather_run(gather_plan(spot, down_table, down_sems))]
    moving.append(normed_gather)
    launch(total_run(spot, partner, total_one, total_one, totals[0], spare_narrow))
    lines[...] = jnp.zeros_like(lines)
    grad = cotangent[...].astype(wide) + dot(own_low, w_edge[:, 0:width])
    hat, scale = norm_stats(second_sum)
    drive(edge_run)

    back_low = jnp.concatenate(back, axis=0)[:, 0:narrow].astype(low)
    grad = grad + dot(back_low, w_edge[:, width : 2 * width])
    put_line("v_final_gain", jnp.sum(grad * hat, axis=0, keepdims=True))
    put_line("v_final_shift", jnp.sum(grad, axis=0, keepdims=True))
    second = norm_back(hat, scale, as_row(gain_two), grad)
    down = second.astype(low)
    down_table[spot.z, spot.y, spot.x] = down.reshape(down_table.shape[3:])
    launch(gathers[1])
    put_line("v_down", jnp.sum(down.astype(wide), axis=0, keepdims=True))
    sums.put("edge_near", dot_rows(back_low, out))
    up = (up_slope[...] * dot_back(down, w_down[...])).astype(low)
    bias_up = jnp.sum(up.astype(wide), axis=0, keepdims=True)
    for piece in range(hidden // width):
        lines[piece : piece + 1, :] = bias_up[:, piece * width : (piece + 1) * width]
    first = second + dot_back(up, w_up[...])
    put_line("v_node_gain", jnp.sum(first * hat_one, axis=0, keepdims=True))
    put_line("v_node_shift", jnp.sum(first, axis=0, keepdims=True))
    mixed = norm_back(hat_one, scale_one, as_row(gain_one), first)
    masked = mask * mixed
    put_line("v_out", jnp.sum(jnp.where(live > 0, masked, 0.0), axis=0, keepdims=True))
    sums.put("message_out", dot_rows(mixed_low, masked.astype(low)))
    shared = (masked / jnp.maximum(live, 1).astype(wide)).astype(low)
    lift = dot_back(shared, w_out[...])

    beat()
    launch(total_run(spot, partner, total_two, total_two, totals[1], spare_narrow))

    own_sum[...] = jnp.zeros_like(own_sum)
    mid_sum[...] = jnp.zeros_like(mid_sum)
    g_mid[...] = jnp.zeros_like(g_mid)

    @pl.loop(0, steps)
    def _(step):
        here = pl.ds(step * slots, slots)
        slope = slope_two[here].astype(wide)
        mids = [jnp.where(live > step * slots + s, slope[s] * lift, 0.0).astype(low) for s in range(slots)]
        mid = jnp.concatenate(mids, axis=0)
        mid_sum[...] += dot(ones, mid)
        g_mid[...] += dot_rows(act_one[here].reshape(slots * count, width), mid)
        slope = slope_one[here].reshape(slots * count, width).astype(wide)
        inner = (slope * dot_back(mid, w_mid[...])).astype(low)
        slope_one[here] = inner.reshape(slots, count, width)
        own_sum[...] += dot(fold, inner)

    own_low = own_sum[...].astype(low)
    sums.put("message_own", dot_rows(node_rows, own_low))
    sums.put("message_mid", g_mid[...])
    put_line("v_mid", mid_sum[0:1])
    put_line("v_in", jnp.sum(own_sum[...], axis=0, keepdims=True))
    beat()
    launch(total_run(spot, partner, total_three, total_three, totals[2], spare_wide))
    part = mixed + dot_back(own_low, w_in[0:width])
    node_part[0] = part[0 : count // 2]
    node_part[1] = part[count // 2 :]

    spread_sum[...] = jnp.zeros_like(spread_sum)
    g_edge[...] = jnp.zeros_like(g_edge)

    @pl.loop(0, steps)
    def _(step):
        here = pl.ds(step * slots, slots)
        inner = slope_one[here].reshape(slots * count, width)
        g_edge[...] += dot_rows(edges[here].reshape(slots * count, narrow), inner)
        spread_sum[...] += dot(pick_columns(rows[step], total), inner)

    spread_low = spread_sum[...].astype(low)
    spread[...] = spread_low.reshape(spread.shape)
    beat()
    launch(owner_run(spot, spread, node_part, w_in.at[width : 2 * width], grad_nodes, node_scratch))
    sums.put("message_near", dot_rows(table[...].reshape(total, width), spread_low))
    sums.put("message_edge", g_edge[...])
    sums.put("lines", lines[...])
    launch(total_run(spot, partner, total_four, total_four, totals[3], spare_wide))

    @pl.loop(0, steps)
    def _(step):
        here = pl.ds(step * slots, slots)
        inner = slope_one[here].reshape(slots * count, width)
        back_part = dot_back(inner, w_in[2 * width :]).reshape(slots, count, narrow)
        partial[here] = (partial[here].astype(wide) + back_part).astype(low)

    leaving = [result_copy, pltpu.make_async_copy(partial, edge_total, puts.at[0])]
    leaving[1].start()
    beat()
    while any(run in gathers for run in moving):
        beat()
    feed = feed_run(
        spot, partner, normed_table, down_table, w_up, b_up, w_down, out_up, out_down,
        feed_parts[0], slope_two, act_one, *feed_parts[1:]
    )
    for place, _ in enumerate(feed):
        if place % FEED_BEAT == FEED_BEAT - 1:
            beat()
    while moving:
        beat()
    for copy in leaving:
        copy.wait()


def unpack(pieces, places, node_in, grad_in, *refs):
    node_out, grad_out, refs = refs[8], refs[9], refs[:8] + refs[10:]
    ins, outs = refs[:8], refs[8:32]
    node_out[...] = node_in[...]
    grad_out[...] = grad_in[...].reshape(grad_out.shape)
    (m_in_far, m_in_b, m_mid_far, m_mid_b, m_out_far, m_out_b, n_gain, n_shift, f_up_far, f_up_b, f_down_far, f_down_b,
     l_gain, l_shift, e_in_far, e_in_b, e_mid, e_mid_b, e_out, e_out_b, e_gain, e_shift, edge_far, result_far) = outs
    near, (m_in, m_mid, m_out, f_up, f_down, e_in, edge), (reads, writes) = refs[32:40], refs[40:47], refs[47:]
    width, narrow, hidden = m_mid.shape[0], e_mid.shape[0], f_up.shape[1]
    coming = [pltpu.make_async_copy(there, here, reads.at[place]) for place, (there, here) in enumerate(zip(ins, near))]
    groups = near[:4]
    (up_low, down_low, part, result) = near[4:]
    for place in (4, 5, 6, 7, 0, 1, 2, 3):
        coming[place].start()
    leaving = []

    def leave(source, target):
        copy = pltpu.make_async_copy(source, target, writes.at[len(leaving)])
        copy.start()
        leaving.append(copy)

    span = down_low.shape[1]
    coming[4].wait()
    for piece in range(hidden // span):
        lanes = slice(piece * span, (piece + 1) * span)
        f_up[:, lanes] = up_low[piece].astype(wide)
        leave(f_up.at[:, lanes], f_up_far.at[:, lanes])
    coming[5].wait()
    for piece in range(hidden // span):
        lanes = slice(piece * span, (piece + 1) * span)
        f_down[lanes] = down_low[piece].astype(wide)
        leave(f_down.at[lanes], f_down_far.at[lanes])
    coming[6].wait()
    chunk = edge.shape[0] // 5
    for piece in range(5):
        here = slice(piece * chunk, (piece + 1) * chunk)
        edge[here] = part[here].astype(wide)
        leave(edge.at[here], edge_far.at[here])
    coming[7].wait()
    leave(result, result_far)
    for copy in coming[:4]:
        copy.wait()

    def move(name, target, first_row=0, first_lane=0, most=None):
        for piece, first, tall, lane, group, row in pieces:
            if piece == name:
                size = min(groups[group].shape[1], (most or width) - lane)
                target[
                    first_row + first : first_row + first + tall, first_lane + lane : first_lane + lane + size
                ] = groups[group][row : row + tall, 0:size].astype(wide)

    move("message_own", m_in)
    move("message_near", m_in, width)
    move("message_edge", m_in, 2 * width)
    leave(m_in, m_in_far)
    move("message_mid", m_mid)
    leave(m_mid, m_mid_far)
    move("message_out", m_out)
    leave(m_out, m_out_far)
    move("edge_own", e_in)
    move("edge_near", e_in, 0, width)
    move("e_in", e_in, 0, 2 * width, narrow)
    leave(e_in, e_in_far)
    move("e_mid", e_mid, 0, 0, narrow)
    move("e_out", e_out, 0, 0, narrow)

    def rows_of(name):
        found = [groups[group][row : row + 16].astype(wide) for piece, _, _, _, group, row in pieces if piece == name]
        return jnp.concatenate(found, axis=1)

    lines, e_lines = rows_of("lines"), rows_of("e_lines")
    for name, ref in (
        ("v_in", m_in_b), ("v_mid", m_mid_b), ("v_out", m_out_b), ("v_node_gain", n_gain), ("v_node_shift", n_shift),
        ("v_final_gain", l_gain), ("v_final_shift", l_shift), ("v_down", f_down_b),
    ):
        ref[...] = lines[places[name]]
    for piece in range(hidden // width):
        f_up_b[piece * width : (piece + 1) * width] = lines[piece]
    for place, ref in enumerate((e_gain, e_shift, e_out_b, e_mid_b, e_in_b)):
        ref[...] = e_lines[place, 0:narrow]
    for copy in leaving:
        copy.wait()


def table_kernel(grid, own, table, *sems):
    spot = Spot(grid)
    copy = pltpu.make_async_copy(own, table.at[spot.z, spot.y, spot.x], sems[-1])
    copy.start()
    meet(spot.peers())
    copy.wait()
    drive(gather_run(gather_plan(spot, table, sems[:-1])))


def owner_kernel(grid, part, out, *scratch):
    spot = Spot(grid)
    meet(spot.peers())
    sums = []
    drive(scatter_run(spot, part, scratch, sums))
    out[0] = sums[0]
    out[1] = sums[1]


def total_run(spot, partner, given, out, scratch, spare=None):
    pair, parts, sems = scratch[0], scratch[1:10], scratch[10]
    (ra1, rb1, ra2, rb2, r3) = parts[:5]
    places = (pair, pair, r3, ra2, rb2, ra1, rb1)
    side_z, side_y, side_x = spot.grid
    z, y, x = spot.z, spot.y, spot.x
    core = spot.core
    mine = out.at[core]

    def go(source, target, kind, device):
        remote(source, target, sems.at[0, kind], sems.at[1, kind], device).start()

    def come(kind):
        wait_bytes(places[kind], sems.at[1, kind])

    if spare is None:
        go(given.at[1 - core], pair, 0, partner)
    else:
        spare[...] = given[1 - core]
        go(spare, pair, 0, partner)
    yield

    def before():
        come(0)
        wait_bytes(pair, sems.at[0, 0])
        mine[...] = (given[core].astype(wide) + pair[...].astype(wide)).astype(low)

    sums = []
    yield from scatter_run(spot, mine, parts, sums, before)
    for half in range(2):
        mine[z, y, x, half] = sums[half].astype(low)

    def first(zj):
        for s in range(1, side_x):
            go(mine.at[zj, y, x, 0], mine.at[zj, y, x, 0], 3, spot.device(z, y, spot.far_x(s)))
        for s in range(1, side_y):
            go(mine.at[zj, y, x, 1], mine.at[zj, y, x, 1], 4, spot.device(z, spot.far_y(s), x))

    for s in range(1, side_z):
        go(mine.at[z, y, x], mine.at[z, y, x], 2, spot.device(spot.far_z(s), y, x))
    first(z)
    yield
    come(2)
    for s in range(1, side_z):
        first(spot.far_z(s))
    yield
    come(3)
    come(4)
    for j in range(side_z):
        zj = flip(z, j)
        for s in range(1, side_y):
            go(mine.at[zj, y, :, 0], mine.at[zj, y, :, 0], 5, spot.device(z, spot.far_y(s), x))
        for s in range(1, side_x):
            go(mine.at[zj, :, x, 1], mine.at[zj, :, x, 1], 6, spot.device(z, y, spot.far_x(s)))
    yield
    come(5)
    come(6)
    go(mine, mine, 1, partner)
    yield
    come(1)
    for kind in range(1, len(places)):
        wait_bytes(places[kind], sems.at[0, kind])


def total_scratch(grid, rows, width):
    return (
        [pltpu.VMEM(grid + (2, rows, width), low)]
        + scatter_scratch(grid, rows, width)
        + [pltpu.SemaphoreType.DMA((2, 7))]
    )


def owner_run(spot, part, node_part, w_near, out, scratch):
    sums = []
    yield from scatter_run(spot, part, scratch, sums)
    for half in range(2):
        out[half] = node_part[half] + dot_back(sums[half].astype(low), w_near[...])


def feed_run(
    spot, partner, normed_table, down_table, w_up, b_up, w_down, out_up, out_down,
    bias, sent, near, sends, arrives, last_sends, last_arrives,
):
    span = w_up.shape[1] // out_up.shape[0]
    half = out_up.shape[0] // 2
    core = spot.core
    width = w_up.shape[0]
    rows = math.prod(normed_table.shape) // width
    bias[...] = as_row(b_up)
    rows_each = sent.shape[1]

    def piece(place):
        normed = normed_table[...].reshape(rows, width)
        down = down_table[...].reshape(rows, width)
        lanes = pl.ds(pl.multiple_of(place * span, span), span)
        act, slope = gelu_pair(dot(normed, w_up[:, lanes]) + bias[:, lanes])
        up = (slope * dot_back(down, w_down[lanes, :])).astype(low)
        return dot_rows(normed, up), dot_rows(act.astype(low), down)

    started = []
    for q in range(half):
        up, down = piece((1 - core) * half + q)
        tall = span // rows_each
        beside = jnp.concatenate([up[0:span], up[span:]], axis=1)
        sent[2 * q * tall : (2 * q + 1) * tall] = beside.astype(low).reshape(tall, rows_each, width)
        sent[(2 * q + 1) * tall : (2 * q + 2) * tall] = down.astype(low).reshape(tall, rows_each, width)
        here = slice(2 * q * tall, (2 * q + 2) * tall)
        pair = [remote(sent.at[here], near.at[here], sends.at[q], arrives.at[q], partner)]
        start_all(pair)
        started.append(pair)
        yield
    finals = []
    for q in range(half):
        place = core * half + q
        up, down = piece(place)
        arrived(started[q])
        beside = near[2 * q * tall : (2 * q + 1) * tall].reshape(span, width).astype(wide)
        near_down = near[(2 * q + 1) * tall : (2 * q + 2) * tall].reshape(span, width).astype(wide)
        near_up = jnp.concatenate([beside[:, 0:span], beside[:, span:]], axis=0)
        out_up[place] = (up + near_up).astype(low)
        out_down[place] = (down + near_down).astype(low)
        pair = [
            remote(out_up.at[place], out_up.at[place], last_sends.at[0, q], last_arrives.at[0, q], partner),
            remote(out_down.at[place], out_down.at[place], last_sends.at[1, q], last_arrives.at[1, q], partner),
        ]
        start_all(pair)
        finals += pair
        yield
    arrived(finals)
    all_sent(flat(started) + finals)


def feed_scratch(width, hidden, pieces, rows=None):
    dma = pltpu.SemaphoreType.DMA
    half = pieces // 2
    spare = [] if rows is None else [pltpu.VMEM((hidden // rows, rows, width), low)] * 2
    return [pltpu.VMEM((1, hidden), wide)] + spare + [dma((half,)), dma((half,)), dma((2, half)), dma((2, half))]


def tail_kernel(
    grid, given, part, node_part, w_near, table, w_up, b_up, w_down, summed, out_nodes, out_up, out_down, *scratch
):
    spot = Spot(grid)
    partner = (1 - spot.core, lax.axis_index("res"))
    meet(spot.peers() + [partner])
    total = total_run(spot, partner, given, summed, scratch[:11])
    owner = owner_run(spot, part, node_part, w_near, out_nodes, scratch[11:20])
    feed = feed_run(spot, partner, table.at[:, :, :, 0], table.at[:, :, :, 1], w_up, b_up, w_down, out_up, out_down, *scratch[20:])
    runs = [owner, total, feed]
    while runs:
        for run in list(runs):
            if next(run, runs) is runs:
                runs.remove(run)


vmem = pl.BlockSpec(memory_space=pltpu.VMEM)
far = pl.BlockSpec(memory_space=pl.ANY)
most_vmem = 67_000_000


def params(collective=None, **more):
    if collective is None:
        return pltpu.CompilerParams(vmem_limit_bytes=most_vmem, **more)
    return pltpu.CompilerParams(
        collective_id=collective, has_side_effects=True, vmem_limit_bytes=most_vmem, **more
    )


def gather_table(grid, rows, collective):
    count, width = rows.shape
    table = pl.pallas_call(
        functools.partial(table_kernel, grid),
        out_shape=jax.ShapeDtypeStruct(grid + (2, count // 2, width), low),
        in_specs=[vmem],
        out_specs=vmem,
        scratch_shapes=gather_sems(grid) + [pltpu.SemaphoreType.DMA],
        compiler_params=params(collective),
        name="gather_table_%d" % width,
    )(rows.reshape(2, count // 2, width))
    return table.reshape(-1, width)


def held(array):
    return pl.BlockSpec(array.shape, lambda step, dims=len(array.shape): (0,) * dims, pipeline_mode=pl.Buffered(1))


def streamed(array, slots):
    return pl.BlockSpec((slots,) + array.shape[1:], lambda step, dims=len(array.shape): (step,) + (0,) * (dims - 1))


def call(kernel, name, steps, slots, inputs, outputs, scratch, collective=None):
    def spec(item, flow):
        return streamed(item, slots if item.shape[0] != steps else 1) if flow else held(item)
    return pl.pallas_call(
        kernel,
        grid=(steps,),
        in_specs=[spec(item, flow) for item, flow in inputs],
        out_specs=[spec(item, flow) for item, flow in outputs],
        out_shape=[item for item, _ in outputs],
        scratch_shapes=scratch,
        compiler_params=params(collective),
        name=name,
    )(*[item for item, _ in inputs])


def per_device(
    node_states, edge_states, neighbours, residue_mask, neighbour_count,
    message_in, message_in_bias, message_mid, message_mid_bias, message_out, message_out_bias,
    node_gain, node_shift, feed_up, feed_up_bias, feed_down, feed_down_bias, final_gain, final_shift,
    edge_in, edge_in_bias, edge_mid, edge_mid_bias, edge_out, edge_out_bias, edge_gain, edge_shift,
    node_cotangent, edge_cotangent,
):
    grid = chip_grid(lax.axis_size("res"))
    nodes = node_states[0]
    count, width = nodes.shape
    edges = jnp.transpose(edge_states[0], (1, 0, 2))
    edge_ct = jnp.transpose(edge_cotangent[0], (1, 0, 2))
    depth, _, narrow = edges.shape
    hidden = feed_up.shape[1]
    total = grid[0] * grid[1] * grid[2] * count
    slots = 20 if total <= 1024 else 12
    steps = depth // slots
    edge_in_t = jnp.transpose(edge_in)
    lanes = -(-narrow // 128) * 128
    shape = jax.ShapeDtypeStruct
    slab = shape((depth, count, width), low)
    node_low, node_wide = shape((count, width), low), shape((count, width), wide)
    scratch = pltpu.VMEM

    square = shape((narrow, narrow), wide)
    if total <= 1024:
        places = line_places(width, hidden)
        blocks = (2,) + grid + (2, 16, width)
        each = math.prod(blocks[:-1])
        cut = sum_pieces(width, narrow, each)
        pieces = hidden // 256
        near_index = jnp.transpose(neighbours, (2, 0, 1))
        half_rows = (2, count // 2, width)
        lane_rows = (2, count // 2, lanes)
        dma = pltpu.SemaphoreType.DMA
        whole, few = shape(blocks, low), shape(blocks[:-1] + (width // 2,), low)
        near = [
            near_index, neighbour_count, residue_mask, nodes.reshape(half_rows), message_in_bias, message_mid_bias,
            message_out_bias, node_gain, node_shift, feed_up_bias, feed_down_bias, final_gain, final_shift,
            edge_in_bias, edge_mid, edge_mid_bias, edge_out, edge_out_bias, edge_gain, edge_shift, node_cotangent[0],
        ]
        distant = [edges, edge_ct, message_in, message_mid, message_out, feed_up, feed_down, edge_in_t]
        strip = scratch((count, narrow), wide)
        (node_out, edge_result, edge_total, grad_nodes, *totals, up_low, down_low) = pl.pallas_call(
            functools.partial(whole_kernel, grid, slots, cut, places),
            out_shape=[node_low, shape(edges.shape, low), shape(edges.shape, low), shape(half_rows, wide),
                       few, few, whole, whole,
                       shape((pieces, width, hidden // pieces), low), shape((pieces, hidden // pieces, width), low)],
            in_specs=[vmem] * len(near) + [far] * len(distant),
            out_specs=[vmem, far, far] + [vmem] * 7,
            scratch_shapes=[scratch(a.shape, low) for a in distant] + [dma((8,)), dma((steps + 2,)), scratch((count, depth), jnp.int32), scratch((steps, 1, slots * count), jnp.int32)]
            + [scratch(slab.shape, low)] * 3
            + [scratch(edges.shape, low), scratch(grid + half_rows, low),
               scratch((count, width), wide), scratch((count, width), wide), scratch((count, hidden), wide),
               scratch(grid + lane_rows, low), strip, scratch((total, narrow), wide), scratch(grid + lane_rows, low),
               strip] + [scratch(square.shape, wide)] * 3 + [scratch((8, narrow), wide)]
            + [scratch((total, width), wide), scratch(grid + half_rows, low),
               scratch((count, width), wide), scratch((8, width), wide), scratch((width, width), wide),
               scratch((narrow, width), wide), scratch((16, width), wide), scratch(half_rows, wide),
               scratch(grid + half_rows, low), scratch(grid + half_rows, low),
               scratch(blocks[1:-1] + (width // 2,), low), scratch(blocks[1:], low)]
            + gather_sems(grid) * 4
            + scatter_scratch(grid, count // 2, lanes) + scatter_scratch(grid, count // 2, width)
            + feed_scratch(width, hidden, pieces) + total_scratch(grid, 16, width // 2) * 2
            + total_scratch(grid, 16, width) * 2,
            compiler_params=params(0), name="whole",
        )(*near, *distant)
        vector, line = shape((width,), wide), shape((narrow,), wide)
        sources = [each_total.reshape(each, -1) for each_total in totals] + [up_low, down_low, edge_total, edge_result]
        kinds = [message_in.shape, vector, message_mid.shape, vector, message_out.shape, vector, vector, vector,
                 feed_up.shape, shape((hidden,), wide), feed_down.shape, vector, vector, vector, edge_in_t.shape, line,
                 square, line, square, line, line, line, edges.shape]
        staged = [kind for kind in kinds if isinstance(kind, tuple)]
        node_out, grad_nodes, *grads, edge_grad, edge_result = pl.pallas_call(
            functools.partial(unpack, cut, places),
            out_shape=[node_low, node_wide] + [shape(kind, wide) if isinstance(kind, tuple) else kind for kind in kinds] + [shape(edges.shape, low)],
            in_specs=[vmem] * 2 + [far] * 8, out_specs=[vmem] * 2 + [far if isinstance(kind, tuple) else vmem for kind in kinds] + [far],
            scratch_shapes=[scratch(a.shape, low) for a in sources] + [scratch(kind, wide) for kind in staged]
            + [dma((8,)), dma((32,))],
            compiler_params=params(), name="unpack",
        )(node_out, grad_nodes, *sources)
    else:
        index = neighbours[0]
        rows = jnp.transpose(index).reshape(steps, 1, slots * count)
        table = gather_table(grid, nodes, 0)
        (slope_one, slope_two, act_one, mixed_low, resid, second_sum, up_slope, node_out, sent, own_edge) = call(
            functools.partial(message_forward, slots), "message_forward", steps, slots,
            [(index, False), (neighbour_count, False), (residue_mask, False), (nodes, False), (table, False), (edges, True)]
            + [(a, False) for a in (
                message_in, message_in_bias, message_mid, message_mid_bias, message_out, message_out_bias,
                node_gain, node_shift, feed_up, feed_up_bias, feed_down, feed_down_bias, final_gain, final_shift,
                edge_in_t, edge_in_bias)],
            [(slab, True)] * 3 + [(node_low, False), (node_wide, False), (node_wide, False),
             (shape((count, hidden), wide), False), (node_low, False),
             (shape((count, lanes), low), False), (shape((count, narrow), wide), False)],
            [scratch((total, width), low), scratch((count, width), wide), scratch((count, width), wide)],
        )
        sent_table = gather_table(grid, sent, 1)
        (edge_result, partial, spread_two, own_edge_grad, e_in, e_mid, e_out, e_vectors) = call(
            functools.partial(edge_pass, slots), "edge_pass", steps, slots,
            [(index, False), (rows, True), (sent_table, False), (own_edge, False), (edges, True), (edge_ct, True)]
            + [(a, False) for a in (edge_in_t, edge_mid, edge_mid_bias, edge_out, edge_out_bias, edge_gain, edge_shift)],
            [(shape(edges.shape, low), True), (shape(edges.shape, low), True), (shape((total, lanes), low), False),
             (shape((count, narrow), wide), False), (square, False), (square, False), (square, False),
             (shape((8, narrow), wide), False)],
            [scratch((total, narrow), wide)],
        )
        back_edge = pl.pallas_call(
            functools.partial(owner_kernel, grid),
            out_shape=shape((2, count // 2, lanes), wide),
            in_specs=[vmem], out_specs=vmem,
            scratch_shapes=scatter_scratch(grid, count // 2, lanes),
            compiler_params=params(2), name="edge_owner",
        )(spread_two.reshape(grid + (2, count // 2, lanes))).reshape(count, lanes)[:, :narrow]
        shares = 4 * grid[0] * grid[1] * grid[2] * 16
        layout = lay_out_rows(width, narrow, hidden, shares)
        table_blocks = grid + (2, count, width)
        (edge_grad, spread, node_part, packed, feed_table) = call(
            functools.partial(node_backward, grid, slots, layout), "node_backward", steps, slots,
            [(rows, True), (neighbour_count, False), (residue_mask, False), (nodes, False), (table, False), (edges, True),
             (slope_one, True), (slope_two, True), (act_one, True), (partial, True)]
            + [(a, False) for a in (
                mixed_low, resid, second_sum, up_slope, node_out, node_cotangent[0], back_edge, own_edge_grad,
                e_in, e_mid, e_out, e_vectors, message_in, message_mid, message_out, node_gain, node_shift,
                feed_up, feed_down, final_gain, edge_in_t)],
            [(shape(edges.shape, wide), True), (shape((total, width), low), False), (node_wide, False),
             (shape((layout["rows"], width), low), False), (shape(table_blocks, low), False)],
            [scratch((count, width), wide), scratch((total, width), wide), scratch((count, width), wide),
             scratch((width, width), wide), scratch((narrow, width), wide), scratch((1, width), wide),
             scratch((32, width), wide), scratch(table_blocks, low)] + gather_sems(grid),
            collective=3,
        )
        chunk = layout["rows"] // (4 * grid[0] * grid[1] * grid[2])
        blocks = (2,) + grid + (2, chunk, width)
        pieces = hidden // 256
        (summed, grad_nodes, up_low, down_low) = pl.pallas_call(
            functools.partial(tail_kernel, grid),
            out_shape=[shape(blocks, low), shape((2, count // 2, width), wide),
                       shape((pieces, width, hidden // pieces), low), shape((pieces, hidden // pieces, width), low)],
            in_specs=[vmem] * 8, out_specs=[vmem] * 4,
            scratch_shapes=total_scratch(grid, chunk, width) + scatter_scratch(grid, count // 2, width)
            + feed_scratch(width, hidden, pieces, count),
            compiler_params=params(4), name="tail",
        )(packed.reshape(blocks), spread.reshape(grid + (2, count // 2, width)), node_part.reshape(2, count // 2, width),
          message_in[width : 2 * width], feed_table, feed_up, feed_up_bias, feed_down)
        grad_nodes = grad_nodes.reshape(count, width)
        vector, line = shape((width,), wide), shape((narrow,), wide)
        grads = pl.pallas_call(
            functools.partial(unpack_rows, layout),
            out_shape=[
                shape(message_in.shape, wide), vector, shape(message_mid.shape, wide), vector,
                shape(message_out.shape, wide), vector, vector, vector, shape(feed_up.shape, wide), shape((hidden,), wide),
                shape(feed_down.shape, wide), vector, vector, vector, shape(edge_in_t.shape, wide), line,
                square, line, square, line, line, line,
            ],
            in_specs=[vmem] * 3, out_specs=[vmem] * 22,
            compiler_params=params(), name="unpack",
        )(summed.reshape(layout["rows"], width), up_low, down_low)
    grads = list(grads)
    grads[14] = jnp.transpose(grads[14])
    back = (1, 0, 2)
    return (
        node_out[None],
        jnp.transpose(edge_result, back)[None],
        grad_nodes[None],
        jnp.transpose(edge_grad, back)[None],
        *grads,
    )


def solution(mesh):
    split, whole = P("batch", "res"), P()
    in_specs = (split,) * 5 + (whole,) * 22 + (split,) * 2
    out_specs = (split,) * 4 + (whole,) * 22
    return jax.shard_map(per_device, mesh=mesh, in_specs=in_specs, out_specs=out_specs, check_vma=False)
```

```python
import functools
import math
import jax
import jax.numpy as jnp
from jax import lax
from jax.experimental import pallas as pl
from jax.experimental.pallas import tpu as pltpu
from jax.sharding import PartitionSpec as P

MESH = pl.DeviceIdType.MESH
low = jnp.bfloat16
FEED_BEAT = 2
wide = jnp.float32


def chip_grid(count):
    side_x = 2 if count < 64 else 4
    side_y = side_x
    return (count // (side_x * side_y), side_y, side_x)


def flip(place, step):
    bit = 1
    while bit <= step:
        if step & bit:
            place = place + bit - 2 * bit * ((place // bit) % 2)
        bit *= 2
    return place


class Spot:
    def __init__(self, grid):
        self.grid = grid
        side_z, side_y, side_x = grid
        me = lax.axis_index("res")
        self.core = lax.axis_index("batch")
        self.z = me // (side_y * side_x)
        self.y = (me // side_x) % side_y
        self.x = me % side_x

    def device(self, z, y, x):
        return (self.core, (z * self.grid[1] + y) * self.grid[2] + x)

    def far_z(self, step):
        return flip(self.z, step)

    def far_y(self, step):
        return flip(self.y, step)

    def far_x(self, step):
        return flip(self.x, step)

    def peers(self):
        found = [self.device(self.far_z(s), self.y, self.x) for s in range(1, self.grid[0])]
        found += [self.device(self.z, self.far_y(s), self.x) for s in range(1, self.grid[1])]
        found += [self.device(self.z, self.y, self.far_x(s)) for s in range(1, self.grid[2])]
        return found


def greet(peers):
    barrier = pltpu.get_barrier_semaphore()
    for peer in peers:
        pl.semaphore_signal(barrier, inc=1, device_id=peer, device_id_type=MESH)


def met(peers):
    pl.semaphore_wait(pltpu.get_barrier_semaphore(), len(peers))


def meet(peers):
    greet(peers)
    met(peers)


def remote(source, target, send, arrive, device):
    return pltpu.make_async_remote_copy(
        src_ref=source, dst_ref=target, send_sem=send, recv_sem=arrive,
        device_id=device, device_id_type=MESH,
    )


def gather_sems(grid):
    side_z, side_y, side_x = grid
    dma = pltpu.SemaphoreType.DMA
    shapes = [(side_z - 1,), (side_z, side_x - 1), (side_z, side_y - 1), (side_z, side_y - 1), (side_z, side_x - 1)]
    return [dma(s) for s in shapes for _ in range(2)]


def gather_plan(spot, table, sems):
    (s1, r1, s2a, r2a, s2b, r2b, s3a, r3a, s3b, r3b) = sems
    side_z, side_y, side_x = spot.grid
    z, y, x = spot.z, spot.y, spot.x

    def push(view, send, arrive, device):
        return remote(view, view, send, arrive, device)

    ups = [
        push(table.at[z, y, x], s1.at[s - 1], r1.at[s - 1], spot.device(spot.far_z(s), y, x))
        for s in range(1, side_z)
    ]
    firsts, lasts = [], []
    for j in range(side_z):
        zj = flip(z, j)
        firsts.append(
            [
                push(table.at[zj, y, x, 0], s2a.at[j, s - 1], r2a.at[j, s - 1], spot.device(z, y, spot.far_x(s)))
                for s in range(1, side_x)
            ]
            + [
                push(table.at[zj, y, x, 1], s2b.at[j, s - 1], r2b.at[j, s - 1], spot.device(z, spot.far_y(s), x))
                for s in range(1, side_y)
            ]
        )
        lasts.append(
            [
                push(table.at[zj, y, :, 0], s3a.at[j, s - 1], r3a.at[j, s - 1], spot.device(z, spot.far_y(s), x))
                for s in range(1, side_y)
            ]
            + [
                push(table.at[zj, :, x, 1], s3b.at[j, s - 1], r3b.at[j, s - 1], spot.device(z, y, spot.far_x(s)))
                for s in range(1, side_x)
            ]
        )
    return ups, firsts, lasts


def start_all(copies):
    for copy in copies:
        copy.start()


def arrived(copies):
    for copy in copies:
        copy.wait_recv()


def all_sent(copies):
    for copy in copies:
        copy.wait_send()


def flat(groups):
    return [copy for group in groups for copy in group]


def gather_run(plan):
    ups, firsts, lasts = plan
    count = len(lasts)
    start_all(ups + firsts[0])
    yield
    for j in range(1, count):
        arrived([ups[j - 1]])
        start_all(firsts[j])
        arrived(firsts[j - 1])
        start_all(lasts[j - 1])
        if j + 1 < count:
            yield
    arrived(firsts[count - 1])
    start_all(lasts[count - 1])
    yield
    for j in range(count):
        arrived(lasts[j])
    yield
    all_sent(ups + flat(firsts) + flat(lasts))


def drive(run):
    for _ in run:
        pass


def scatter_scratch(grid, rows, width):
    side_z, side_y, side_x = grid
    return [
        pltpu.VMEM((side_z, side_y - 1, side_x, rows, width), low),
        pltpu.VMEM((side_z, side_x - 1, side_y, rows, width), low),
        pltpu.VMEM((side_z, side_x - 1, rows, width), low),
        pltpu.VMEM((side_z, side_y - 1, rows, width), low),
        pltpu.VMEM((side_z - 1, 2, rows, width), low),
        pltpu.VMEM((side_z, side_x, rows, width), low),
        pltpu.VMEM((side_z, side_y, rows, width), low),
        pltpu.VMEM((side_z, 2, rows, width), low),
        pltpu.SemaphoreType.DMA((2, 5)),
    ]


def wait_bytes(like, sem):
    pltpu.make_async_copy(like, like, sem).wait()


def scatter_run(spot, part, scratch, result, before=None):
    (ra1, rb1, ra2, rb2, r3, ka, kb, tot, sems) = scratch
    places = (ra1, rb1, ra2, rb2, r3)
    side_z, side_y, side_x = spot.grid
    z, y, x = spot.z, spot.y, spot.x

    def go(source, target, kind, device):
        remote(source, target, sems.at[0, kind], sems.at[1, kind], device).start()

    def come(kind):
        wait_bytes(places[kind], sems.at[1, kind])

    order = range(side_z - 1, -1, -1)
    if before is not None:
        before()
    for j in order:
        zj = flip(z, j)
        for s in range(1, side_y):
            go(part.at[zj, spot.far_y(s), :, 0], ra1.at[j, s - 1], 0, spot.device(z, spot.far_y(s), x))
        for s in range(1, side_x):
            go(part.at[zj, :, spot.far_x(s), 1], rb1.at[j, s - 1], 1, spot.device(z, y, spot.far_x(s)))
    yield
    come(0)
    for j in order:
        total = part[flip(z, j), y, :, 0].astype(wide)
        for s in range(side_y - 1):
            total = total + ra1[j, s].astype(wide)
        ka[j] = total.astype(low)
        for s in range(1, side_x):
            go(ka.at[j, spot.far_x(s)], ra2.at[j, s - 1], 2, spot.device(z, y, spot.far_x(s)))
    come(1)
    for j in order:
        total = part[flip(z, j), :, x, 1].astype(wide)
        for s in range(side_x - 1):
            total = total + rb1[j, s].astype(wide)
        kb[j] = total.astype(low)
        for s in range(1, side_y):
            go(kb.at[j, spot.far_y(s)], rb2.at[j, s - 1], 3, spot.device(z, spot.far_y(s), x))
    yield
    come(2)
    come(3)
    for j in order:
        upper = ka[j, x].astype(wide)
        for s in range(side_x - 1):
            upper = upper + ra2[j, s].astype(wide)
        lower = kb[j, y].astype(wide)
        for s in range(side_y - 1):
            lower = lower + rb2[j, s].astype(wide)
        if j:
            tot[j, 0] = upper.astype(low)
            tot[j, 1] = lower.astype(low)
            go(tot.at[j], r3.at[j - 1], 4, spot.device(flip(z, j), y, x))
    yield
    come(4)
    for s in range(side_z - 1):
        upper = upper + r3[s, 0].astype(wide)
        lower = lower + r3[s, 1].astype(wide)
    result += [upper, lower]
    for kind, like in enumerate(places):
        wait_bytes(like, sems.at[0, kind])
eps_norm = 1e-05
root_half = 0.7071067811865476
turn_scale = 0.5641895835477563
minus_log2e = -1.4426950408889634


def dot(left, right):
    return jnp.dot(left, right, preferred_element_type=wide)


def dot_back(left, right):
    return lax.dot_general(left, right, (((1,), (1,)), ((), ())), preferred_element_type=wide)


def dot_rows(left, right):
    return lax.dot_general(left, right, (((0,), (0,)), ((), ())), preferred_element_type=wide)


def gelu_pair(values):
    scaled = values * root_half
    share = 0.5 + 0.5 * lax.erf(scaled)
    slope = share + scaled * turn_scale * jnp.exp2(scaled * scaled * minus_log2e)
    return values * share, slope


def norm_stats(values):
    centre = jnp.mean(values, axis=-1, keepdims=True)
    centred = values - centre
    variance = jnp.mean(centred * centred, axis=-1, keepdims=True)
    scale = lax.rsqrt(variance + eps_norm)
    return centred * scale, scale


def norm_back(hat, scale, gain, grad):
    inner = grad * gain
    return scale * (
        inner
        - jnp.mean(inner, axis=-1, keepdims=True)
        - hat * jnp.mean(inner * hat, axis=-1, keepdims=True)
    )


def as_row(ref, start=None, size=None):
    return ref[...].astype(wide).reshape(1, ref.shape[0])


def as_column(row, count):
    rows = lax.broadcasted_iota(jnp.int32, (count, count), 0)
    lanes = lax.broadcasted_iota(jnp.int32, (count, count), 1)
    return jnp.sum(jnp.where(rows == lanes, jnp.broadcast_to(row, (count, count)), 0), axis=1, keepdims=True)


def slot_column(index, slot):
    lanes = lax.broadcasted_iota(jnp.int32, index.shape, 1)
    return jnp.sum(jnp.where(lanes == slot, index, 0), axis=1, keepdims=True)


def pick_rows(index, first, slots, total):
    count = index.shape[0]
    lanes = lax.broadcasted_iota(jnp.int16, (count, total), 1)
    one, none = jnp.ones((), low), jnp.zeros((), low)
    return jnp.concatenate(
        [
            jnp.where(jnp.broadcast_to(slot_column(index, first + s), (count, total)).astype(jnp.int16) == lanes, one, none)
            for s in range(slots)
        ],
        axis=0,
    )


def pick_columns(row, total):
    rows = lax.broadcasted_iota(jnp.int16, (total, row.shape[1]), 0)
    one, none = jnp.ones((), low), jnp.zeros((), low)
    return jnp.where(rows == jnp.broadcast_to(row.astype(jnp.int16), rows.shape), one, none)


def message_forward(
    slots, index, counts, masks, nodes, table, edges, w_in, b_in, w_mid, b_mid, w_out, b_out,
    gain_one, shift_one, w_up, b_up, w_down, b_down, gain_two, shift_two, w_edge, b_edge,
    slope_one, slope_two, act_one, mixed_low, resid, second_sum, up_slope, node_out, sent, own_edge,
    projected, own, pooled,
):
    step = pl.program_id(0)
    count, width = nodes.shape
    total = table.shape[0]
    live = as_column(counts[...], count)

    @pl.when(step == 0)
    def _():
        projected[...] = dot(table[...], w_in[width : 2 * width]).astype(low)
        own[...] = dot(nodes[...], w_in[0:width]) + as_row(b_in)
        pooled[...] = jnp.zeros_like(pooled)

    picks = pick_rows(index[...], step * slots, slots, total)
    edge_rows = edges[...].reshape(slots * count, edges.shape[2])
    pre = dot(picks, projected[...]) + dot(edge_rows, w_in[2 * width :])
    pre = pre.reshape(slots, count, width) + own[...][None]
    act, slope = gelu_pair(pre)
    act = act.astype(low)
    act_one[...] = act
    slope_one[...] = slope.astype(low)
    pre = dot(act.reshape(slots * count, width), w_mid[...]) + as_row(b_mid)
    act, slope = gelu_pair(pre)
    act = act.reshape(slots, count, width)
    slope_two[...] = slope.astype(low).reshape(slots, count, width)
    gathered = pooled[...]
    for s in range(slots):
        gathered = gathered + jnp.where(live > step * slots + s, act[s], 0.0)
    pooled[...] = gathered

    @pl.when(step == pl.num_programs(0) - 1)
    def _():
        mean = pooled[...] / jnp.maximum(live, 1).astype(wide)
        mean_low = mean.astype(low)
        mixed_low[...] = mean_low
        some = jnp.where(live > 0, 1.0, 0.0)
        mask = as_column(masks[...], count).astype(wide)
        aggregate = dot(mean_low, w_out[...]) + some * as_row(b_out)
        total_sum = nodes[...].astype(wide) + mask * aggregate
        resid[...] = total_sum
        hat, _ = norm_stats(total_sum)
        first = hat * as_row(gain_one) + as_row(shift_one)
        up = dot(first.astype(low), w_up[...]) + as_row(b_up)
        act_up, slope_up = gelu_pair(up)
        act_up = act_up.astype(low)
        up_slope[...] = slope_up
        summed = first + dot(act_up, w_down[...]) + as_row(b_down)
        second_sum[...] = summed
        hat, _ = norm_stats(summed)
        out = (hat * as_row(gain_two) + as_row(shift_two)).astype(low)
        node_out[...] = out
        pad = jnp.zeros((count, sent.shape[1] - w_edge.shape[0]), low)
        sent[...] = jnp.concatenate([dot_back(out, w_edge[:, width : 2 * width]).astype(low), pad], axis=1)
        own_edge[...] = dot_back(out, w_edge[:, 0:width]) + as_row(b_edge)


def edge_pass(
    slots, index, rows, table, own_edge, edges, cotangent, w_edge, w_mid, b_mid, w_out, b_out, gain, shift,
    result, partial, spread, own_grad, g_in, g_mid, g_out, vectors, spread_sum,
):
    step = pl.program_id(0)
    count, width = own_edge.shape
    total = table.shape[0]
    base = w_edge.shape[1] - width

    @pl.when(step == 0)
    def _():
        spread_sum[...] = jnp.zeros_like(spread_sum)
        for ref in (own_grad, g_in, g_mid, g_out, vectors):
            ref[...] = jnp.zeros_like(ref)

    w_here = w_edge[:, base:]
    picks = pick_rows(index[...], step * slots, slots, total)
    edge_rows = edges[...].reshape(slots * count, width)
    pre = dot(picks, table[...])[:, 0:width] + dot_back(edge_rows, w_here)
    pre = (pre.reshape(slots, count, width) + own_edge[...][None]).reshape(slots * count, width)
    act_one, slope_one = gelu_pair(pre)
    act_one = act_one.astype(low)
    pre = dot(act_one, w_mid[...]) + as_row(b_mid)
    act_two, slope_two = gelu_pair(pre)
    act_two = act_two.astype(low)
    pre = dot(act_two, w_out[...]) + as_row(b_out)
    hat, scale = norm_stats(edge_rows.astype(wide) + pre)
    gain_row = as_row(gain)
    result[...] = (hat * gain_row + as_row(shift)).astype(low).reshape(slots, count, width)
    grad = cotangent[...].reshape(slots * count, width).astype(wide)
    sum_grad = norm_back(hat, scale, gain_row, grad)
    three = sum_grad.astype(low)
    g_out[...] += dot_rows(act_two, three)
    two = (slope_two * dot_back(three, w_out[...])).astype(low)
    g_mid[...] += dot_rows(act_one, two)
    one = (slope_one * dot_back(two, w_mid[...])).astype(low)
    g_in[...] += dot_rows(one, edge_rows)
    vectors[...] += jnp.concatenate(
        [
            jnp.sum(piece, axis=0, keepdims=True)
            for piece in (grad * hat, grad, three.astype(wide), two.astype(wide), one.astype(wide))
        ]
        + [jnp.zeros((3, width), wide)],
        axis=0,
    )
    own_grad[...] += jnp.sum(one.astype(wide).reshape(slots, count, width), axis=0)
    partial[...] = (sum_grad + dot(one, w_here)).astype(low).reshape(slots, count, width)
    spread_sum[...] += dot(pick_columns(rows[0], total), one)

    @pl.when(step == pl.num_programs(0) - 1)
    def _():
        pad = jnp.zeros((total, spread.shape[1] - width), low)
        spread[...] = jnp.concatenate([spread_sum[...].astype(low), pad], axis=1)


def node_backward(
    grid, slots, layout, rows, counts, masks, nodes, table, edges, slope_one, slope_two, act_one, partial,
    mixed_low, resid, second_sum, up_slope, node_out, cotangent, back_edge, own_edge_grad,
    e_in, e_mid, e_out, e_vectors,
    w_in, w_mid, w_out, gain_one, shift_one, w_up, w_down, gain_two, w_edge,
    edge_grad, spread, node_part, packed, feed_table,
    level, spread_sum, own_sum, g_mid, g_edge, bias_mid, lines, held_table, *sems,
):
    step = pl.program_id(0)
    last = pl.num_programs(0) - 1
    spot = Spot(grid)
    peers = spot.peers()
    ups, firsts, lasts = gather_plan(spot, held_table, sems)
    count, width = nodes.shape
    total = table.shape[0]
    narrow = w_edge.shape[0]
    hidden = w_up.shape[1]
    live = as_column(counts[...], count)

    def put(name, value):
        row = layout[name]
        packed[row : row + value.shape[0], :] = value.astype(low)

    def put_line(name, value):
        row = layout[name]
        lines[row : row + value.shape[0], 0 : value.shape[1]] = value

    @pl.when(step == 0)
    def _():
        greet(peers)
        for ref in (spread_sum, own_sum, g_mid, g_edge, bias_mid, lines):
            ref[...] = jnp.zeros_like(ref)
        out = node_out[...]
        own_low = own_edge_grad[...].astype(low)
        back_low = back_edge[...].astype(low)
        put("edge_own", dot_rows(own_low, out))
        put("edge_near", dot_rows(back_low, out))
        pad = jnp.zeros((narrow, width // 2 - narrow), wide)
        put("edge_a", jnp.concatenate([e_in[...], pad, e_mid[...], pad], axis=1))
        put("edge_b", jnp.concatenate([e_out[...], pad, jnp.zeros((narrow, width // 2), wide)], axis=1))
        put_line("e_vectors", e_vectors[...])
        grad = (
            cotangent[...].astype(wide)
            + dot(own_low, w_edge[:, 0:width])
            + dot(back_low, w_edge[:, width : 2 * width])
        )
        hat, scale = norm_stats(second_sum[...])
        put_line("v_final_gain", jnp.sum(grad * hat, axis=0, keepdims=True))
        put_line("v_final_shift", jnp.sum(grad, axis=0, keepdims=True))
        second = norm_back(hat, scale, as_row(gain_two), grad)
        down = second.astype(low)
        put_line("v_down", jnp.sum(down.astype(wide), axis=0, keepdims=True))
        held_table[spot.z, spot.y, spot.x, 1] = down
        up = (up_slope[...] * dot_back(down, w_down[...])).astype(low)
        bias_up = jnp.sum(up.astype(wide), axis=0, keepdims=True)
        hat, scale = norm_stats(resid[...])
        normed = (hat * as_row(gain_one) + as_row(shift_one)).astype(low)
        held_table[spot.z, spot.y, spot.x, 0] = normed
        met(peers)
        start_all(ups + firsts[0])
        for piece in range(hidden // width):
            lines[layout["v_up"] + piece : layout["v_up"] + piece + 1, :] = bias_up[:, piece * width : (piece + 1) * width]
        first = second + dot_back(up, w_up[...])
        put_line("v_node_gain", jnp.sum(first * hat, axis=0, keepdims=True))
        put_line("v_node_shift", jnp.sum(first, axis=0, keepdims=True))
        mixed = norm_back(hat, scale, as_row(gain_one), first)
        node_part[...] = mixed
        masked = as_column(masks[...], count).astype(wide) * mixed
        put_line("v_out", jnp.sum(jnp.where(live > 0, masked, 0.0), axis=0, keepdims=True))
        put("message_out", dot_rows(mixed_low[...], masked.astype(low)))
        shared = (masked / jnp.maximum(live, 1).astype(wide)).astype(low)
        level[...] = dot_back(shared, w_out[...])

    @pl.when(step == 1)
    def _():
        for j in range(1, len(firsts)):
            arrived([ups[j - 1]])
            start_all(firsts[j])

    @pl.when(step == 2)
    def _():
        for j in range(len(lasts)):
            arrived(firsts[j])
            start_all(lasts[j])

    lift = level[...]
    slope = slope_two[...].astype(wide)
    mid = jnp.concatenate(
        [jnp.where(live > step * slots + s, slope[s] * lift, 0.0).astype(low) for s in range(slots)], axis=0
    )
    flat_one = act_one[...].reshape(slots * count, width)
    g_mid[...] += dot_rows(flat_one, mid)
    bias_mid[...] += jnp.sum(mid.astype(wide), axis=0, keepdims=True)
    slope = slope_one[...].reshape(slots * count, width).astype(wide)
    inner = (slope * dot_back(mid, w_mid[...])).astype(low)
    own_sum[...] += jnp.sum(inner.astype(wide).reshape(slots, count, width), axis=0)
    edge_rows = edges[...].reshape(slots * count, narrow)
    g_edge[...] += dot_rows(edge_rows, inner)
    edge_grad[...] = partial[...].astype(wide) + dot_back(inner, w_in[2 * width :]).reshape(slots, count, narrow)
    spread_sum[...] += dot(pick_columns(rows[0], total), inner)

    @pl.when(step == pl.num_programs(0) - 1)
    def _():
        spread_low = spread_sum[...].astype(low)
        spread[...] = spread_low
        own_low = own_sum[...].astype(low)
        put("message_in", dot_rows(nodes[...], own_low))
        put("message_near", dot_rows(table[...], spread_low))
        put("message_edge", g_edge[...])
        put("message_mid", g_mid[...])
        put_line("v_mid", bias_mid[...])
        put_line("v_in", jnp.sum(own_sum[...], axis=0, keepdims=True))
        here = layout["lines"]
        tall = lines.shape[0]
        packed[here : here + tall, :] = lines[...].astype(low)
        rest = packed.shape[0] - here - tall
        if rest:
            packed[here + tall :, :] = jnp.zeros((rest, width), low)
        node_part[...] += dot_back(own_low, w_in[0:width])
        arrived(flat(lasts))
        all_sent(ups + flat(firsts) + flat(lasts))
        feed_table[...] = held_table[...]


def lay_out_rows(width, narrow, hidden, shares):
    pieces = hidden // width
    sizes = [
        ("message_in", width), ("message_near", width), ("message_edge", narrow), ("message_mid", width),
        ("message_out", width), ("edge_own", narrow),
        ("edge_near", narrow), ("edge_a", narrow), ("edge_b", narrow), ("lines", 32),
    ]
    layout, row = {}, 0
    for name, size in sizes:
        layout[name] = row
        row += size
    layout["rows"] = -(-row // shares) * shares
    layout["e_vectors"] = 0
    layout["v_up"] = 8
    singles = ("v_final_gain", "v_final_shift", "v_down", "v_node_gain", "v_node_shift", "v_out", "v_mid", "v_in")
    for place, name in enumerate(singles):
        layout[name] = 8 + pieces + place
    return layout


def unpack_rows(layout, packed, feed_up_low, feed_down_low, *outs):
    (m_in, m_in_b, m_mid, m_mid_b, m_out, m_out_b, n_gain, n_shift, f_up, f_up_b, f_down, f_down_b,
     l_gain, l_shift, e_in, e_in_b, e_mid, e_mid_b, e_out, e_out_b, e_gain, e_shift) = outs
    width = m_mid.shape[0]
    narrow = e_mid.shape[0]
    hidden = f_up.shape[1]
    half = width // 2

    def big(name, tall, lanes=slice(None)):
        return packed[layout[name] : layout[name] + tall, lanes].astype(wide)

    m_in[0:width] = big("message_in", width)
    m_in[width : 2 * width] = big("message_near", width)
    m_in[2 * width :] = big("message_edge", narrow)
    m_mid[...] = big("message_mid", width)
    m_out[...] = big("message_out", width)
    span = feed_down_low.shape[1]
    for piece in range(hidden // span):
        f_down[piece * span : (piece + 1) * span] = feed_down_low[piece].astype(wide)
        f_up[:, piece * span : (piece + 1) * span] = feed_up_low[piece].astype(wide)
    e_in[:, 0:width] = big("edge_own", narrow)
    e_in[:, width : 2 * width] = big("edge_near", narrow)
    e_in[:, 2 * width :] = big("edge_a", narrow, slice(0, narrow))
    e_mid[...] = big("edge_a", narrow, slice(half, half + narrow))
    e_out[...] = big("edge_b", narrow, slice(0, narrow))
    lines = packed[layout["lines"] : layout["lines"] + 32, :].astype(wide)

    def one(name):
        return lines[layout[name]]

    m_in_b[...] = one("v_in")
    m_mid_b[...] = one("v_mid")
    m_out_b[...] = one("v_out")
    n_gain[...] = one("v_node_gain")
    n_shift[...] = one("v_node_shift")
    l_gain[...] = one("v_final_gain")
    l_shift[...] = one("v_final_shift")
    f_down_b[...] = one("v_down")
    for piece in range(hidden // width):
        f_up_b[piece * width : (piece + 1) * width] = lines[layout["v_up"] + piece]
    for place, ref in enumerate((e_gain, e_shift, e_out_b, e_mid_b, e_in_b)):
        ref[...] = lines[place, 0:narrow]


def sum_pieces(width, narrow, cap):
    half = width // 2
    pieces = []
    row = 0
    for name, tall, lane in (
        ("edge_own", narrow, 0), ("edge_own", narrow, half), ("e_in", narrow, 0), ("e_mid", narrow, 0),
        ("e_out", narrow, 0), ("e_lines", 16, 0),
    ):
        pieces.append((name, 0, tall, lane, 0, row))
        row += tall
    pieces += [("message_out", 0, width, 0, 1, 0), ("message_out", 0, width, half, 1, width)]
    place = 0
    for name, tall in (
        ("edge_near", narrow), ("message_mid", width), ("message_own", width), ("message_near", width),
        ("message_edge", narrow), ("lines", 16),
    ):
        done = 0
        while done < tall:
            size = min(tall - done, cap - place % cap)
            pieces.append((name, done, size, 0, 2 + place // cap, place % cap))
            place += size
            done += size
    return pieces


def line_places(width, hidden):
    pieces = hidden // width
    singles = ("v_final_gain", "v_final_shift", "v_down", "v_node_gain", "v_node_shift", "v_out", "v_mid", "v_in")
    places = {name: pieces + place for place, name in enumerate(singles)}
    places["v_up"] = 0
    return places


class Sums:
    def __init__(self, pieces, groups):
        self.pieces, self.groups = pieces, groups

    def put(self, name, value):
        value = value.astype(low)
        for piece, first, tall, lane, group, row in self.pieces:
            if piece != name:
                continue
            ref = self.groups[group]
            part = value[first : first + tall, lane : lane + ref.shape[-1]]
            if part.shape[1] < ref.shape[-1]:
                part = jnp.concatenate([part, jnp.zeros((tall, ref.shape[-1] - part.shape[1]), low)], axis=1)
            for start in range(0, tall, 16):
                place, rest = [], (row + start) // 16
                for size in reversed(ref.shape[:-2]):
                    place.append(rest % size)
                    rest //= size
                ref[tuple(reversed(place))] = part[start : start + 16]


def whole_kernel(
    grid, slots, pieces, places,
    near_index, counts, masks, nodes, b_in, b_mid, b_out, gain_one, shift_one, b_up, b_down, gain_two, shift_two,
    eb_in, ew_mid, eb_mid, ew_out, eb_out, gain_three, shift_three, cotangent,
    edges_far, edge_ct_far, w_in_far, w_mid_far, w_out_far, w_up_far, w_down_far, w_edge_far,
    node_out, edge_result, edge_total, grad_nodes, total_one, total_two, total_three, total_four, out_up, out_down,
    edges, edge_ct, w_in, w_mid, w_out, w_up, w_down, w_edge, fetches, puts, index, rows,
    slope_one, slope_two, act_one, partial, table, own, pooled, up_slope, sent_table, own_edge,
    spread_edge, spread_two, own_edge_grad, e_in, e_mid, e_out, e_vectors,
    spread_sum, spread, own_sum, mid_sum, g_mid, g_edge, lines, node_part, normed_table, down_table,
    spare_narrow, spare_wide,
    *scratch,
):
    scratch = list(scratch)

    def take(size):
        taken = scratch[:size]
        del scratch[:size]
        return taken

    spot = Spot(grid)
    partner = (1 - spot.core, lax.axis_index("res"))
    peers = spot.peers() + [partner]
    greet(peers)
    _, half_count, width = nodes.shape
    count = 2 * half_count
    total = spread_sum.shape[0]
    narrow = w_edge.shape[0]
    hidden = w_up.shape[1]
    steps = rows.shape[0]
    local = pltpu.make_async_copy(nodes, table.at[spot.z, spot.y, spot.x], puts.at[steps + 1])
    local.start()
    pairs = (
        (w_in_far, w_in), (edges_far, edges), (w_mid_far, w_mid), (w_out_far, w_out), (w_up_far, w_up),
        (w_down_far, w_down), (w_edge_far, w_edge), (edge_ct_far, edge_ct),
    )
    coming = [pltpu.make_async_copy(there, near, fetches.at[place]) for place, (there, near) in enumerate(pairs)]
    start_all(coming)
    node_sems, sent_sems, normed_sems, down_sems = take(10), take(10), take(10), take(10)
    edge_scratch, node_scratch, feed_parts = take(9), take(9), take(5)
    totals = [take(11) for _ in range(4)]
    sums = Sums(pieces, (total_one, total_two, total_three, total_four))
    live = as_column(counts[...], count)
    lane = lax.broadcasted_iota(jnp.int32, (count, slots * count), 1)
    same = lane % count == lax.broadcasted_iota(jnp.int32, (count, slots * count), 0)
    fold = jnp.where(same, 1.0, 0.0).astype(low)
    ones = jnp.ones((8, slots * count), low)
    mask = as_column(masks[...], count).astype(wide)
    node_rows = nodes[...].reshape(count, width)
    local.wait()
    met(peers)
    node_gather = gather_run(gather_plan(spot, table, node_sems))
    next(node_gather)
    coming[0].wait()
    index[...] = jnp.transpose(near_index[:, 0, :])
    for step in range(steps):
        rows[step] = jnp.concatenate([near_index[step * slots + s] for s in range(slots)], axis=1)
    own[...] = dot(node_rows, w_in[0:width]) + as_row(b_in)
    pooled[...] = jnp.zeros_like(pooled)
    drive(node_gather)
    spread[...] = dot(table[...].reshape(total, width), w_in[width : 2 * width]).astype(low).reshape(spread.shape)
    for copy in coming[1:3]:
        copy.wait()

    @pl.loop(0, steps)
    def _(step):
        here = pl.ds(step * slots, slots)
        picks = pick_rows(index[...], step * slots, slots, total)
        edge_rows = edges[here].reshape(slots * count, narrow)
        pre = dot(picks, spread[...].reshape(total, width)) + dot(edge_rows, w_in[2 * width :])
        pre = pre.reshape(slots, count, width) + own[...][None]
        act, slope = gelu_pair(pre)
        act = act.astype(low)
        act_one[here] = act
        slope_one[here] = slope.astype(low)
        pre = dot(act.reshape(slots * count, width), w_mid[...]) + as_row(b_mid)
        act, slope = gelu_pair(pre)
        slope_two[here] = slope.astype(low).reshape(slots, count, width)
        valid = jnp.where(same & (live > step * slots + lane // count), 1.0, 0.0).astype(low)
        pooled[...] += dot(valid, act.astype(low))

    mixed_low = (pooled[...] / jnp.maximum(live, 1).astype(wide)).astype(low)
    some = jnp.where(live > 0, 1.0, 0.0)
    for copy in coming[3:]:
        copy.wait()
    aggregate = dot(mixed_low, w_out[...]) + some * as_row(b_out)
    hat_one, scale_one = norm_stats(node_rows.astype(wide) + mask * aggregate)
    first = hat_one * as_row(gain_one) + as_row(shift_one)
    first_low = first.astype(low)
    normed_table[spot.z, spot.y, spot.x] = first_low.reshape(normed_table.shape[3:])
    act_up, slope_up = gelu_pair(dot(first_low, w_up[...]) + as_row(b_up))
    up_slope[...] = slope_up
    second_sum = first + dot(act_up.astype(low), w_down[...]) + as_row(b_down)
    hat, _ = norm_stats(second_sum)
    out = (hat * as_row(gain_two) + as_row(shift_two)).astype(low)
    node_out[...] = out
    pad = jnp.zeros((count, sent_table.shape[-1] - narrow), low)
    sent = jnp.concatenate([dot_back(out, w_edge[:, width : 2 * width]).astype(low), pad], axis=1)
    sent_table[spot.z, spot.y, spot.x] = sent.reshape(sent_table.shape[3:])
    sent_gather = gather_run(gather_plan(spot, sent_table, sent_sems))
    next(sent_gather)
    normed_gather = gather_run(gather_plan(spot, normed_table, normed_sems))
    own_edge[...] = dot_back(out, w_edge[:, 0:width]) + as_row(eb_in)
    spread_edge[...] = jnp.zeros_like(spread_edge)
    for ref in (own_edge_grad, e_in, e_mid, e_out, e_vectors):
        ref[...] = jnp.zeros_like(ref)
    next(sent_gather)
    next(normed_gather)
    drive(sent_gather)
    w_here = w_edge[:, 2 * width :]

    @pl.loop(0, steps)
    def _(step):
        here = pl.ds(step * slots, slots)
        for beat in range(1, steps):
            @pl.when(step == beat)
            def _():
                next(normed_gather, None)

        picks = pick_rows(index[...], step * slots, slots, total)
        edge_rows = edges[here].reshape(slots * count, narrow)
        near_part = dot(picks, sent_table[...].reshape(total, sent_table.shape[-1]))[:, 0:narrow]
        pre = near_part + dot_back(edge_rows, w_here)
        pre = (pre.reshape(slots, count, narrow) + own_edge[...][None]).reshape(slots * count, narrow)
        act_a, slope_a = gelu_pair(pre)
        act_a = act_a.astype(low)
        pre = dot(act_a, ew_mid[...]) + as_row(eb_mid)
        act_b, slope_b = gelu_pair(pre)
        act_b = act_b.astype(low)
        pre = dot(act_b, ew_out[...]) + as_row(eb_out)
        hat, scale = norm_stats(edge_rows.astype(wide) + pre)
        gain_row = as_row(gain_three)
        grad_low = edge_ct[here].reshape(slots * count, narrow)
        grad = grad_low.astype(wide)
        edge_ct[here] = (hat * gain_row + as_row(shift_three)).astype(low).reshape(slots, count, narrow)
        sum_grad = norm_back(hat, scale, gain_row, grad)
        three = sum_grad.astype(low)
        e_out[...] += dot_rows(act_b, three)
        two = (slope_b * dot_back(three, ew_out[...])).astype(low)
        e_mid[...] += dot_rows(act_a, two)
        one = (slope_a * dot_back(two, ew_mid[...])).astype(low)
        e_in[...] += dot_rows(one, edge_rows)
        e_vectors[...] += jnp.concatenate(
            [
                jnp.sum(grad * hat, axis=0, keepdims=True), dot(ones, grad_low)[0:1], dot(ones, three)[0:1],
                dot(ones, two)[0:1], jnp.zeros((4, narrow), wide),
            ],
            axis=0,
        )
        own_edge_grad[...] += dot(fold, one)
        partial[here] = (sum_grad + dot(one, w_here)).astype(low).reshape(slots, count, narrow)
        spread_edge[...] += dot(pick_columns(rows[step], total), one)

    result_copy = pltpu.make_async_copy(edge_ct, edge_result, puts.at[steps])
    result_copy.start()
    pad = jnp.zeros((total, spread_two.shape[-1] - narrow), low)
    spread_two[...] = jnp.concatenate([spread_edge[...].astype(low), pad], axis=1).reshape(spread_two.shape)

    moving = []

    def launch(run):
        next(run)
        moving.append(run)

    def beat():
        for run in list(moving):
            if next(run, moving) is moving:
                moving.remove(run)

    def put_line(name, value):
        lines[places[name] : places[name] + value.shape[0], :] = value

    back = []
    edge_run = scatter_run(spot, spread_two, edge_scratch, back)
    next(edge_run)
    own_low = own_edge_grad[...].astype(low)
    sums.put("edge_own", dot_rows(own_low, out))
    sums.put("e_in", e_in[...])
    sums.put("e_mid", e_mid[...])
    sums.put("e_out", e_out[...])
    sums.put("e_lines", jnp.concatenate(
        [e_vectors[0:4], jnp.sum(own_edge_grad[...], axis=0, keepdims=True), jnp.zeros((11, narrow), wide)], axis=0
    ))
    gathers = [normed_gather, gather_run(gather_plan(spot, down_table, down_sems))]
    moving.append(normed_gather)
    launch(total_run(spot, partner, total_one, total_one, totals[0], spare_narrow))
    lines[...] = jnp.zeros_like(lines)
    grad = cotangent[...].astype(wide) + dot(own_low, w_edge[:, 0:width])
    hat, scale = norm_stats(second_sum)
    drive(edge_run)

    back_low = jnp.concatenate(back, axis=0)[:, 0:narrow].astype(low)
    grad = grad + dot(back_low, w_edge[:, width : 2 * width])
    put_line("v_final_gain", jnp.sum(grad * hat, axis=0, keepdims=True))
    put_line("v_final_shift", jnp.sum(grad, axis=0, keepdims=True))
    second = norm_back(hat, scale, as_row(gain_two), grad)
    down = second.astype(low)
    down_table[spot.z, spot.y, spot.x] = down.reshape(down_table.shape[3:])
    launch(gathers[1])
    put_line("v_down", jnp.sum(down.astype(wide), axis=0, keepdims=True))
    sums.put("edge_near", dot_rows(back_low, out))
    up = (up_slope[...] * dot_back(down, w_down[...])).astype(low)
    bias_up = jnp.sum(up.astype(wide), axis=0, keepdims=True)
    for piece in range(hidden // width):
        lines[piece : piece + 1, :] = bias_up[:, piece * width : (piece + 1) * width]
    first = second + dot_back(up, w_up[...])
    put_line("v_node_gain", jnp.sum(first * hat_one, axis=0, keepdims=True))
    put_line("v_node_shift", jnp.sum(first, axis=0, keepdims=True))
    mixed = norm_back(hat_one, scale_one, as_row(gain_one), first)
    masked = mask * mixed
    put_line("v_out", jnp.sum(jnp.where(live > 0, masked, 0.0), axis=0, keepdims=True))
    sums.put("message_out", dot_rows(mixed_low, masked.astype(low)))
    shared = (masked / jnp.maximum(live, 1).astype(wide)).astype(low)
    lift = dot_back(shared, w_out[...])

    beat()
    launch(total_run(spot, partner, total_two, total_two, totals[1], spare_narrow))

    own_sum[...] = jnp.zeros_like(own_sum)
    mid_sum[...] = jnp.zeros_like(mid_sum)
    g_mid[...] = jnp.zeros_like(g_mid)

    @pl.loop(0, steps)
    def _(step):
        here = pl.ds(step * slots, slots)
        slope = slope_two[here].astype(wide)
        mids = [jnp.where(live > step * slots + s, slope[s] * lift, 0.0).astype(low) for s in range(slots)]
        mid = jnp.concatenate(mids, axis=0)
        mid_sum[...] += dot(ones, mid)
        g_mid[...] += dot_rows(act_one[here].reshape(slots * count, width), mid)
        slope = slope_one[here].reshape(slots * count, width).astype(wide)
        inner = (slope * dot_back(mid, w_mid[...])).astype(low)
        slope_one[here] = inner.reshape(slots, count, width)
        own_sum[...] += dot(fold, inner)

    own_low = own_sum[...].astype(low)
    sums.put("message_own", dot_rows(node_rows, own_low))
    sums.put("message_mid", g_mid[...])
    put_line("v_mid", mid_sum[0:1])
    put_line("v_in", jnp.sum(own_sum[...], axis=0, keepdims=True))
    beat()
    launch(total_run(spot, partner, total_three, total_three, totals[2], spare_wide))
    part = mixed + dot_back(own_low, w_in[0:width])
    node_part[0] = part[0 : count // 2]
    node_part[1] = part[count // 2 :]

    spread_sum[...] = jnp.zeros_like(spread_sum)
    g_edge[...] = jnp.zeros_like(g_edge)

    for step in range(steps):
        here = slice(step * slots, (step + 1) * slots)
        inner = slope_one[here].reshape(slots * count, width)
        g_edge[...] += dot_rows(edges[here].reshape(slots * count, narrow), inner)
        spread_sum[...] += dot(pick_columns(rows[step], total), inner)

    spread_low = spread_sum[...].astype(low)
    spread[...] = spread_low.reshape(spread.shape)
    beat()
    launch(owner_run(spot, spread, node_part, w_in.at[width : 2 * width], grad_nodes, node_scratch))
    sums.put("message_near", dot_rows(table[...].reshape(total, width), spread_low))
    sums.put("message_edge", g_edge[...])
    sums.put("lines", lines[...])
    launch(total_run(spot, partner, total_four, total_four, totals[3], spare_wide))

    @pl.loop(0, steps)
    def _(step):
        here = pl.ds(step * slots, slots)
        inner = slope_one[here].reshape(slots * count, width)
        back_part = dot_back(inner, w_in[2 * width :]).reshape(slots, count, narrow)
        partial[here] = (partial[here].astype(wide) + back_part).astype(low)

    leaving = [result_copy, pltpu.make_async_copy(partial, edge_total, puts.at[0])]
    leaving[1].start()
    beat()
    while any(run in gathers for run in moving):
        beat()
    feed = feed_run(
        spot, partner, normed_table, down_table, w_up, b_up, w_down, out_up, out_down,
        feed_parts[0], slope_two, act_one, *feed_parts[1:]
    )
    for place, _ in enumerate(feed):
        if place % FEED_BEAT == FEED_BEAT - 1:
            beat()
    while moving:
        beat()
    for copy in leaving:
        copy.wait()


def unpack(pieces, places, node_in, grad_in, *refs):
    node_out, grad_out, refs = refs[8], refs[9], refs[:8] + refs[10:]
    ins, outs = refs[:8], refs[8:32]
    node_out[...] = node_in[...]
    grad_out[...] = grad_in[...].reshape(grad_out.shape)
    (m_in_far, m_in_b, m_mid_far, m_mid_b, m_out_far, m_out_b, n_gain, n_shift, f_up_far, f_up_b, f_down_far, f_down_b,
     l_gain, l_shift, e_in_far, e_in_b, e_mid, e_mid_b, e_out, e_out_b, e_gain, e_shift, edge_far, result_far) = outs
    near, (m_in, m_mid, m_out, f_up, f_down, e_in, edge), (reads, writes) = refs[32:40], refs[40:47], refs[47:]
    width, narrow, hidden = m_mid.shape[0], e_mid.shape[0], f_up.shape[1]
    coming = [pltpu.make_async_copy(there, here, reads.at[place]) for place, (there, here) in enumerate(zip(ins, near))]
    groups = near[:4]
    (up_low, down_low, part, result) = near[4:]
    for place in (4, 5, 6, 7, 0, 1, 2, 3):
        coming[place].start()
    leaving = []

    def leave(source, target):
        copy = pltpu.make_async_copy(source, target, writes.at[len(leaving)])
        copy.start()
        leaving.append(copy)

    span = down_low.shape[1]
    coming[4].wait()
    for piece in range(hidden // span):
        lanes = slice(piece * span, (piece + 1) * span)
        f_up[:, lanes] = up_low[piece].astype(wide)
        leave(f_up.at[:, lanes], f_up_far.at[:, lanes])
    coming[5].wait()
    for piece in range(hidden // span):
        lanes = slice(piece * span, (piece + 1) * span)
        f_down[lanes] = down_low[piece].astype(wide)
        leave(f_down.at[lanes], f_down_far.at[lanes])
    coming[6].wait()
    chunk = edge.shape[0] // 5
    for piece in range(5):
        here = slice(piece * chunk, (piece + 1) * chunk)
        edge[here] = part[here].astype(wide)
        leave(edge.at[here], edge_far.at[here])
    coming[7].wait()
    leave(result, result_far)
    for copy in coming[:4]:
        copy.wait()

    def move(name, target, first_row=0, first_lane=0, most=None):
        for piece, first, tall, lane, group, row in pieces:
            if piece == name:
                size = min(groups[group].shape[1], (most or width) - lane)
                target[
                    first_row + first : first_row + first + tall, first_lane + lane : first_lane + lane + size
                ] = groups[group][row : row + tall, 0:size].astype(wide)

    move("message_own", m_in)
    move("message_near", m_in, width)
    move("message_edge", m_in, 2 * width)
    leave(m_in, m_in_far)
    move("message_mid", m_mid)
    leave(m_mid, m_mid_far)
    move("message_out", m_out)
    leave(m_out, m_out_far)
    move("edge_own", e_in)
    move("edge_near", e_in, 0, width)
    move("e_in", e_in, 0, 2 * width, narrow)
    leave(e_in, e_in_far)
    move("e_mid", e_mid, 0, 0, narrow)
    move("e_out", e_out, 0, 0, narrow)

    def rows_of(name):
        found = [groups[group][row : row + 16].astype(wide) for piece, _, _, _, group, row in pieces if piece == name]
        return jnp.concatenate(found, axis=1)

    lines, e_lines = rows_of("lines"), rows_of("e_lines")
    for name, ref in (
        ("v_in", m_in_b), ("v_mid", m_mid_b), ("v_out", m_out_b), ("v_node_gain", n_gain), ("v_node_shift", n_shift),
        ("v_final_gain", l_gain), ("v_final_shift", l_shift), ("v_down", f_down_b),
    ):
        ref[...] = lines[places[name]]
    for piece in range(hidden // width):
        f_up_b[piece * width : (piece + 1) * width] = lines[piece]
    for place, ref in enumerate((e_gain, e_shift, e_out_b, e_mid_b, e_in_b)):
        ref[...] = e_lines[place, 0:narrow]
    for copy in leaving:
        copy.wait()


def table_kernel(grid, own, table, *sems):
    spot = Spot(grid)
    copy = pltpu.make_async_copy(own, table.at[spot.z, spot.y, spot.x], sems[-1])
    copy.start()
    meet(spot.peers())
    copy.wait()
    drive(gather_run(gather_plan(spot, table, sems[:-1])))


def owner_kernel(grid, part, out, *scratch):
    spot = Spot(grid)
    meet(spot.peers())
    sums = []
    drive(scatter_run(spot, part, scratch, sums))
    out[0] = sums[0]
    out[1] = sums[1]


def total_run(spot, partner, given, out, scratch, spare=None):
    pair, parts, sems = scratch[0], scratch[1:10], scratch[10]
    (ra1, rb1, ra2, rb2, r3) = parts[:5]
    places = (pair, pair, r3, ra2, rb2, ra1, rb1)
    side_z, side_y, side_x = spot.grid
    z, y, x = spot.z, spot.y, spot.x
    core = spot.core
    mine = out.at[core]

    def go(source, target, kind, device):
        remote(source, target, sems.at[0, kind], sems.at[1, kind], device).start()

    def come(kind):
        wait_bytes(places[kind], sems.at[1, kind])

    if spare is None:
        go(given.at[1 - core], pair, 0, partner)
    else:
        spare[...] = given[1 - core]
        go(spare, pair, 0, partner)
    yield

    def before():
        come(0)
        wait_bytes(pair, sems.at[0, 0])
        mine[...] = (given[core].astype(wide) + pair[...].astype(wide)).astype(low)

    sums = []
    yield from scatter_run(spot, mine, parts, sums, before)
    for half in range(2):
        mine[z, y, x, half] = sums[half].astype(low)

    def first(zj):
        for s in range(1, side_x):
            go(mine.at[zj, y, x, 0], mine.at[zj, y, x, 0], 3, spot.device(z, y, spot.far_x(s)))
        for s in range(1, side_y):
            go(mine.at[zj, y, x, 1], mine.at[zj, y, x, 1], 4, spot.device(z, spot.far_y(s), x))

    for s in range(1, side_z):
        go(mine.at[z, y, x], mine.at[z, y, x], 2, spot.device(spot.far_z(s), y, x))
    first(z)
    yield
    come(2)
    for s in range(1, side_z):
        first(spot.far_z(s))
    yield
    come(3)
    come(4)
    for j in range(side_z):
        zj = flip(z, j)
        for s in range(1, side_y):
            go(mine.at[zj, y, :, 0], mine.at[zj, y, :, 0], 5, spot.device(z, spot.far_y(s), x))
        for s in range(1, side_x):
            go(mine.at[zj, :, x, 1], mine.at[zj, :, x, 1], 6, spot.device(z, y, spot.far_x(s)))
    yield
    come(5)
    come(6)
    go(mine, mine, 1, partner)
    yield
    come(1)
    for kind in range(1, len(places)):
        wait_bytes(places[kind], sems.at[0, kind])


def total_scratch(grid, rows, width):
    return (
        [pltpu.VMEM(grid + (2, rows, width), low)]
        + scatter_scratch(grid, rows, width)
        + [pltpu.SemaphoreType.DMA((2, 7))]
    )


def owner_run(spot, part, node_part, w_near, out, scratch):
    sums = []
    yield from scatter_run(spot, part, scratch, sums)
    for half in range(2):
        out[half] = node_part[half] + dot_back(sums[half].astype(low), w_near[...])


def feed_run(
    spot, partner, normed_table, down_table, w_up, b_up, w_down, out_up, out_down,
    bias, sent, near, sends, arrives, last_sends, last_arrives,
):
    span = w_up.shape[1] // out_up.shape[0]
    half = out_up.shape[0] // 2
    core = spot.core
    width = w_up.shape[0]
    rows = math.prod(normed_table.shape) // width
    bias[...] = as_row(b_up)
    rows_each = sent.shape[1]

    def piece(place):
        normed = normed_table[...].reshape(rows, width)
        down = down_table[...].reshape(rows, width)
        lanes = pl.ds(pl.multiple_of(place * span, span), span)
        act, slope = gelu_pair(dot(normed, w_up[:, lanes]) + bias[:, lanes])
        up = (slope * dot_back(down, w_down[lanes, :])).astype(low)
        return dot_rows(normed, up), dot_rows(act.astype(low), down)

    started = []
    for q in range(half):
        up, down = piece((1 - core) * half + q)
        tall = span // rows_each
        beside = jnp.concatenate([up[0:span], up[span:]], axis=1)
        sent[2 * q * tall : (2 * q + 1) * tall] = beside.astype(low).reshape(tall, rows_each, width)
        sent[(2 * q + 1) * tall : (2 * q + 2) * tall] = down.astype(low).reshape(tall, rows_each, width)
        here = slice(2 * q * tall, (2 * q + 2) * tall)
        pair = [remote(sent.at[here], near.at[here], sends.at[q], arrives.at[q], partner)]
        start_all(pair)
        started.append(pair)
        yield
    finals = []
    for q in range(half):
        place = core * half + q
        up, down = piece(place)
        arrived(started[q])
        beside = near[2 * q * tall : (2 * q + 1) * tall].reshape(span, width).astype(wide)
        near_down = near[(2 * q + 1) * tall : (2 * q + 2) * tall].reshape(span, width).astype(wide)
        near_up = jnp.concatenate([beside[:, 0:span], beside[:, span:]], axis=0)
        out_up[place] = (up + near_up).astype(low)
        out_down[place] = (down + near_down).astype(low)
        pair = [
            remote(out_up.at[place], out_up.at[place], last_sends.at[0, q], last_arrives.at[0, q], partner),
            remote(out_down.at[place], out_down.at[place], last_sends.at[1, q], last_arrives.at[1, q], partner),
        ]
        start_all(pair)
        finals += pair
        yield
    arrived(finals)
    all_sent(flat(started) + finals)


def feed_scratch(width, hidden, pieces, rows=None):
    dma = pltpu.SemaphoreType.DMA
    half = pieces // 2
    spare = [] if rows is None else [pltpu.VMEM((hidden // rows, rows, width), low)] * 2
    return [pltpu.VMEM((1, hidden), wide)] + spare + [dma((half,)), dma((half,)), dma((2, half)), dma((2, half))]


def tail_kernel(
    grid, given, part, node_part, w_near, table, w_up, b_up, w_down, summed, out_nodes, out_up, out_down, *scratch
):
    spot = Spot(grid)
    partner = (1 - spot.core, lax.axis_index("res"))
    meet(spot.peers() + [partner])
    total = total_run(spot, partner, given, summed, scratch[:11])
    owner = owner_run(spot, part, node_part, w_near, out_nodes, scratch[11:20])
    feed = feed_run(spot, partner, table.at[:, :, :, 0], table.at[:, :, :, 1], w_up, b_up, w_down, out_up, out_down, *scratch[20:])
    runs = [owner, total, feed]
    while runs:
        for run in list(runs):
            if next(run, runs) is runs:
                runs.remove(run)


vmem = pl.BlockSpec(memory_space=pltpu.VMEM)
far = pl.BlockSpec(memory_space=pl.ANY)
most_vmem = 67_000_000


def params(collective=None, **more):
    if collective is None:
        return pltpu.CompilerParams(vmem_limit_bytes=most_vmem, **more)
    return pltpu.CompilerParams(
        collective_id=collective, has_side_effects=True, vmem_limit_bytes=most_vmem, **more
    )


def gather_table(grid, rows, collective):
    count, width = rows.shape
    table = pl.pallas_call(
        functools.partial(table_kernel, grid),
        out_shape=jax.ShapeDtypeStruct(grid + (2, count // 2, width), low),
        in_specs=[vmem],
        out_specs=vmem,
        scratch_shapes=gather_sems(grid) + [pltpu.SemaphoreType.DMA],
        compiler_params=params(collective),
        name="gather_table_%d" % width,
    )(rows.reshape(2, count // 2, width))
    return table.reshape(-1, width)


def held(array):
    return pl.BlockSpec(array.shape, lambda step, dims=len(array.shape): (0,) * dims, pipeline_mode=pl.Buffered(1))


def streamed(array, slots):
    return pl.BlockSpec((slots,) + array.shape[1:], lambda step, dims=len(array.shape): (step,) + (0,) * (dims - 1))


def call(kernel, name, steps, slots, inputs, outputs, scratch, collective=None):
    def spec(item, flow):
        return streamed(item, slots if item.shape[0] != steps else 1) if flow else held(item)
    return pl.pallas_call(
        kernel,
        grid=(steps,),
        in_specs=[spec(item, flow) for item, flow in inputs],
        out_specs=[spec(item, flow) for item, flow in outputs],
        out_shape=[item for item, _ in outputs],
        scratch_shapes=scratch,
        compiler_params=params(collective),
        name=name,
    )(*[item for item, _ in inputs])


def per_device(
    node_states, edge_states, neighbours, residue_mask, neighbour_count,
    message_in, message_in_bias, message_mid, message_mid_bias, message_out, message_out_bias,
    node_gain, node_shift, feed_up, feed_up_bias, feed_down, feed_down_bias, final_gain, final_shift,
    edge_in, edge_in_bias, edge_mid, edge_mid_bias, edge_out, edge_out_bias, edge_gain, edge_shift,
    node_cotangent, edge_cotangent,
):
    grid = chip_grid(lax.axis_size("res"))
    nodes = node_states[0]
    count, width = nodes.shape
    edges = jnp.transpose(edge_states[0], (1, 0, 2))
    edge_ct = jnp.transpose(edge_cotangent[0], (1, 0, 2))
    depth, _, narrow = edges.shape
    hidden = feed_up.shape[1]
    total = grid[0] * grid[1] * grid[2] * count
    slots = 20 if total <= 1024 else 12
    steps = depth // slots
    edge_in_t = jnp.transpose(edge_in)
    lanes = -(-narrow // 128) * 128
    shape = jax.ShapeDtypeStruct
    slab = shape((depth, count, width), low)
    node_low, node_wide = shape((count, width), low), shape((count, width), wide)
    scratch = pltpu.VMEM

    square = shape((narrow, narrow), wide)
    if total <= 1024:
        places = line_places(width, hidden)
        blocks = (2,) + grid + (2, 16, width)
        each = math.prod(blocks[:-1])
        cut = sum_pieces(width, narrow, each)
        pieces = hidden // 256
        near_index = jnp.transpose(neighbours, (2, 0, 1))
        half_rows = (2, count // 2, width)
        lane_rows = (2, count // 2, lanes)
        dma = pltpu.SemaphoreType.DMA
        whole, few = shape(blocks, low), shape(blocks[:-1] + (width // 2,), low)
        near = [
            near_index, neighbour_count, residue_mask, nodes.reshape(half_rows), message_in_bias, message_mid_bias,
            message_out_bias, node_gain, node_shift, feed_up_bias, feed_down_bias, final_gain, final_shift,
            edge_in_bias, edge_mid, edge_mid_bias, edge_out, edge_out_bias, edge_gain, edge_shift, node_cotangent[0],
        ]
        distant = [edges, edge_ct, message_in, message_mid, message_out, feed_up, feed_down, edge_in_t]
        strip = scratch((count, narrow), wide)
        (node_out, edge_result, edge_total, grad_nodes, *totals, up_low, down_low) = pl.pallas_call(
            functools.partial(whole_kernel, grid, slots, cut, places),
            out_shape=[node_low, shape(edges.shape, low), shape(edges.shape, low), shape(half_rows, wide),
                       few, few, whole, whole,
                       shape((pieces, width, hidden // pieces), low), shape((pieces, hidden // pieces, width), low)],
            in_specs=[vmem] * len(near) + [far] * len(distant),
            out_specs=[vmem, far, far] + [vmem] * 7,
            scratch_shapes=[scratch(a.shape, low) for a in distant] + [dma((8,)), dma((steps + 2,)), scratch((count, depth), jnp.int32), scratch((steps, 1, slots * count), jnp.int32)]
            + [scratch(slab.shape, low)] * 3
            + [scratch(edges.shape, low), scratch(grid + half_rows, low),
               scratch((count, width), wide), scratch((count, width), wide), scratch((count, hidden), wide),
               scratch(grid + lane_rows, low), strip, scratch((total, narrow), wide), scratch(grid + lane_rows, low),
               strip] + [scratch(square.shape, wide)] * 3 + [scratch((8, narrow), wide)]
            + [scratch((total, width), wide), scratch(grid + half_rows, low),
               scratch((count, width), wide), scratch((8, width), wide), scratch((width, width), wide),
               scratch((narrow, width), wide), scratch((16, width), wide), scratch(half_rows, wide),
               scratch(grid + half_rows, low), scratch(grid + half_rows, low),
               scratch(blocks[1:-1] + (width // 2,), low), scratch(blocks[1:], low)]
            + gather_sems(grid) * 4
            + scatter_scratch(grid, count // 2, lanes) + scatter_scratch(grid, count // 2, width)
            + feed_scratch(width, hidden, pieces) + total_scratch(grid, 16, width // 2) * 2
            + total_scratch(grid, 16, width) * 2,
            compiler_params=params(0), name="whole",
        )(*near, *distant)
        vector, line = shape((width,), wide), shape((narrow,), wide)
        sources = [each_total.reshape(each, -1) for each_total in totals] + [up_low, down_low, edge_total, edge_result]
        kinds = [message_in.shape, vector, message_mid.shape, vector, message_out.shape, vector, vector, vector,
                 feed_up.shape, shape((hidden,), wide), feed_down.shape, vector, vector, vector, edge_in_t.shape, line,
                 square, line, square, line, line, line, edges.shape]
        staged = [kind for kind in kinds if isinstance(kind, tuple)]
        node_out, grad_nodes, *grads, edge_grad, edge_result = pl.pallas_call(
            functools.partial(unpack, cut, places),
            out_shape=[node_low, node_wide] + [shape(kind, wide) if isinstance(kind, tuple) else kind for kind in kinds] + [shape(edges.shape, low)],
            in_specs=[vmem] * 2 + [far] * 8, out_specs=[vmem] * 2 + [far if isinstance(kind, tuple) else vmem for kind in kinds] + [far],
            scratch_shapes=[scratch(a.shape, low) for a in sources] + [scratch(kind, wide) for kind in staged]
            + [dma((8,)), dma((32,))],
            compiler_params=params(), name="unpack",
        )(node_out, grad_nodes, *sources)
    else:
        index = neighbours[0]
        rows = jnp.transpose(index).reshape(steps, 1, slots * count)
        table = gather_table(grid, nodes, 0)
        (slope_one, slope_two, act_one, mixed_low, resid, second_sum, up_slope, node_out, sent, own_edge) = call(
            functools.partial(message_forward, slots), "message_forward", steps, slots,
            [(index, False), (neighbour_count, False), (residue_mask, False), (nodes, False), (table, False), (edges, True)]
            + [(a, False) for a in (
                message_in, message_in_bias, message_mid, message_mid_bias, message_out, message_out_bias,
                node_gain, node_shift, feed_up, feed_up_bias, feed_down, feed_down_bias, final_gain, final_shift,
                edge_in_t, edge_in_bias)],
            [(slab, True)] * 3 + [(node_low, False), (node_wide, False), (node_wide, False),
             (shape((count, hidden), wide), False), (node_low, False),
             (shape((count, lanes), low), False), (shape((count, narrow), wide), False)],
            [scratch((total, width), low), scratch((count, width), wide), scratch((count, width), wide)],
        )
        sent_table = gather_table(grid, sent, 1)
        (edge_result, partial, spread_two, own_edge_grad, e_in, e_mid, e_out, e_vectors) = call(
            functools.partial(edge_pass, slots), "edge_pass", steps, slots,
            [(index, False), (rows, True), (sent_table, False), (own_edge, False), (edges, True), (edge_ct, True)]
            + [(a, False) for a in (edge_in_t, edge_mid, edge_mid_bias, edge_out, edge_out_bias, edge_gain, edge_shift)],
            [(shape(edges.shape, low), True), (shape(edges.shape, low), True), (shape((total, lanes), low), False),
             (shape((count, narrow), wide), False), (square, False), (square, False), (square, False),
             (shape((8, narrow), wide), False)],
            [scratch((total, narrow), wide)],
        )
        back_edge = pl.pallas_call(
            functools.partial(owner_kernel, grid),
            out_shape=shape((2, count // 2, lanes), wide),
            in_specs=[vmem], out_specs=vmem,
            scratch_shapes=scatter_scratch(grid, count // 2, lanes),
            compiler_params=params(2), name="edge_owner",
        )(spread_two.reshape(grid + (2, count // 2, lanes))).reshape(count, lanes)[:, :narrow]
        shares = 4 * grid[0] * grid[1] * grid[2] * 16
        layout = lay_out_rows(width, narrow, hidden, shares)
        table_blocks = grid + (2, count, width)
        (edge_grad, spread, node_part, packed, feed_table) = call(
            functools.partial(node_backward, grid, slots, layout), "node_backward", steps, slots,
            [(rows, True), (neighbour_count, False), (residue_mask, False), (nodes, False), (table, False), (edges, True),
             (slope_one, True), (slope_two, True), (act_one, True), (partial, True)]
            + [(a, False) for a in (
                mixed_low, resid, second_sum, up_slope, node_out, node_cotangent[0], back_edge, own_edge_grad,
                e_in, e_mid, e_out, e_vectors, message_in, message_mid, message_out, node_gain, node_shift,
                feed_up, feed_down, final_gain, edge_in_t)],
            [(shape(edges.shape, wide), True), (shape((total, width), low), False), (node_wide, False),
             (shape((layout["rows"], width), low), False), (shape(table_blocks, low), False)],
            [scratch((count, width), wide), scratch((total, width), wide), scratch((count, width), wide),
             scratch((width, width), wide), scratch((narrow, width), wide), scratch((1, width), wide),
             scratch((32, width), wide), scratch(table_blocks, low)] + gather_sems(grid),
            collective=3,
        )
        chunk = layout["rows"] // (4 * grid[0] * grid[1] * grid[2])
        blocks = (2,) + grid + (2, chunk, width)
        pieces = hidden // 256
        (summed, grad_nodes, up_low, down_low) = pl.pallas_call(
            functools.partial(tail_kernel, grid),
            out_shape=[shape(blocks, low), shape((2, count // 2, width), wide),
                       shape((pieces, width, hidden // pieces), low), shape((pieces, hidden // pieces, width), low)],
            in_specs=[vmem] * 8, out_specs=[vmem] * 4,
            scratch_shapes=total_scratch(grid, chunk, width) + scatter_scratch(grid, count // 2, width)
            + feed_scratch(width, hidden, pieces, count),
            compiler_params=params(4), name="tail",
        )(packed.reshape(blocks), spread.reshape(grid + (2, count // 2, width)), node_part.reshape(2, count // 2, width),
          message_in[width : 2 * width], feed_table, feed_up, feed_up_bias, feed_down)
        grad_nodes = grad_nodes.reshape(count, width)
        vector, line = shape((width,), wide), shape((narrow,), wide)
        grads = pl.pallas_call(
            functools.partial(unpack_rows, layout),
            out_shape=[
                shape(message_in.shape, wide), vector, shape(message_mid.shape, wide), vector,
                shape(message_out.shape, wide), vector, vector, vector, shape(feed_up.shape, wide), shape((hidden,), wide),
                shape(feed_down.shape, wide), vector, vector, vector, shape(edge_in_t.shape, wide), line,
                square, line, square, line, line, line,
            ],
            in_specs=[vmem] * 3, out_specs=[vmem] * 22,
            compiler_params=params(), name="unpack",
        )(summed.reshape(layout["rows"], width), up_low, down_low)
    grads = list(grads)
    grads[14] = jnp.transpose(grads[14])
    back = (1, 0, 2)
    return (
        node_out[None],
        jnp.transpose(edge_result, back)[None],
        grad_nodes[None],
        jnp.transpose(edge_grad, back)[None],
        *grads,
    )


def solution(mesh):
    split, whole = P("batch", "res"), P()
    in_specs = (split,) * 5 + (whole,) * 22 + (split,) * 2
    out_specs = (split,) * 4 + (whole,) * 22
    return jax.shard_map(per_device, mesh=mesh, in_specs=in_specs, out_specs=out_specs, check_vma=False)
```
